512 devices in a mesh: seq: 64 (over z, x, y_lo), tp: 8 (over y_hi, core).
Axes of the slice: x: 4, y: 8 (y_hi: 4, y_lo: 2; y = y_hi * 2 + y_lo), z: 8, core: 2. Of those that a mesh axis runs over, the one named last changes fastest.
Arguments:
- tokens: bfloat16 [16384, 4096], P('seq', 'tp'), may hold values from -6 to 6
- x_weight: bfloat16 [4096, 8192], P('seq', 'tp'), may hold values from -0.09375 to 0.09375
- bc_weight: bfloat16 [4096, 256], P('seq', 'tp'), may hold values from -0.09375 to 0.09375
- dt_weight: bfloat16 [4096, 128], P('seq', 'tp'), may hold values from -0.09375 to 0.09375
- conv_x: float32 [4, 8192], P(None, 'tp'), may hold values from -2.5 to 2.5
- conv_bc: float32 [4, 256], replicated, may hold values from -2.5 to 2.5
- dt_bias: float32 [128], P('tp'), may hold values from -3 to 0
- decay_rate: float32 [128], P('tp'), may hold values from 6.1035155e-07 to 0.07
- d_skip: float32 [128], P('tp'), may hold values from 0.5 to 2
- norm_gain: float32 [8192], P('tp'), may hold values from 0.5 to 1.5
- initial_state: float32 [128, 64, 128], P('tp'), may hold values from -16 to 16
- steer: float32 [8192], P('tp'), may hold values from -6 to 6
Outputs:
- steered: bfloat16 [16384, 8192], P('seq', 'tp')
The draws below stay inside these ranges and needn't reach their ends.
All inputs are finite; a program needn't handle non-finite values.
Results may differ from the reference program's by a relative error of at most 0.0055.
Values may be sent and summed in bfloat16 or wider, within the bound.
No kernel may reach another device: no remote copies, remote signals or barrier semaphores. Data moves between devices by JAX's collectives and lax.ppermute only.
A program may use at most 64 MiB of HBM per device.

```python
import math
import jax
import jax.numpy as jnp
from jax import lax

D = 4096
P_SIZE = 64
N = 128
WIDTH = 4
GROUP = 128
HEADS = 128
INNER = 8192
TOKENS = 16384


def shard_levels(own_key, shape, pieces, low, largest):
    gain, own = 1.0, jax.random.fold_in(own_key, 6)
    for axis_at, blocks in pieces:
        draws = jnp.exp(jax.random.uniform(jax.random.fold_in(own, axis_at), (blocks,), jnp.float32, low / len(pieces), largest / len(pieces)))
        gain = gain * jnp.repeat(draws, shape[axis_at] // blocks).reshape([-1 if axis == axis_at else 1 for axis in range(len(shape))])
    return gain


def noise(rng, dims, width, bound, shards=(), kind=jnp.bfloat16):
    drawn = jax.random.normal(rng, dims, jnp.float32) * width
    if len(shards) > 0:
        drawn = shard_levels(rng, dims, shards, -0.22, 0.18) * drawn
    return jnp.clip(drawn, min=-bound, max=bound).astype(kind)


def setup_inputs(seed: int = 0) -> dict:
    splits = jax.random.split(jax.random.key(seed), 13)
    tokens = noise(splits[0], (TOKENS, D), 1.0, 6.0, ((0, 64), (1, 8)))
    x_weight = noise(splits[1], (D, INNER), D ** -0.5, 0.09375, ((0, 64), (1, 8)))
    bc_weight = noise(splits[2], (D, 2 * N), D ** -0.5, 0.09375, ((0, 64), (1, 8)))
    dt_weight = noise(splits[3], (D, HEADS), D ** -0.5, 0.09375, ((0, 64), (1, 8)))
    conv_x = noise(splits[4], (WIDTH, INNER), 0.5, 2.5, ((1, 8),), jnp.float32)
    conv_bc = noise(splits[5], (WIDTH, 2 * N), 0.5, 2.5, (), jnp.float32)
    dt_bias = jnp.clip(-3.0 + 3.0 * jax.random.uniform(splits[6], (HEADS,), jnp.float32) ** shard_levels(splits[6], (HEADS,), ((0, 8),), -0.2, 0.2), -3.0, 0.0)
    decay_rate = jnp.clip(jnp.exp(math.log(0.07) - 11.649971 * jax.random.uniform(splits[7], (HEADS,), jnp.float32) ** shard_levels(splits[7], (HEADS,), ((0, 8),), -0.2, 0.2)), 6.103515488575795e-07, 0.07)
    d_skip = jnp.clip(jnp.exp(math.log(2.0) - 1.3862944 * jax.random.uniform(splits[8], (HEADS,), jnp.float32) ** shard_levels(splits[8], (HEADS,), ((0, 8),), -0.2, 0.2)), 0.5, 2.0)
    norm_gain = jnp.clip(1.0 + 0.1 * jax.random.normal(splits[9], (INNER,), jnp.float32), 0.5, 1.5)
    initial_state = noise(splits[10], (HEADS, P_SIZE, N), 4.0, 16.0, ((0, 8),), jnp.float32)
    steer = noise(splits[11], (INNER,), 1.0, 6.0, ((0, 8),), jnp.float32)
    return dict(tokens=tokens, x_weight=x_weight, bc_weight=bc_weight, dt_weight=dt_weight, conv_x=conv_x, conv_bc=conv_bc, dt_bias=dt_bias, decay_rate=decay_rate, d_skip=d_skip, norm_gain=norm_gain, initial_state=initial_state, steer=steer)


EPSILON = 1e-05

def convolve(pre_values, kernel):
    kernel_rows = kernel.shape[0]
    length = pre_values.shape[0]
    padded = jnp.concatenate([jnp.zeros((kernel_rows - 1, pre_values.shape[1]), pre_values.dtype), pre_values], 0)
    summed = kernel[0] * padded[0:length].astype(jnp.float32)
    for offset in range(1, kernel_rows):
        summed = summed + kernel[offset] * padded[offset:offset + length].astype(jnp.float32)
    return jax.nn.silu(summed).astype(jnp.bfloat16)

def reference(tokens, x_weight, bc_weight, dt_weight, conv_x, conv_bc, dt_bias, decay_rate, d_skip, norm_gain, initial_state, steer):
    x_pre = jnp.dot(tokens, x_weight, preferred_element_type=jnp.float32).astype(jnp.bfloat16)
    bc_pre = jnp.dot(tokens, bc_weight, preferred_element_type=jnp.float32).astype(jnp.bfloat16)
    dt_raw = jnp.dot(tokens, dt_weight, preferred_element_type=jnp.float32)
    x_conv = convolve(x_pre, conv_x)
    bc_conv = convolve(bc_pre, conv_bc)
    step_size = jax.nn.softplus(dt_raw + dt_bias[None, :])
    log_decay = -step_size * decay_rate[None, :]
    blocks = TOKENS // GROUP
    x_blocks = x_conv.reshape(blocks, GROUP, HEADS, P_SIZE)
    b_blocks = bc_conv[:, :N].reshape(blocks, GROUP, N)
    c_blocks = bc_conv[:, N:].reshape(blocks, GROUP, N)
    a_blocks = log_decay.reshape(blocks, GROUP, HEADS)
    dt_blocks = step_size.reshape(blocks, GROUP, HEADS)
    steer_rows = steer.reshape(HEADS, P_SIZE)
    gain_rows = norm_gain.reshape(HEADS, P_SIZE)
    causal = lax.broadcasted_iota(jnp.int32, (GROUP, GROUP), 0) >= lax.broadcasted_iota(jnp.int32, (GROUP, GROUP), 1)

    def block_update(carry_state, inputs):
        x_block, b_block, c_block, a_block, dt_block = inputs
        cumulative = jnp.cumsum(a_block, axis=0)
        scores = jnp.dot(c_block, b_block.T, preferred_element_type=jnp.float32)
        differ = cumulative[:, None, :] - cumulative[None, :, :]
        decays = jnp.where(causal[:, :, None], jnp.exp(jnp.where(causal[:, :, None], differ, 0.0)), 0.0)
        mixing = (scores[:, :, None] * decays * dt_block[None, :, :]).astype(jnp.bfloat16)
        x_float = x_block.astype(jnp.float32)
        inside = jnp.einsum('tsh,shp->thp', mixing.astype(jnp.float32), x_float)
        carried_in = jnp.einsum('tn,hpn->thp', c_block.astype(jnp.float32), carry_state, precision=lax.Precision.HIGHEST)
        outputs = inside + jnp.exp(cumulative)[:, :, None] * carried_in + d_skip[None, :, None] * x_float
        to_end = jnp.exp(cumulative[-1][None, :] - cumulative) * dt_block
        scaled = (x_float * to_end[:, :, None]).astype(jnp.bfloat16)
        added_state = jnp.einsum('shp,sn->hpn', scaled.astype(jnp.float32), b_block.astype(jnp.float32))
        next_state = jnp.exp(cumulative[-1])[:, None, None] * carry_state + added_state
        mean_square = lax.optimization_barrier(jnp.mean(outputs * outputs, axis=-1, keepdims=True))
        normed = outputs * lax.rsqrt(mean_square + EPSILON) * gain_rows[None, :, :]
        penalty = lax.optimization_barrier(jnp.sum(normed * steer_rows[None, :, :], axis=(1, 2))) / jnp.sqrt(jnp.float32(INNER))
        result = (normed - penalty[:, None, None] * steer_rows[None, :, :]).astype(jnp.bfloat16)
        return (next_state, result)
    final_state, results = lax.scan(block_update, initial_state.astype(jnp.float32), (x_blocks, b_blocks, c_blocks, a_blocks, dt_blocks))
    return results.reshape(TOKENS, INNER)
```

```python
import functools
import math

import jax
import jax.numpy as jnp
from jax import lax
from jax.experimental import pallas as pl
from jax.experimental.pallas import tpu as pltpu
from jax.sharding import Mesh, PartitionSpec as P

EPSILON = 1e-05
GROUP = 128
N = 128
HALO = 16
HEAD = 64
HIGHEST = lax.Precision.HIGHEST

SEQ = ("z", "x", "yl")
TP = ("yh", "c")
SIZES = {"z": 8, "x": 4, "yl": 2, "yh": 4, "c": 2}


def call(kernel, outs, *args, flops=0, bytes_accessed=0, smem=()):
    specs = [
        pl.BlockSpec(memory_space=pltpu.SMEM if at in smem else pltpu.VMEM)
        for at in range(len(args))
    ]
    return pl.pallas_call(
        kernel,
        out_shape=outs,
        in_specs=specs,
        out_specs=jax.tree.map(lambda _: pl.BlockSpec(memory_space=pltpu.VMEM), outs),
        compiler_params=pltpu.CompilerParams(vmem_limit_bytes=48 * 1024 * 1024),
        cost_estimate=pl.CostEstimate(
            flops=flops, bytes_accessed=bytes_accessed, transcendentals=0
        ),
    )(*args)


def dot(a, b, dims, precision=None):
    return lax.dot_general(
        a, b, (dims, ((), ())), precision=precision, preferred_element_type=jnp.float32
    )


def expander(heads, channels):
    row = lax.broadcasted_iota(jnp.int32, (heads, channels), 0)
    column = lax.broadcasted_iota(jnp.int32, (heads, channels), 1)
    return jnp.where(column // (channels // heads) == row, 1.0, 0.0)


def project_kernel(mine_ref, feats_ref, w_ref, keep_ref, send_ref, bc_ref, dt_ref, acc, bc_acc, dt_acc):
    step = pl.program_id(0)
    mine = mine_ref[0]
    channels = keep_ref.shape[1]
    bc_rows = bc_ref.shape[0]

    @pl.when(step == 0)
    def _():
        acc[...] = jnp.zeros_like(acc)
        bc_acc[...] = jnp.zeros_like(bc_acc)
        dt_acc[...] = jnp.zeros_like(dt_acc)

    weights = w_ref[0, 0:channels, :]
    for half in range(2):
        acc[half] += dot(feats_ref[0, half, 0], weights, ((1,), (0,)))
    own = feats_ref[0, mine, 0]
    bc_acc[...] += dot(w_ref[0, channels : channels + bc_rows, :], own, ((1,), (1,)))
    dt_acc[...] += dot(w_ref[0, channels + bc_rows :, :], own[HALO:], ((1,), (1,)))

    @pl.when(step == pl.num_programs(0) - 1)
    def _():
        keep_ref[...] = acc[mine].astype(jnp.bfloat16)
        send_ref[...] = acc[1 - mine].astype(jnp.bfloat16)
        bc_ref[...] = bc_acc[...].astype(jnp.bfloat16)
        dt_ref[...] = dt_acc[...]


def project(mine, feats, weights, bc_rows, dt_rows):
    _, _, _, rows, depth = feats.shape
    blocks, height, channels = weights.shape
    tokens = rows - HALO
    return pl.pallas_call(
        project_kernel,
        grid_spec=pltpu.PrefetchScalarGridSpec(
            num_scalar_prefetch=1,
            grid=(blocks,),
            in_specs=[
                pl.BlockSpec((1, 2, 1, rows, depth), lambda j, m: (j // 2, 0, j % 2, 0, 0)),
                pl.BlockSpec((1, height, channels), lambda j, m: (j, 0, 0)),
            ],
            out_specs=[
                pl.BlockSpec((rows, channels), lambda j, m: (0, 0)),
                pl.BlockSpec((rows, channels), lambda j, m: (0, 0)),
                pl.BlockSpec((bc_rows, rows), lambda j, m: (0, 0)),
                pl.BlockSpec((dt_rows, tokens), lambda j, m: (0, 0)),
            ],
            scratch_shapes=[
                pltpu.VMEM((2, rows, channels), jnp.float32),
                pltpu.VMEM((bc_rows, rows), jnp.float32),
                pltpu.VMEM((dt_rows, tokens), jnp.float32),
            ],
        ),
        out_shape=[
            jax.ShapeDtypeStruct((rows, channels), jnp.bfloat16),
            jax.ShapeDtypeStruct((rows, channels), jnp.bfloat16),
            jax.ShapeDtypeStruct((bc_rows, rows), jnp.bfloat16),
            jax.ShapeDtypeStruct((dt_rows, tokens), jnp.float32),
        ],
        compiler_params=pltpu.CompilerParams(vmem_limit_bytes=48 * 1024 * 1024),
    )(mine, feats, weights)


def convolved(values, taps, tokens):
    summed = taps[0:1] * values[HALO - 3 : HALO - 3 + tokens]
    for k in range(1, 4):
        summed = summed + taps[k : k + 1] * values[HALO - 3 + k : HALO - 3 + k + tokens]
    return (summed / (1.0 + jnp.exp(-summed))).astype(jnp.bfloat16)


def state_kernel(
    mine_ref, keep_ref, got_ref, bc_ref, dt_ref, conv_x_ref, conv_bc_ref, bias_ref, rate_ref,
    x_ref, bconv_ref, cum_ref, step_ref, pay_ref, added_ref,
):
    mine = mine_ref[0]
    tokens, channels = x_ref.shape
    half = channels // 2
    heads = dt_ref.shape[0]
    for lane in range(0, channels, 128):
        at = lane % half
        own, got = keep_ref[:, at : at + 128], got_ref[:, at : at + 128]
        values = jnp.where(mine == lane // half, own, got).astype(jnp.float32)
        x_ref[:, lane : lane + 128] = convolved(values, conv_x_ref[:, lane : lane + 128], tokens)
    for lane in range(0, 2 * N, 128):
        values = bc_ref[:, lane : lane + 128].astype(jnp.float32)
        bconv_ref[:, lane : lane + 128] = convolved(
            values, conv_bc_ref[:, lane : lane + 128], tokens
        )
    raw = dt_ref[...] + bias_ref[...]
    step_size = jnp.maximum(raw, 0.0) + jnp.log1p(jnp.exp(-jnp.abs(raw)))
    log_decay = -step_size * rate_ref[...]
    step_ref[...] = step_size
    upper = jnp.where(
        lax.broadcasted_iota(jnp.int32, (GROUP, GROUP), 0)
        <= lax.broadcasted_iota(jnp.int32, (GROUP, GROUP), 1),
        1.0,
        0.0,
    )
    spread = expander(heads, channels)
    ends = []
    for block in range(tokens // GROUP):
        at = slice(block * GROUP, (block + 1) * GROUP)
        cumulative = dot(log_decay[:, at], upper, ((1,), (0,)), HIGHEST)
        cum_ref[:, at] = cumulative
        end = cumulative[:, GROUP - 1 : GROUP]
        to_end = jnp.exp(end - cumulative) * step_size[:, at]
        wide = dot(to_end.T, spread, ((1,), (0,)), HIGHEST)
        scaled = (x_ref[at, :].astype(jnp.float32) * wide).astype(jnp.bfloat16)
        added_ref[block] = dot(scaled, bconv_ref[at, 0:N], ((0,), (0,)))
        ends.append(end)
    second = jnp.exp(ends[1])
    total = jnp.exp(ends[0] + ends[1])
    high = total.astype(jnp.bfloat16).astype(jnp.float32)
    low = total - high
    share = pay_ref.shape[0] // heads
    row = lax.broadcasted_iota(jnp.int32, (16, N), 0)
    for head in range(heads):
        at = slice(head * HEAD, (head + 1) * HEAD)
        state = added_ref[0, at] * second[head : head + 1] + added_ref[1, at]
        tail = jnp.where(
            row == 0, high[head : head + 1], jnp.where(row == 1, low[head : head + 1], 0.0)
        ).astype(jnp.bfloat16)
        for part in range(share):
            pay_ref[head * share + part, 0:16] = state[part * 16 : (part + 1) * 16].astype(
                jnp.bfloat16
            )
            pay_ref[head * share + part, 16:32] = tail


def prefix_kernel(got_ref, start_ref, out_ref):
    running = start_ref[...]
    for source in range(got_ref.shape[0]):
        out_ref[source] = running.astype(jnp.bfloat16)
        tail = got_ref[source, 16:32].astype(jnp.float32)
        running = (tail[0:1] + tail[1:2]) * running + got_ref[source, 0:16].astype(jnp.float32)


def inside_kernel(x_ref, bc_ref, cum_ref, step_ref, out_ref):
    tokens, channels = x_ref.shape
    heads = cum_ref.shape[0]
    causal = lax.broadcasted_iota(jnp.int32, (GROUP, GROUP), 0) >= lax.broadcasted_iota(
        jnp.int32, (GROUP, GROUP), 1
    )
    for block in range(tokens // GROUP):
        at = slice(block * GROUP, (block + 1) * GROUP)
        scores = dot(bc_ref[at, N:], bc_ref[at, 0:N], ((1,), (1,)))
        cumulative = cum_ref[:, at]
        columns = cumulative.T
        for pair in range(0, heads, 2):
            parts = []
            for head in (pair, pair + 1):
                differ = columns[:, head : head + 1] - cumulative[head : head + 1]
                decays = jnp.exp(jnp.where(causal, differ, -1e30))
                mixing = (scores * decays * step_ref[head : head + 1, at]).astype(jnp.bfloat16)
                parts.append(
                    dot(mixing, x_ref[at, head * HEAD : (head + 1) * HEAD], ((1,), (0,)))
                )
            out_ref[at, pair * HEAD : (pair + 2) * HEAD] = jnp.concatenate(parts, 1)


def output_kernel(
    inside_ref, x_ref, bc_ref, cum_ref, entering_ref, added_ref, skip_ref, gain_ref, steer_ref,
    normed_ref, dot_ref, state_ref,
):
    tokens, channels = x_ref.shape
    heads = cum_ref.shape[0]
    spread = expander(heads, channels)
    end = jnp.exp(cum_ref[:, GROUP - 1 : GROUP])
    state_ref[0] = entering_ref[...].astype(jnp.float32)
    for head in range(heads):
        at = slice(head * HEAD, (head + 1) * HEAD)
        state_ref[1, at] = state_ref[0, at] * end[head : head + 1] + added_ref[at]
    for block in range(tokens // GROUP):
        at = slice(block * GROUP, (block + 1) * GROUP)
        carried = dot(
            bc_ref[at, N:].astype(jnp.float32), state_ref[block], ((1,), (1,)), HIGHEST
        )
        growth = dot(jnp.exp(cum_ref[:, at]).T, spread, ((1,), (0,)), HIGHEST)
        y = inside_ref[at] + growth * carried + skip_ref[...] * x_ref[at].astype(jnp.float32)
        squares = dot(y * y, spread, ((1,), (1,)), HIGHEST) * (1.0 / HEAD)
        scale = dot(lax.rsqrt(squares + EPSILON), spread, ((1,), (0,)), HIGHEST)
        normed = y * scale * gain_ref[...]
        normed_ref[at] = normed
        dot_ref[:, at] = dot(steer_ref[...], normed, ((1,), (1,)), HIGHEST)


def steer_kernel(factor, normed_ref, dots_ref, steer_ref, out_ref):
    for lane in range(0, normed_ref.shape[1], 256):
        at = slice(lane, lane + 256)
        penalty = dot(dots_ref[...], steer_ref[:, at], ((0,), (0,)), HIGHEST)
        out_ref[:, at] = (normed_ref[:, at] - penalty * factor).astype(jnp.bfloat16)


def per_device(
    tokens, x_weight, bc_weight, dt_weight, conv_x, conv_bc, dt_bias, decay_rate, d_skip,
    norm_gain, initial_state, steer,
):
    local, width = tokens.shape
    k_rows, channels = x_weight.shape
    half = channels // 2
    heads = dt_weight.shape[1]
    bc_rows = bc_weight.shape[1]
    small = bc_rows + heads
    seq_count = SIZES["z"] * SIZES["x"] * SIZES["yl"]
    tp_count = SIZES["yh"] * SIZES["c"]
    mine = lax.axis_index("yl").astype(jnp.int32).reshape(1)

    earlier = lax.ppermute(
        tokens[local - HALO :], SEQ, [(i, i + 1) for i in range(seq_count - 1)]
    )
    extended = jnp.concatenate([earlier, tokens], 0)
    feats = lax.all_gather(extended, ("yh", "yl", "c"), axis=0, tiled=False)
    feats = feats.reshape(SIZES["yh"], 2, SIZES["c"], local + HALO, width)

    fan = SIZES["x"] * SIZES["yl"]
    packed_rows = small * k_rows // half
    packed = jnp.concatenate([bc_weight, dt_weight], 1).T.reshape(packed_rows, half)
    panel = jnp.concatenate(
        [
            x_weight.reshape(k_rows, 2, half).transpose(1, 0, 2),
            jnp.broadcast_to(packed[None], (2, packed_rows, half)),
            jnp.zeros((2, -packed_rows % 8, half), jnp.bfloat16),
        ],
        1,
    )
    panel = jnp.broadcast_to(panel[None], (SIZES["x"],) + panel.shape).reshape(
        fan, panel.shape[1], half
    )
    got = lax.all_to_all(panel, ("x", "yl"), 0, 0)
    tall = got[:, :k_rows].reshape(fan * k_rows, half)
    flat = got[:, k_rows : k_rows + packed_rows].reshape(
        fan, packed_rows, half // k_rows, k_rows
    )
    flat = flat.transpose(1, 2, 0, 3).reshape(small, fan * k_rows)
    block = jnp.concatenate([tall, flat], 0)
    weights = lax.all_gather(block, "z", axis=0, tiled=False)

    keep, send, bc_pre, dt_raw = project(mine, feats, weights, bc_rows, heads)
    other = lax.ppermute(send, "yl", [(0, 1), (1, 0)])
    bc_all = lax.all_to_all(jnp.broadcast_to(bc_pre[None], (tp_count,) + bc_pre.shape), TP, 0, 0)
    bc_all = bc_all.reshape(tp_count * bc_rows, local + HALO).T

    f32, bf16 = jnp.float32, jnp.bfloat16
    x_conv, bc_conv, cumulative, step_size, payload, added = call(
        state_kernel,
        [
            jax.ShapeDtypeStruct((local, channels), bf16),
            jax.ShapeDtypeStruct((local, 2 * N), bf16),
            jax.ShapeDtypeStruct((heads, local), f32),
            jax.ShapeDtypeStruct((heads, local), f32),
            jax.ShapeDtypeStruct((seq_count, 32, N), bf16),
            jax.ShapeDtypeStruct((local // GROUP, channels, N), f32),
        ],
        mine, keep, other, bc_all, dt_raw, conv_x, conv_bc, dt_bias[:, None], decay_rate[:, None],
        smem=(0,),
    )
    states = lax.all_to_all(payload, SEQ, 0, 0)
    share = channels // seq_count
    start = lax.dynamic_slice_in_dim(
        initial_state.reshape(channels, N), lax.axis_index(SEQ) * share, share, 0
    )
    pieces = call(prefix_kernel, jax.ShapeDtypeStruct((seq_count, share, N), bf16), states, start)
    entering = lax.all_to_all(pieces, SEQ, 0, 0).reshape(channels, N)

    inside = call(
        inside_kernel,
        jax.ShapeDtypeStruct((local, channels), f32),
        x_conv, bc_conv, cumulative, step_size,
        flops=2 * heads * local * GROUP * HEAD, bytes_accessed=4 * local * channels,
    )
    normed, dots, _ = call(
        output_kernel,
        [
            jax.ShapeDtypeStruct((local, channels), f32),
            jax.ShapeDtypeStruct((1, local), f32),
            jax.ShapeDtypeStruct((2, channels, N), f32),
        ],
        inside, x_conv, bc_conv, cumulative, entering, added[0],
        jnp.repeat(d_skip, HEAD)[None], norm_gain[None], steer[None],
    )
    partials = lax.all_to_all(jnp.broadcast_to(dots[None], (tp_count, 1, local)), TP, 0, 0)
    factor = 1.0 / math.sqrt(channels * tp_count)
    return call(
        functools.partial(steer_kernel, factor),
        jax.ShapeDtypeStruct((local, channels), bf16),
        normed, partials.reshape(tp_count, local),
        jnp.broadcast_to(steer[None], (tp_count, channels)),
    )


def solution(mesh):
    fine = Mesh(mesh.devices.reshape(tuple(SIZES.values())), tuple(SIZES))
    both = P(SEQ, TP)
    placed = (
        both, both, both, both, P(None, TP), P(), P(TP), P(TP), P(TP), P(TP),
        P(TP, None, None), P(TP),
    )
    return jax.shard_map(
        per_device, mesh=fine, in_specs=placed, out_specs=both, check_vma=False
    )
```

```python
import functools
import math

import jax
import jax.numpy as jnp
from jax import lax
from jax.experimental import pallas as pl
from jax.experimental.pallas import tpu as pltpu
from jax.sharding import Mesh, PartitionSpec as P

EPSILON = 1e-05
GROUP = 128
N = 128
HALO = 16
HEAD = 64
HIGHEST = lax.Precision.HIGHEST

SEQ = ("z", "x", "yl")
TP = ("yh", "c")
SIZES = {"z": 8, "x": 4, "yl": 2, "yh": 4, "c": 2}


def call(kernel, outs, scalars, *args, blocks=None, scratch=(), flops=0, bytes_accessed=0):
    blocks = blocks or {}
    specs = [
        pl.BlockSpec(*blocks[at])
        if at in blocks
        else pl.BlockSpec(arg.shape, functools.partial(lambda rank, i, s: (0,) * rank, arg.ndim))
        for at, arg in enumerate(args)
    ]
    whole = [
        pl.BlockSpec(out.shape, functools.partial(lambda rank, i, s: (0,) * rank, len(out.shape)))
        for out in outs
    ]
    return pl.pallas_call(
        kernel,
        grid_spec=pltpu.PrefetchScalarGridSpec(
            num_scalar_prefetch=1,
            grid=(1,),
            in_specs=specs,
            out_specs=whole,
            scratch_shapes=list(scratch),
        ),
        out_shape=outs,
        compiler_params=pltpu.CompilerParams(vmem_limit_bytes=48 * 1024 * 1024),
        cost_estimate=pl.CostEstimate(
            flops=flops, bytes_accessed=bytes_accessed, transcendentals=0
        ),
    )(scalars, *args)


def dot(a, b, dims, precision=None):
    return lax.dot_general(
        a, b, (dims, ((), ())), precision=precision, preferred_element_type=jnp.float32
    )


def expander(heads, channels):
    row = lax.broadcasted_iota(jnp.int32, (heads, channels), 0)
    column = lax.broadcasted_iota(jnp.int32, (heads, channels), 1)
    return jnp.where(column // (channels // heads) == row, 1.0, 0.0)


def project_kernel(
    where_ref, own_ref, other_ref, w0, w1, w2, w3, w4, w5, w6, w7, w8,
    x_ref, bc_ref, dt_ref, weights, acc, bc_acc, dt_acc, sem,
):
    step = pl.program_id(0)
    blocks = weights.shape[0]
    channels = x_ref.shape[2]
    bc_rows, dt_rows = bc_ref.shape[0], dt_ref.shape[0]
    rows = x_ref.shape[1]
    tokens = rows - HALO
    cut = w7.shape[0]
    copies = [
        [pltpu.make_async_copy(ref, weights.at[at], sem.at[at])]
        for at, ref in enumerate((w0, w1, w2, w3, w4, w5, w6))
    ]
    copies.append(
        [
            pltpu.make_async_copy(w7, weights.at[7, 0:cut], sem.at[7]),
            pltpu.make_async_copy(w8, weights.at[7, cut:], sem.at[8]),
        ]
    )

    @pl.when(step == 0)
    def _():
        for group in copies:
            for copy in group:
                copy.start()
        acc[...] = jnp.zeros_like(acc)
        bc_acc[...] = jnp.zeros_like(bc_acc)
        dt_acc[...] = jnp.zeros_like(dt_acc)

    for at, group in enumerate(copies):

        @pl.when(step == at)
        def _():
            for copy in group:
                copy.wait()

    mine = where_ref[blocks + step] == 1
    for half in range(2):
        feats = jnp.where(mine, own_ref[0, half], other_ref[0, half])
        acc[half] += dot(feats, weights[step, 0:channels], ((1,), (0,)))
        bc_acc[half] += dot(
            weights[step, channels : channels + bc_rows], feats, ((1,), (1,))
        )
        dt_acc[half] += dot(weights[step, channels + bc_rows :], feats[HALO:], ((1,), (1,)))

    @pl.when(step == blocks - 1)
    def _():
        x_ref[...] = acc[...].astype(jnp.bfloat16)
        for half in range(2):
            bc_ref[:, half, :] = bc_acc[half].astype(jnp.bfloat16)
            dt_ref[:, half * tokens : (half + 1) * tokens] = dt_acc[half]


def project(where, own, other, weights, bc_rows, dt_rows):
    _, _, rows, depth = own.shape
    height, channels = weights[0].shape
    blocks = len(weights) - 1
    tokens = rows - HALO
    feat = pl.BlockSpec((1, 2, rows, depth), lambda j, m: (m[j], 0, 0, 0))
    return pl.pallas_call(
        project_kernel,
        grid_spec=pltpu.PrefetchScalarGridSpec(
            num_scalar_prefetch=1,
            grid=(blocks,),
            in_specs=[feat, feat] + [pl.BlockSpec(memory_space=pl.ANY)] * len(weights),
            out_specs=[
                pl.BlockSpec((2, rows, channels), lambda j, m: (0, 0, 0)),
                pl.BlockSpec((bc_rows, 2, rows), lambda j, m: (0, 0, 0)),
                pl.BlockSpec((dt_rows, 2 * tokens), lambda j, m: (0, 0)),
            ],
            scratch_shapes=[
                pltpu.VMEM((blocks, height, channels), jnp.bfloat16),
                pltpu.VMEM((2, rows, channels), jnp.float32),
                pltpu.VMEM((2, bc_rows, rows), jnp.float32),
                pltpu.VMEM((2, dt_rows, tokens), jnp.float32),
                pltpu.SemaphoreType.DMA((blocks + 1,)),
            ],
        ),
        out_shape=[
            jax.ShapeDtypeStruct((2, rows, channels), jnp.bfloat16),
            jax.ShapeDtypeStruct((bc_rows, 2, rows), jnp.bfloat16),
            jax.ShapeDtypeStruct((dt_rows, 2 * tokens), jnp.float32),
        ],
        compiler_params=pltpu.CompilerParams(vmem_limit_bytes=48 * 1024 * 1024),
    )(where, own, other, *weights)


def convolved(values, taps, tokens):
    summed = taps[0:1] * values[HALO - 3 : HALO - 3 + tokens]
    for k in range(1, 4):
        summed = summed + taps[k : k + 1] * values[HALO - 3 + k : HALO - 3 + k + tokens]
    return (summed / (1.0 + jnp.exp(-summed))).astype(jnp.bfloat16)


def state_kernel(
    mine_ref, pre_ref, bc_ref, dt_ref, conv_x_ref, conv_bc_ref, bias_ref, rate_ref,
    x_ref, bconv_ref, cum_ref, step_ref, pay_ref, added_ref,
):
    tokens, channels = x_ref.shape
    halves, rows, _ = pre_ref.shape
    local = tokens // halves
    heads = dt_ref.shape[0]
    for part in range(halves):
        at = slice(part * local, (part + 1) * local)
        for lane in range(0, channels, 128):
            on = slice(lane, lane + 128)
            values = pre_ref[part, :, on].astype(jnp.float32)
            x_ref[at, on] = convolved(values, conv_x_ref[:, on], local)
        for lane in range(0, 2 * N, 128):
            on = slice(lane, lane + 128)
            values = bc_ref[part, :, on].astype(jnp.float32)
            bconv_ref[at, on] = convolved(values, conv_bc_ref[:, on], local)
    raw = dt_ref[...] + bias_ref[...]
    step_size = jnp.maximum(raw, 0.0) + jnp.log1p(jnp.exp(-jnp.abs(raw)))
    log_decay = -step_size * rate_ref[...]
    step_ref[...] = step_size
    upper = jnp.where(
        lax.broadcasted_iota(jnp.int32, (GROUP, GROUP), 0)
        <= lax.broadcasted_iota(jnp.int32, (GROUP, GROUP), 1),
        1.0,
        0.0,
    )
    spread = expander(heads, channels)
    ends = []
    for block in range(tokens // GROUP):
        at = slice(block * GROUP, (block + 1) * GROUP)
        cumulative = dot(log_decay[:, at], upper, ((1,), (0,)), HIGHEST)
        cum_ref[:, at] = cumulative
        end = cumulative[:, GROUP - 1 : GROUP]
        to_end = jnp.exp(end - cumulative) * step_size[:, at]
        wide = dot(to_end.T, spread, ((1,), (0,)), HIGHEST)
        scaled = (x_ref[at, :].astype(jnp.float32) * wide).astype(jnp.bfloat16)
        added_ref[block] = dot(scaled, bconv_ref[at, 0:N], ((0,), (0,)))
        ends.append(end)
    growths = [jnp.exp(end) for end in ends]
    total = jnp.exp(functools.reduce(lambda p, q: p + q, ends))
    high = total.astype(jnp.bfloat16).astype(jnp.float32)
    low = total - high
    share = pay_ref.shape[0] // heads
    tail_rows = pay_ref.shape[1] - 16
    row = lax.broadcasted_iota(jnp.int32, (tail_rows, N), 0)
    for head in range(heads):
        at = slice(head * HEAD, (head + 1) * HEAD)
        state = added_ref[0, at]
        for block in range(1, tokens // GROUP):
            state = state * growths[block][head : head + 1] + added_ref[block, at]
        tail = jnp.where(
            row == 0, high[head : head + 1], jnp.where(row == 1, low[head : head + 1], 0.0)
        ).astype(jnp.bfloat16)
        for part in range(share):
            pay_ref[head * share + part, 0:16] = state[part * 16 : (part + 1) * 16].astype(
                jnp.bfloat16
            )
            pay_ref[head * share + part, 16:] = tail


def prefix_kernel(at_ref, got_ref, start_ref, out_ref):
    running = start_ref[...]
    for source in range(got_ref.shape[0]):
        out_ref[source] = running.astype(jnp.bfloat16)
        tail = got_ref[source, 16:].astype(jnp.float32)
        running = (tail[0:1] + tail[1:2]) * running + got_ref[source, 0:16].astype(jnp.float32)


def inside_kernel(mine_ref, x_ref, bc_ref, cum_ref, step_ref, out_ref):
    tokens, channels = x_ref.shape
    heads = cum_ref.shape[0]
    causal = lax.broadcasted_iota(jnp.int32, (GROUP, GROUP), 0) >= lax.broadcasted_iota(
        jnp.int32, (GROUP, GROUP), 1
    )
    for block in range(tokens // GROUP):
        at = slice(block * GROUP, (block + 1) * GROUP)
        scores = dot(bc_ref[at, N:], bc_ref[at, 0:N], ((1,), (1,)))
        cumulative = cum_ref[:, at]
        columns = cumulative.T
        for pair in range(0, heads, 2):
            parts = []
            for head in (pair, pair + 1):
                differ = columns[:, head : head + 1] - cumulative[head : head + 1]
                decays = jnp.exp(jnp.where(causal, differ, -1e30))
                mixing = (scores * decays * step_ref[head : head + 1, at]).astype(jnp.bfloat16)
                parts.append(
                    dot(mixing, x_ref[at, head * HEAD : (head + 1) * HEAD], ((1,), (0,)))
                )
            out_ref[at, pair * HEAD : (pair + 2) * HEAD] = jnp.concatenate(parts, 1)


def output_kernel(
    mine_ref, inside_ref, x_ref, bc_ref, cum_ref, entering_ref, added_ref, skip_ref, gain_ref,
    steer_ref, keep_ref, send_ref, dot_ref, state_ref,
):
    mine = mine_ref[0]
    tokens, channels = x_ref.shape
    local = tokens // 2
    heads = cum_ref.shape[0]
    spread = expander(heads, channels)
    state_ref[...] = entering_ref[...].astype(jnp.float32)
    for block in range(tokens // GROUP):
        at = slice(block * GROUP, (block + 1) * GROUP)
        carried = dot(bc_ref[at, N:].astype(jnp.float32), state_ref[...], ((1,), (1,)), HIGHEST)
        growth = dot(jnp.exp(cum_ref[:, at]).T, spread, ((1,), (0,)), HIGHEST)
        y = inside_ref[at] + growth * carried + skip_ref[...] * x_ref[at].astype(jnp.float32)
        squares = dot(y * y, spread, ((1,), (1,)), HIGHEST) * (1.0 / HEAD)
        scale = dot(lax.rsqrt(squares + EPSILON), spread, ((1,), (0,)), HIGHEST)
        normed = y * scale * gain_ref[...]
        part = block * GROUP // local
        on = slice(block * GROUP - part * local, (block + 1) * GROUP - part * local)

        @pl.when(mine == part)
        def _():
            keep_ref[on] = normed

        @pl.when(mine != part)
        def _():
            send_ref[on] = normed.astype(jnp.bfloat16)

        dot_ref[part, :, on] = dot(steer_ref[...], normed, ((1,), (1,)), HIGHEST)
        if block + 1 < tokens // GROUP:
            end = jnp.exp(cum_ref[:, (block + 1) * GROUP - 1 : (block + 1) * GROUP])
            for head in range(heads):
                rows = slice(head * HEAD, (head + 1) * HEAD)
                state_ref[rows] = state_ref[rows] * end[head : head + 1] + added_ref[block, rows]


def steer_kernel(factor, mine_ref, keep_ref, other_ref, dots_ref, steer_ref, out_ref):
    first = mine_ref[0] == 0
    half = keep_ref.shape[1]
    for lane in range(0, half, 256):
        at = slice(lane, lane + 256)
        later = slice(half + lane, half + lane + 256)
        own, other = keep_ref[:, at], other_ref[:, at].astype(jnp.float32)
        left, right = jnp.where(first, own, other), jnp.where(first, other, own)
        for on, normed in ((at, left), (later, right)):
            penalty = dot(dots_ref[...], steer_ref[:, on], ((0,), (0,)), HIGHEST)
            out_ref[:, on] = (normed - penalty * factor).astype(jnp.bfloat16)


def ring(block, axis):
    count = SIZES[axis]
    forward = [(i, (i + 1) % count) for i in range(count)]
    backward = [(i, (i - 1) % count) for i in range(count)]
    pieces, offsets = [block], [0]
    ahead = behind = block
    for hop in range(1, count // 2):
        ahead = lax.ppermute(ahead, axis, forward)
        behind = lax.ppermute(behind, axis, backward)
        pieces += [ahead, behind]
        offsets += [-hop, hop]
    cut = (block.shape[0] // 2 + 15) // 16 * 16
    pieces.append(lax.ppermute(ahead[:cut], axis, forward))
    pieces.append(lax.ppermute(behind[cut:], axis, backward))
    offsets.append(count // 2)
    return pieces, offsets


def per_device(
    tokens, x_weight, bc_weight, dt_weight, conv_x, conv_bc, dt_bias, decay_rate, d_skip,
    norm_gain, initial_state, steer,
):
    local, width = tokens.shape
    k_rows, channels = x_weight.shape
    half = channels // 2
    heads = dt_weight.shape[1] // 2
    bc_rows = bc_weight.shape[1] // 2
    small = bc_rows + heads
    seq_count = SIZES["z"] * SIZES["x"] * SIZES["yl"]
    tp_count = SIZES["yh"] * SIZES["c"]
    z, core = lax.axis_index("z"), lax.axis_index("c")
    mine = lax.axis_index("yl").astype(jnp.int32).reshape(1)
    f32, bf16 = jnp.float32, jnp.bfloat16

    earlier = lax.ppermute(
        tokens[local - HALO :], SEQ, [(i, i + 1) for i in range(seq_count - 1)]
    )
    extended = jnp.concatenate([earlier, tokens], 0)
    line = SIZES["yh"] * 2
    own = lax.all_to_all(
        jnp.broadcast_to(extended[None], (line,) + extended.shape), ("yh", "yl"), 0, 0
    ).reshape(SIZES["yh"], 2, local + HALO, width)
    other = lax.ppermute(own, "c", [(0, 1), (1, 0)])

    fan = SIZES["x"] * SIZES["yl"]
    packed_rows = small * k_rows // half
    packed = jnp.concatenate(
        [
            bc_weight.reshape(k_rows, 2, bc_rows).transpose(1, 2, 0),
            dt_weight.reshape(k_rows, 2, heads).transpose(1, 2, 0),
        ],
        1,
    ).reshape(2, packed_rows, half)
    panel = jnp.concatenate(
        [
            x_weight.reshape(k_rows, 2, half).transpose(1, 0, 2),
            packed,
            jnp.zeros((2, -packed_rows % 8, half), bf16),
        ],
        1,
    )
    panel = jnp.broadcast_to(panel[None], (SIZES["x"],) + panel.shape).reshape(
        fan, panel.shape[1], half
    )
    got = lax.all_to_all(panel, ("x", "yl"), 0, 0)
    tall = got[:, :k_rows].reshape(fan * k_rows, half)
    flat = got[:, k_rows : k_rows + packed_rows].reshape(
        fan, packed_rows, half // k_rows, k_rows
    )
    flat = flat.transpose(1, 2, 0, 3).reshape(small, fan * k_rows)
    pieces, offsets = ring(jnp.concatenate([tall, flat], 0), "z")
    source = (z + jnp.array(offsets, jnp.int32)) % SIZES["z"]
    where = jnp.concatenate([source // 2, (source % 2 == core).astype(jnp.int32)])

    x_pre, bc_pre, dt_raw = project(where, own, other, pieces, bc_rows, heads)
    bc_all = lax.all_to_all(
        jnp.broadcast_to(
            bc_pre.reshape(1, bc_rows, -1), (2 * tp_count, bc_rows, 2 * (local + HALO))
        ),
        ("yh", "c", "yl"), 0, 0,
    )
    bc_all = bc_all.reshape(2 * N, -1).T.reshape(2, local + HALO, 2 * N)

    pair = 2 * local
    plane = SIZES["z"] * SIZES["x"]
    share = half // plane
    halves = {
        3: ((conv_x.shape[0], half), lambda i, s: (0, s[0])),
        5: ((heads, 1), lambda i, s: (s[0], 0)),
        6: ((heads, 1), lambda i, s: (s[0], 0)),
    }
    x_conv, bc_conv, cumulative, step_size, payload, added = call(
        state_kernel,
        [
            jax.ShapeDtypeStruct((pair, half), bf16),
            jax.ShapeDtypeStruct((pair, 2 * N), bf16),
            jax.ShapeDtypeStruct((heads, pair), f32),
            jax.ShapeDtypeStruct((heads, pair), f32),
            jax.ShapeDtypeStruct((plane, share + 8, N), bf16),
            jax.ShapeDtypeStruct((pair // GROUP, half, N), f32),
        ],
        mine, x_pre, bc_all, dt_raw, conv_x, conv_bc, dt_bias[:, None], decay_rate[:, None],
        blocks=halves,
    )
    states = lax.all_to_all(payload, ("z", "x"), 0, 0)
    place = mine * plane + lax.axis_index(("z", "x")).astype(jnp.int32)
    (prefixes,) = call(
        prefix_kernel,
        [jax.ShapeDtypeStruct((plane, share, N), bf16)],
        place, states, initial_state.reshape(channels, N),
        blocks={1: ((share, N), lambda i, s: (s[0], 0))},
    )
    entering = lax.all_to_all(prefixes, ("z", "x"), 0, 0).reshape(half, N)

    (inside,) = call(
        inside_kernel,
        [jax.ShapeDtypeStruct((pair, half), f32)],
        mine, x_conv, bc_conv, cumulative, step_size,
        flops=2 * heads * pair * GROUP * HEAD, bytes_accessed=4 * pair * half,
    )
    lanes = ((1, half), lambda i, s: (0, s[0]))
    keep, send, dots = call(
        output_kernel,
        [
            jax.ShapeDtypeStruct((local, half), f32),
            jax.ShapeDtypeStruct((local, half), bf16),
            jax.ShapeDtypeStruct((2, 1, local), f32),
        ],
        mine, inside, x_conv, bc_conv, cumulative, entering, added,
        jnp.repeat(d_skip, HEAD)[None], norm_gain[None], steer[None],
        blocks={6: lanes, 7: lanes, 8: lanes},
        scratch=[pltpu.VMEM((half, N), f32)],
    )
    swapped = lax.ppermute(send, "yl", [(0, 1), (1, 0)])
    shape = (SIZES["yh"], 2, SIZES["c"], 1, local)
    partials = lax.all_to_all(
        jnp.broadcast_to(dots[None, :, None], shape).reshape(2 * tp_count, 1, local),
        ("yh", "yl", "c"), 0, 0,
    )
    factor = 1.0 / math.sqrt(channels * tp_count)
    (out,) = call(
        functools.partial(steer_kernel, factor),
        [jax.ShapeDtypeStruct((local, channels), bf16)],
        mine, keep, swapped, partials.reshape(2 * tp_count, local),
        jnp.broadcast_to(steer[None], (2 * tp_count, channels)),
    )
    return out


def solution(mesh):
    fine = Mesh(mesh.devices.reshape(tuple(SIZES.values())), tuple(SIZES))
    both = P(SEQ, TP)
    placed = (
        both, both, both, both, P(None, TP), P(), P(TP), P(TP), P(TP), P(TP),
        P(TP, None, None), P(TP),
    )
    return jax.shard_map(
        per_device, mesh=fine, in_specs=placed, out_specs=both, check_vma=False
    )
```

```python
import functools
import math

import jax
import jax.numpy as jnp
from jax import lax
from jax.experimental import pallas as pl
from jax.experimental.pallas import tpu as pltpu
from jax.sharding import Mesh, PartitionSpec as P

EPSILON = 1e-05
GROUP = 128
N = 128
HALO = 16
HEAD = 64
HIGHEST = lax.Precision.HIGHEST

SEQ = ("z", "x", "yl")
TP = ("yh", "c")
SIZES = {"z": 8, "x": 4, "yl": 2, "yh": 4, "c": 2}


def call(kernel, outs, scalars, *args, blocks=None, scratch=(), flops=0, bytes_accessed=0):
    blocks = blocks or {}
    specs = [
        pl.BlockSpec(*blocks[at])
        if at in blocks
        else pl.BlockSpec(arg.shape, functools.partial(lambda rank, i, s: (0,) * rank, arg.ndim))
        for at, arg in enumerate(args)
    ]
    whole = [
        pl.BlockSpec(out.shape, functools.partial(lambda rank, i, s: (0,) * rank, len(out.shape)))
        for out in outs
    ]
    return pl.pallas_call(
        kernel,
        grid_spec=pltpu.PrefetchScalarGridSpec(
            num_scalar_prefetch=1,
            grid=(1,),
            in_specs=specs,
            out_specs=whole,
            scratch_shapes=list(scratch),
        ),
        out_shape=outs,
        compiler_params=pltpu.CompilerParams(vmem_limit_bytes=48 * 1024 * 1024),
        cost_estimate=pl.CostEstimate(
            flops=flops, bytes_accessed=bytes_accessed, transcendentals=0
        ),
    )(scalars, *args)


def dot(a, b, dims, precision=None):
    return lax.dot_general(
        a, b, (dims, ((), ())), precision=precision, preferred_element_type=jnp.float32
    )


def parts(value):
    high = value.astype(jnp.bfloat16)
    rest = value - high.astype(jnp.float32)
    middle = rest.astype(jnp.bfloat16)
    low = (rest - middle.astype(jnp.float32)).astype(jnp.bfloat16)
    return high, middle, low


def left_dot(value, exact, dims):
    return sum(dot(part, exact, dims) for part in parts(value))


def right_dot(exact, value, dims):
    return sum(dot(exact, part, dims) for part in parts(value))


def expander(heads, channels):
    row = lax.broadcasted_iota(jnp.int32, (heads, channels), 0)
    column = lax.broadcasted_iota(jnp.int32, (heads, channels), 1)
    return jnp.where(column // (channels // heads) == row, 1.0, 0.0).astype(jnp.bfloat16)


def project_kernel(
    where_ref, own_ref, other_ref, w0, w1, w2, w3, w4, w5, w6, w7, w8,
    x_ref, bc_ref, dt_ref, weights, acc, small, sem,
):
    step = pl.program_id(0)
    blocks = weights.shape[0]
    channels = x_ref.shape[2]
    bc_rows, dt_rows = bc_ref.shape[0], dt_ref.shape[0]
    rows = x_ref.shape[1]
    tokens = rows - HALO
    cut = w7.shape[0]
    copies = [
        [pltpu.make_async_copy(ref, weights.at[at], sem.at[at])]
        for at, ref in enumerate((w0, w1, w2, w3, w4, w5, w6))
    ]
    copies.append(
        [
            pltpu.make_async_copy(w7, weights.at[7, 0:cut], sem.at[7]),
            pltpu.make_async_copy(w8, weights.at[7, cut:], sem.at[8]),
        ]
    )

    @pl.when(step == 0)
    def _():
        for group in copies:
            for copy in group:
                copy.start()
        acc[...] = jnp.zeros_like(acc)
        small[...] = jnp.zeros_like(small)

    for at, group in enumerate(copies):

        @pl.when(step == at)
        def _():
            for copy in group:
                copy.wait()

    mine = where_ref[blocks + step] == 1
    for half in range(2):
        feats = jnp.where(mine, own_ref[0, half], other_ref[0, half])
        acc[half] += dot(feats, weights[step, 0:channels], ((1,), (0,)))
        small[half, 0:rows, 0 : bc_rows + dt_rows] += dot(
            feats, weights[step, channels:], ((1,), (1,))
        )

    @pl.when(step == blocks - 1)
    def _():
        x_ref[...] = acc[...].astype(jnp.bfloat16)
        for half in range(2):
            turned = small[half].T
            bc_ref[:, half, :] = turned[0:bc_rows, 0:rows].astype(jnp.bfloat16)
            turned = small[half, HALO:rows].T
            dt_ref[:, half * tokens : (half + 1) * tokens] = turned[bc_rows : bc_rows + dt_rows]


def project(where, own, other, weights, bc_rows, dt_rows):
    _, _, rows, depth = own.shape
    height, channels = weights[0].shape
    blocks = len(weights) - 1
    tokens = rows - HALO
    feat = pl.BlockSpec((1, 2, rows, depth), lambda j, m: (m[j], 0, 0, 0))
    return pl.pallas_call(
        project_kernel,
        grid_spec=pltpu.PrefetchScalarGridSpec(
            num_scalar_prefetch=1,
            grid=(blocks,),
            in_specs=[feat, feat] + [pl.BlockSpec(memory_space=pl.ANY)] * len(weights),
            out_specs=[
                pl.BlockSpec((2, rows, channels), lambda j, m: (0, 0, 0)),
                pl.BlockSpec((bc_rows, 2, rows), lambda j, m: (0, 0, 0)),
                pl.BlockSpec((dt_rows, 2 * tokens), lambda j, m: (0, 0)),
            ],
            scratch_shapes=[
                pltpu.VMEM((blocks, height, channels), jnp.bfloat16),
                pltpu.VMEM((2, rows, channels), jnp.float32),
                pltpu.VMEM((2, (rows + 127) // 128 * 128, 128), jnp.float32),
                pltpu.SemaphoreType.DMA((blocks + 1,)),
            ],
        ),
        out_shape=[
            jax.ShapeDtypeStruct((2, rows, channels), jnp.bfloat16),
            jax.ShapeDtypeStruct((bc_rows, 2, rows), jnp.bfloat16),
            jax.ShapeDtypeStruct((dt_rows, 2 * tokens), jnp.float32),
        ],
        compiler_params=pltpu.CompilerParams(vmem_limit_bytes=48 * 1024 * 1024),
    )(where, own, other, *weights)


def convolved(values, taps, tokens):
    summed = taps[0:1] * values[HALO - 3 : HALO - 3 + tokens]
    for k in range(1, 4):
        summed = summed + taps[k : k + 1] * values[HALO - 3 + k : HALO - 3 + k + tokens]
    return (summed / (1.0 + jnp.exp(-summed))).astype(jnp.bfloat16)


def conv_kernel(
    mine_ref, pre_ref, dt_ref, conv_ref, head_ref, x_ref, cum_ref, step_ref, scaled_ref
):
    tokens, channels = x_ref.shape
    halves, rows, _ = pre_ref.shape
    local = tokens // halves
    heads = dt_ref.shape[0]
    for part in range(halves):
        at = slice(part * local, (part + 1) * local)
        for lane in range(0, channels, 128):
            on = slice(lane, lane + 128)
            values = pre_ref[part, :, on].astype(jnp.float32)
            x_ref[at, on] = convolved(values, conv_ref[:, on], local)
    raw = dt_ref[...] + head_ref[:, 0:1]
    step_size = jnp.maximum(raw, 0.0) + jnp.log1p(jnp.exp(-jnp.abs(raw)))
    log_decay = -step_size * head_ref[:, 1:2]
    step_ref[...] = step_size
    upper = jnp.where(
        lax.broadcasted_iota(jnp.int32, (GROUP, GROUP), 0)
        <= lax.broadcasted_iota(jnp.int32, (GROUP, GROUP), 1),
        1.0,
        0.0,
    ).astype(jnp.bfloat16)
    spread = expander(heads, channels)
    for block in range(tokens // GROUP):
        at = slice(block * GROUP, (block + 1) * GROUP)
        cumulative = left_dot(log_decay[:, at], upper, ((1,), (0,)))
        cum_ref[:, at] = cumulative
        to_end = jnp.exp(cumulative[:, GROUP - 1 : GROUP] - cumulative) * step_size[:, at]
        wide = left_dot(to_end.T, spread, ((1,), (0,)))
        scaled = x_ref[at, :].astype(jnp.float32) * wide
        scaled_ref[:, at] = scaled.T.astype(jnp.bfloat16)


def state_kernel(
    mine_ref, bc_ref, conv_ref, cum_ref, scaled_ref, bconv_ref, pay_ref, local_ref
):
    halves, rows, _ = bc_ref.shape
    channels, tokens = scaled_ref.shape
    local = tokens // halves
    heads = cum_ref.shape[0]
    for part in range(halves):
        at = slice(part * local, (part + 1) * local)
        for lane in range(0, 2 * N, 128):
            on = slice(lane, lane + 128)
            values = bc_ref[part, :, on].astype(jnp.float32)
            bconv_ref[at, on] = convolved(values, conv_ref[:, on], local)
    total = jnp.zeros((heads, 1), jnp.float32)
    blocks = tokens // GROUP
    for block in range(blocks):
        at = slice(block * GROUP, (block + 1) * GROUP)
        added = dot(scaled_ref[:, at], bconv_ref[at, 0:N], ((1,), (0,)))
        end = cum_ref[:, (block + 1) * GROUP - 1 : (block + 1) * GROUP]
        total = total + end
        growth = jnp.exp(end)
        for head in range(heads):
            on = slice(head * HEAD, (head + 1) * HEAD)
            if block:
                local_ref[block, on] = (
                    local_ref[block - 1, on] * growth[head : head + 1] + added[on]
                )
            else:
                local_ref[block, on] = added[on]
    total = jnp.exp(total)
    high = total.astype(jnp.bfloat16).astype(jnp.float32)
    low = total - high
    share = pay_ref.shape[0] // heads
    tail_rows = pay_ref.shape[1] - 16
    row = lax.broadcasted_iota(jnp.int32, (tail_rows, N), 0)
    for head in range(heads):
        tail = jnp.where(
            row == 0, high[head : head + 1], jnp.where(row == 1, low[head : head + 1], 0.0)
        ).astype(jnp.bfloat16)
        for part in range(head * share, (head + 1) * share):
            pay_ref[part, 0:16] = local_ref[blocks - 1, part * 16 : (part + 1) * 16].astype(
                jnp.bfloat16
            )
            pay_ref[part, 16:] = tail


def prefix_kernel(at_ref, got_ref, start_ref, out_ref):
    running = start_ref[...]
    for source in range(got_ref.shape[0]):
        out_ref[source] = running.astype(jnp.bfloat16)
        tail = got_ref[source, 16:].astype(jnp.float32)
        running = (tail[0:1] + tail[1:2]) * running + got_ref[source, 0:16].astype(jnp.float32)


def inside_kernel(
    mine_ref, x_ref, bc_ref, cum_ref, step_ref, local_ref, chan_ref, out_ref, growth_ref
):
    tokens, channels = x_ref.shape
    heads = cum_ref.shape[0]
    spread = expander(heads, channels)
    causal = lax.broadcasted_iota(jnp.int32, (GROUP, GROUP), 0) >= lax.broadcasted_iota(
        jnp.int32, (GROUP, GROUP), 1
    )
    before = jnp.zeros((heads, 1), jnp.float32)
    for block in range(tokens // GROUP):
        at = slice(block * GROUP, (block + 1) * GROUP)
        c_block = bc_ref[at, N:]
        scores = dot(c_block, bc_ref[at, 0:N], ((1,), (1,)))
        cumulative = cum_ref[:, at]
        columns = cumulative.T
        growth_ref[at] = left_dot(jnp.exp(cumulative + before).T, spread, ((1,), (0,)))
        before = before + cumulative[:, GROUP - 1 : GROUP]
        rest = chan_ref[0:1] * x_ref[at].astype(jnp.float32)
        if block:
            carried = right_dot(c_block, local_ref[block - 1], ((1,), (1,)))
            rest = rest + left_dot(jnp.exp(columns), spread, ((1,), (0,))) * carried
        for pair in range(0, heads, 2):
            found = []
            for head in (pair, pair + 1):
                differ = columns[:, head : head + 1] - cumulative[head : head + 1]
                decays = jnp.exp(jnp.where(causal, differ, -1e30))
                mixing = (scores * decays * step_ref[head : head + 1, at]).astype(jnp.bfloat16)
                found.append(
                    dot(mixing, x_ref[at, head * HEAD : (head + 1) * HEAD], ((1,), (0,)))
                )
            on = slice(pair * HEAD, (pair + 2) * HEAD)
            out_ref[at, on] = jnp.concatenate(found, 1) + rest[:, on]


def output_kernel(
    mine_ref, inside_ref, growth_ref, bc_ref, entering_ref, chan_ref, keep_ref, send_ref, dot_ref
):
    mine = mine_ref[0]
    tokens, channels = inside_ref.shape
    local = tokens // 2
    spread = expander(channels // HEAD, channels)
    gain, steer = chan_ref[1:2], chan_ref[2:3]
    for block in range(tokens // GROUP):
        at = slice(block * GROUP, (block + 1) * GROUP)
        carried = dot(bc_ref[at, N:], entering_ref[...], ((1,), (1,)))
        y = inside_ref[at] + growth_ref[at] * carried
        squares = left_dot(y * y, spread, ((1,), (1,))) * (1.0 / HEAD)
        scale = left_dot(lax.rsqrt(squares + EPSILON), spread, ((1,), (0,)))
        normed = y * scale * gain
        part = block * GROUP // local
        on = slice(block * GROUP - part * local, (block + 1) * GROUP - part * local)

        @pl.when(mine == part)
        def _():
            keep_ref[on] = normed

        @pl.when(mine != part)
        def _():
            send_ref[on] = normed.astype(jnp.bfloat16)

        terms = normed * steer
        folded = terms[:, 0:128]
        for lane in range(128, channels, 128):
            folded = folded + terms[:, lane : lane + 128]
        dot_ref[part, :, on] = jnp.sum(folded.T, axis=0, keepdims=True)


def steer_kernel(factor, mine_ref, keep_ref, other_ref, dots_ref, chan_ref, out_ref):
    first = mine_ref[0] == 0
    half = keep_ref.shape[1]
    dots = dots_ref[...]
    for lane in range(0, half, 256):
        at = slice(lane, lane + 256)
        later = slice(half + lane, half + lane + 256)
        own, other = keep_ref[:, at], other_ref[:, at].astype(jnp.float32)
        left, right = jnp.where(first, own, other), jnp.where(first, other, own)
        for on, normed in ((at, left), (later, right)):
            steer = jnp.broadcast_to(chan_ref[2:3, on], (dots.shape[0], 256))
            penalty = dot(dots, steer, ((0,), (0,)), HIGHEST)
            out_ref[:, on] = (normed - penalty * factor).astype(jnp.bfloat16)


def ring(block, axis):
    count = SIZES[axis]
    forward = [(i, (i + 1) % count) for i in range(count)]
    backward = [(i, (i - 1) % count) for i in range(count)]
    pieces, offsets = [block], [0]
    ahead = behind = block
    for hop in range(1, count // 2):
        ahead = lax.ppermute(ahead, axis, forward)
        behind = lax.ppermute(behind, axis, backward)
        ahead, behind = lax.optimization_barrier((ahead, behind))
        pieces += [ahead, behind]
        offsets += [-hop, hop]
    cut = (block.shape[0] // 2 + 15) // 16 * 16
    pieces.append(lax.ppermute(ahead[:cut], axis, forward))
    pieces.append(lax.ppermute(behind[cut:], axis, backward))
    offsets.append(count // 2)
    return pieces, offsets


def per_device(
    tokens, x_weight, bc_weight, dt_weight, conv_x, conv_bc, dt_bias, decay_rate, d_skip,
    norm_gain, initial_state, steer,
):
    local, width = tokens.shape
    k_rows, channels = x_weight.shape
    half = channels // 2
    heads = dt_weight.shape[1] // 2
    bc_rows = bc_weight.shape[1] // 2
    small = bc_rows + heads
    seq_count = SIZES["z"] * SIZES["x"] * SIZES["yl"]
    tp_count = SIZES["yh"] * SIZES["c"]
    z, core = lax.axis_index("z"), lax.axis_index("c")
    mine = lax.axis_index("yl").astype(jnp.int32).reshape(1)
    f32, bf16 = jnp.float32, jnp.bfloat16

    earlier = lax.ppermute(
        tokens[local - HALO :], SEQ, [(i, i + 1) for i in range(seq_count - 1)]
    )
    extended = jnp.concatenate([earlier, tokens], 0)
    line = SIZES["yh"] * 2
    copies = jnp.broadcast_to(extended[None], (line,) + extended.shape)

    fan = SIZES["x"] * SIZES["yl"]
    packed_rows = small * k_rows // half
    packed = jnp.concatenate(
        [
            bc_weight.reshape(k_rows, 2, bc_rows).transpose(1, 2, 0),
            dt_weight.reshape(k_rows, 2, heads).transpose(1, 2, 0),
        ],
        1,
    ).reshape(2, packed_rows, half)
    panel = jnp.concatenate(
        [
            x_weight.reshape(k_rows, 2, half).transpose(1, 0, 2),
            packed,
            jnp.zeros((2, -packed_rows % 8, half), bf16),
        ],
        1,
    )
    panel = jnp.broadcast_to(panel[None], (SIZES["x"],) + panel.shape).reshape(
        fan, panel.shape[1], half
    )
    got = lax.all_to_all(panel, ("x", "yl"), 0, 0)
    tall = got[:, :k_rows].reshape(fan * k_rows, half)
    flat = got[:, k_rows : k_rows + packed_rows].reshape(
        fan, packed_rows, half // k_rows, k_rows
    )
    flat = flat.transpose(1, 2, 0, 3).reshape(small, fan * k_rows)
    pieces, offsets = ring(jnp.concatenate([tall, flat], 0), "z")

    copies = lax.optimization_barrier((copies, got))[0]
    own = lax.all_to_all(copies, ("yh", "yl"), 0, 0).reshape(
        SIZES["yh"], 2, local + HALO, width
    )
    own = lax.optimization_barrier((own, pieces[5], pieces[6]))[0]
    other = lax.ppermute(own, "c", [(0, 1), (1, 0)])

    channel_rows = jnp.concatenate(
        [
            jnp.repeat(d_skip, HEAD)[None], norm_gain[None], steer[None],
            jnp.zeros((5, channels), f32),
        ],
        0,
    )
    head_columns = jnp.stack([dt_bias, decay_rate], 1)
    channel_rows, head_columns, _ = lax.optimization_barrier(
        (channel_rows, head_columns, pieces[3])
    )
    source = (z + jnp.array(offsets, jnp.int32)) % SIZES["z"]
    where = jnp.concatenate([source // 2, (source % 2 == core).astype(jnp.int32)])

    x_pre, bc_pre, dt_raw = project(where, own, other, pieces, bc_rows, heads)
    bc_all = lax.all_to_all(
        jnp.broadcast_to(
            bc_pre.reshape(1, bc_rows, -1), (2 * tp_count, bc_rows, 2 * (local + HALO))
        ),
        ("yh", "c", "yl"), 0, 0,
    )
    bc_all = bc_all.reshape(2 * N, -1).T.reshape(2, local + HALO, 2 * N)

    pair = 2 * local
    plane = SIZES["z"] * SIZES["x"]
    share = half // plane
    x_conv, cumulative, step_size, scaled = call(
        conv_kernel,
        [
            jax.ShapeDtypeStruct((pair, half), bf16),
            jax.ShapeDtypeStruct((heads, pair), f32),
            jax.ShapeDtypeStruct((heads, pair), f32),
            jax.ShapeDtypeStruct((half, pair), bf16),
        ],
        mine, x_pre, dt_raw, conv_x, head_columns,
        blocks={
            2: ((conv_x.shape[0], half), lambda i, s: (0, s[0])),
            3: ((heads, 2), lambda i, s: (s[0], 0)),
        },
        flops=10**9, bytes_accessed=8 * pair * half,
    )
    bc_conv, payload, locals_ = call(
        state_kernel,
        [
            jax.ShapeDtypeStruct((pair, 2 * N), bf16),
            jax.ShapeDtypeStruct((plane, share + 8, N), bf16),
            jax.ShapeDtypeStruct((pair // GROUP, half, N), f32),
        ],
        mine, bc_all, conv_bc, cumulative, scaled,
    )
    states = lax.all_to_all(payload, ("z", "x"), 0, 0)
    place = mine * plane + lax.axis_index(("z", "x")).astype(jnp.int32)
    (prefixes,) = call(
        prefix_kernel,
        [jax.ShapeDtypeStruct((plane, share, N), bf16)],
        place, states, initial_state.reshape(channels, N),
        blocks={1: ((share, N), lambda i, s: (s[0], 0))},
    )
    entering = lax.all_to_all(prefixes, ("z", "x"), 0, 0).reshape(half, N)

    lanes = ((8, half), lambda i, s: (0, s[0]))
    inside, growth = call(
        inside_kernel,
        [jax.ShapeDtypeStruct((pair, half), f32), jax.ShapeDtypeStruct((pair, half), f32)],
        mine, x_conv, bc_conv, cumulative, step_size, locals_, channel_rows,
        blocks={5: lanes},
        flops=10**9, bytes_accessed=12 * pair * half,
    )
    keep, send, dots = call(
        output_kernel,
        [
            jax.ShapeDtypeStruct((local, half), f32),
            jax.ShapeDtypeStruct((local, half), bf16),
            jax.ShapeDtypeStruct((2, 1, local), f32),
        ],
        mine, inside, growth, bc_conv, entering, channel_rows,
        blocks={4: lanes},
    )
    swapped = lax.ppermute(send, "yl", [(0, 1), (1, 0)])
    shape = (SIZES["yh"], 2, SIZES["c"], 1, local)
    partials = lax.all_to_all(
        jnp.broadcast_to(dots[None, :, None], shape).reshape(2 * tp_count, 1, local),
        ("yh", "yl", "c"), 0, 0,
    )
    factor = 1.0 / math.sqrt(channels * tp_count)
    (out,) = call(
        functools.partial(steer_kernel, factor),
        [jax.ShapeDtypeStruct((local, channels), bf16)],
        mine, keep, swapped, partials.reshape(2 * tp_count, local),
        channel_rows,
    )
    return out


def solution(mesh):
    fine = Mesh(mesh.devices.reshape(tuple(SIZES.values())), tuple(SIZES))
    both = P(SEQ, TP)
    placed = (
        both, both, both, both, P(None, TP), P(), P(TP), P(TP), P(TP), P(TP),
        P(TP, None, None), P(TP),
    )
    return jax.shard_map(
        per_device, mesh=fine, in_specs=placed, out_specs=both, check_vma=False
    )
```

```python
import functools
import math

import jax
import jax.numpy as jnp
from jax import lax
from jax.experimental import pallas as pl
from jax.experimental.pallas import tpu as pltpu
from jax.sharding import Mesh, PartitionSpec as P

EPSILON = 1e-05
GROUP = 128
N = 128
HALO = 16
HEAD = 64
ALL_VMEM = 67043328
HIGHEST = lax.Precision.HIGHEST

SEQ = ("z", "x", "yl")
TP = ("yh", "c")
SIZES = {"z": 8, "x": 4, "yl": 2, "yh": 4, "c": 2}


def call(kernel, outs, scalars, *args, blocks=None, scratch=(), flops=0, bytes_accessed=0):
    blocks = blocks or {}
    specs = [
        pl.BlockSpec(*blocks[at])
        if at in blocks
        else pl.BlockSpec(arg.shape, functools.partial(lambda rank, i, s: (0,) * rank, arg.ndim))
        for at, arg in enumerate(args)
    ]
    whole = [
        pl.BlockSpec(out.shape, functools.partial(lambda rank, i, s: (0,) * rank, len(out.shape)))
        for out in outs
    ]
    return pl.pallas_call(
        kernel,
        grid_spec=pltpu.PrefetchScalarGridSpec(
            num_scalar_prefetch=1,
            grid=(1,),
            in_specs=specs,
            out_specs=whole,
            scratch_shapes=list(scratch),
        ),
        out_shape=outs,
        compiler_params=pltpu.CompilerParams(vmem_limit_bytes=20 * 1024 * 1024),
        cost_estimate=pl.CostEstimate(
            flops=flops, bytes_accessed=bytes_accessed, transcendentals=0
        ),
    )(scalars, *args)


def dot(a, b, dims, precision=None):
    return lax.dot_general(
        a, b, (dims, ((), ())), precision=precision, preferred_element_type=jnp.float32
    )


def parts(value):
    high = value.astype(jnp.bfloat16)
    rest = value - high.astype(jnp.float32)
    middle = rest.astype(jnp.bfloat16)
    low = (rest - middle.astype(jnp.float32)).astype(jnp.bfloat16)
    return high, middle, low


def left_dot(value, exact, dims):
    return sum(dot(part, exact, dims) for part in parts(value))


def right_dot(exact, value, dims):
    return sum(dot(exact, part, dims) for part in parts(value))


def expander(heads, channels):
    row = lax.broadcasted_iota(jnp.int32, (heads, channels), 0)
    column = lax.broadcasted_iota(jnp.int32, (heads, channels), 1)
    return jnp.where(column // (channels // heads) == row, 1.0, 0.0).astype(jnp.bfloat16)


def panel_kernel(x_ref, bc_ref, dt_ref, panel_ref, side_ref):
    k_rows, channels = x_ref.shape
    half, quarter = channels // 2, channels // 4
    bc_rows, heads = bc_ref.shape[1] // 2, dt_ref.shape[1] // 2
    row = lax.broadcasted_iota(jnp.int32, (k_rows, k_rows), 0)
    column = lax.broadcasted_iota(jnp.int32, (k_rows, k_rows), 1)
    same = jnp.where(row == column, 1.0, 0.0).astype(jnp.bfloat16)
    bc = dot(bc_ref[...], same, ((0,), (0,))).astype(jnp.bfloat16)
    dt = dot(dt_ref[...], same, ((0,), (0,)))
    small = bc_rows + heads
    for part in range(2):
        top = x_ref[:, part * half : part * half + quarter]
        rest = x_ref[:, part * half + quarter : (part + 1) * half]
        narrow = jnp.concatenate(
            [
                bc[part * bc_rows : (part + 1) * bc_rows].astype(jnp.float32),
                dt[part * heads : (part + 1) * heads],
            ],
            0,
        )
        narrow = jnp.concatenate([narrow, jnp.zeros((small, quarter - k_rows), jnp.float32)], 1)
        narrow = narrow.astype(jnp.bfloat16)
        for at in range(part, panel_ref.shape[0], 2):
            panel_ref[at, 0:k_rows] = top
            panel_ref[at, k_rows:] = narrow
        for at in range(part, side_ref.shape[0], 2):
            side_ref[at] = rest


def project_kernel(
    where_ref, feats_ref, side_ref, w0, w1, w2, w3, w4, w5, w6, w7, w8,
    x_ref, bc_ref, dt_ref, feats, first, second, acc, small, sem,
):
    blocks = first.shape[0]
    bc_rows, dt_rows = bc_ref.shape[0], dt_ref.shape[0]
    rows = x_ref.shape[1]
    depth = feats.shape[3]
    half = first.shape[2]
    flat = dt_rows + bc_rows
    tokens = rows - HALO
    cut = w7.shape[0]
    parts = ((0, w0), (1, w1), (2, w2), (3, w3), (4, w4), (5, w5), (6, w6))
    for step in range(blocks):
        at = where_ref[step]
        pltpu.make_async_copy(
            feats_ref.at[at // 2, :, at % 2], feats.at[step], sem.at[0, step]
        ).start()
        if step < blocks - 1:
            pltpu.make_async_copy(parts[step][1], first.at[step], sem.at[1, step]).start()
        else:
            pltpu.make_async_copy(w7, first.at[step, 0:cut], sem.at[1, step]).start()
            pltpu.make_async_copy(w8, first.at[step, cut:], sem.at[1, step + 1]).start()
        pltpu.make_async_copy(
            side_ref.at[:, at], second.at[step], sem.at[2, step]
        ).start()
    small[...] = jnp.zeros_like(small)
    for step in range(blocks):
        pltpu.make_async_copy(feats_ref.at[0, :, 0], feats.at[step], sem.at[0, step]).wait()
        if step < blocks - 1:
            pltpu.make_async_copy(parts[step][1], first.at[step], sem.at[1, step]).wait()
        else:
            pltpu.make_async_copy(w7, first.at[step, 0:cut], sem.at[1, step]).wait()
            pltpu.make_async_copy(w8, first.at[step, cut:], sem.at[1, step + 1]).wait()
        pltpu.make_async_copy(side_ref.at[:, 0], second.at[step], sem.at[2, step]).wait()
        for part in range(2):
            values = feats[step, part]
            left = dot(values, first[step, 0:depth], ((1,), (0,)))
            right = dot(values, second[step].reshape(depth, half), ((1,), (0,)))
            if step:
                acc[part, :, 0:half] += left
                acc[part, :, half:] += right
            else:
                acc[part, :, 0:half] = left
                acc[part, :, half:] = right
            narrow = small[part, 0:rows, 0:flat]
            for at in range(depth // half):
                narrow = narrow + dot(
                    values[:, at * half : (at + 1) * half],
                    first[step, depth + at * flat : depth + (at + 1) * flat],
                    ((1,), (1,)),
                )
            small[part, 0:rows, 0:flat] = narrow
    x_ref[...] = acc[...].astype(jnp.bfloat16)
    for part in range(2):
        turned = small[part].T
        bc_ref[:, part, :] = turned[0:bc_rows, 0:rows].astype(jnp.bfloat16)
        turned = small[part, HALO:rows].T
        dt_ref[:, part * tokens : (part + 1) * tokens] = turned[bc_rows:flat]


def project(where, tokens_by_block, side, weights, bc_rows, dt_rows):
    _, _, _, rows, depth = tokens_by_block.shape
    height, half = weights[0].shape
    blocks = len(weights) - 1
    tokens = rows - HALO
    outs = [
        jax.ShapeDtypeStruct((2, rows, 2 * half), jnp.bfloat16),
        jax.ShapeDtypeStruct((bc_rows, 2, rows), jnp.bfloat16),
        jax.ShapeDtypeStruct((dt_rows, 2 * tokens), jnp.float32),
    ]
    return pl.pallas_call(
        project_kernel,
        in_specs=[pl.BlockSpec(memory_space=pltpu.SMEM)]
        + [pl.BlockSpec(memory_space=pltpu.HBM)] * (len(weights) + 2),
        out_specs=[pl.BlockSpec(memory_space=pltpu.VMEM)] * 3,
        scratch_shapes=[
            pltpu.VMEM((blocks, 2, rows, depth), jnp.bfloat16),
            pltpu.VMEM((blocks, height, half), jnp.bfloat16),
            pltpu.VMEM((blocks,) + (side.shape[0],) + side.shape[2:], jnp.bfloat16),
            pltpu.VMEM((2, rows, 2 * half), jnp.float32),
            pltpu.VMEM((2, (rows + 127) // 128 * 128, 128), jnp.float32),
            pltpu.SemaphoreType.DMA((3, blocks + 1)),
        ],
        out_shape=outs,
        compiler_params=pltpu.CompilerParams(vmem_limit_bytes=ALL_VMEM),
    )(where, tokens_by_block, side, *weights)


def convolved(values, taps, tokens):
    summed = taps[0:1] * values[HALO - 3 : HALO - 3 + tokens]
    for k in range(1, 4):
        summed = summed + taps[k : k + 1] * values[HALO - 3 + k : HALO - 3 + k + tokens]
    return (summed / (1.0 + jnp.exp(-summed))).astype(jnp.bfloat16)


def conv_kernel(
    mine_ref, pre_ref, dt_ref, conv_ref, head_ref, x_ref, cum_ref, step_ref, scaled_ref
):
    tokens, channels = x_ref.shape
    halves, rows, _ = pre_ref.shape
    local = tokens // halves
    heads = dt_ref.shape[0]
    for part in range(halves):
        at = slice(part * local, (part + 1) * local)
        for lane in range(0, channels, 128):
            on = slice(lane, lane + 128)
            values = pre_ref[part, :, on].astype(jnp.float32)
            x_ref[at, on] = convolved(values, conv_ref[:, on], local)
    raw = dt_ref[...] + head_ref[:, 0:1]
    step_size = jnp.maximum(raw, 0.0) + jnp.log1p(jnp.exp(-jnp.abs(raw)))
    log_decay = -step_size * head_ref[:, 1:2]
    step_ref[...] = step_size
    upper = jnp.where(
        lax.broadcasted_iota(jnp.int32, (GROUP, GROUP), 0)
        <= lax.broadcasted_iota(jnp.int32, (GROUP, GROUP), 1),
        1.0,
        0.0,
    ).astype(jnp.bfloat16)
    spread = expander(heads, channels)
    for block in range(tokens // GROUP):
        at = slice(block * GROUP, (block + 1) * GROUP)
        cumulative = left_dot(log_decay[:, at], upper, ((1,), (0,)))
        cum_ref[:, at] = cumulative
        to_end = jnp.exp(cumulative[:, GROUP - 1 : GROUP] - cumulative) * step_size[:, at]
        wide = left_dot(to_end.T, spread, ((1,), (0,)))
        scaled = x_ref[at, :].astype(jnp.float32) * wide
        scaled_ref[:, at] = scaled.T.astype(jnp.bfloat16)


def state_kernel(
    mine_ref, bc_ref, conv_ref, cum_ref, scaled_ref, bconv_ref, pay_ref, local_ref
):
    halves, rows, _ = bc_ref.shape
    channels, tokens = scaled_ref.shape
    local = tokens // halves
    heads = cum_ref.shape[0]
    for part in range(halves):
        at = slice(part * local, (part + 1) * local)
        for lane in range(0, 2 * N, 128):
            on = slice(lane, lane + 128)
            values = bc_ref[part, :, on].astype(jnp.float32)
            bconv_ref[at, on] = convolved(values, conv_ref[:, on], local)
    total = jnp.zeros((heads, 1), jnp.float32)
    blocks = tokens // GROUP
    for block in range(blocks):
        at = slice(block * GROUP, (block + 1) * GROUP)
        added = dot(scaled_ref[:, at], bconv_ref[at, 0:N], ((1,), (0,)))
        end = cum_ref[:, (block + 1) * GROUP - 1 : (block + 1) * GROUP]
        total = total + end
        growth = jnp.exp(end)
        for head in range(heads):
            on = slice(head * HEAD, (head + 1) * HEAD)
            if block:
                local_ref[block, on] = (
                    local_ref[block - 1, on] * growth[head : head + 1] + added[on]
                )
            else:
                local_ref[block, on] = added[on]
    total = jnp.exp(total)
    high = total.astype(jnp.bfloat16).astype(jnp.float32)
    low = total - high
    share = pay_ref.shape[0] // heads
    tail_rows = pay_ref.shape[1] - 16
    row = lax.broadcasted_iota(jnp.int32, (tail_rows, N), 0)
    for head in range(heads):
        tail = jnp.where(
            row == 0, high[head : head + 1], jnp.where(row == 1, low[head : head + 1], 0.0)
        ).astype(jnp.bfloat16)
        for part in range(head * share, (head + 1) * share):
            pay_ref[part, 0:16] = local_ref[blocks - 1, part * 16 : (part + 1) * 16].astype(
                jnp.bfloat16
            )
            pay_ref[part, 16:] = tail


def prefix_kernel(at_ref, got_ref, start_ref, out_ref):
    running = start_ref[...]
    for source in range(got_ref.shape[0]):
        out_ref[source] = running.astype(jnp.bfloat16)
        tail = got_ref[source, 16:].astype(jnp.float32)
        running = (tail[0:1] + tail[1:2]) * running + got_ref[source, 0:16].astype(jnp.float32)


def inside_kernel(
    mine_ref, x_ref, bc_ref, cum_ref, step_ref, local_ref, chan_ref, out_ref, growth_ref
):
    tokens, channels = x_ref.shape
    heads = cum_ref.shape[0]
    spread = expander(heads, channels)
    causal = lax.broadcasted_iota(jnp.int32, (GROUP, GROUP), 0) >= lax.broadcasted_iota(
        jnp.int32, (GROUP, GROUP), 1
    )
    before = jnp.zeros((heads, 1), jnp.float32)
    for block in range(tokens // GROUP):
        at = slice(block * GROUP, (block + 1) * GROUP)
        c_block = bc_ref[at, N:]
        scores = dot(c_block, bc_ref[at, 0:N], ((1,), (1,)))
        cumulative = cum_ref[:, at]
        columns = cumulative.T
        growth_ref[at] = left_dot(jnp.exp(cumulative + before).T, spread, ((1,), (0,)))
        before = before + cumulative[:, GROUP - 1 : GROUP]
        rest = chan_ref[0:1] * x_ref[at].astype(jnp.float32)
        if block:
            carried = right_dot(c_block, local_ref[block - 1], ((1,), (1,)))
            rest = rest + left_dot(jnp.exp(columns), spread, ((1,), (0,))) * carried
        for pair in range(0, heads, 2):
            found = []
            for head in (pair, pair + 1):
                differ = columns[:, head : head + 1] - cumulative[head : head + 1]
                decays = jnp.exp(jnp.where(causal, differ, -1e30))
                mixing = (scores * decays * step_ref[head : head + 1, at]).astype(jnp.bfloat16)
                found.append(
                    dot(mixing, x_ref[at, head * HEAD : (head + 1) * HEAD], ((1,), (0,)))
                )
            on = slice(pair * HEAD, (pair + 2) * HEAD)
            out_ref[at, on] = jnp.concatenate(found, 1) + rest[:, on]


def output_kernel(
    mine_ref, inside_ref, growth_ref, bc_ref, entering_ref, chan_ref, keep_ref, send_ref, dot_ref
):
    mine = mine_ref[0]
    tokens, channels = inside_ref.shape
    local = tokens // 2
    spread = expander(channels // HEAD, channels)
    gain, steer = chan_ref[1:2], chan_ref[2:3]
    for block in range(tokens // GROUP):
        at = slice(block * GROUP, (block + 1) * GROUP)
        carried = dot(bc_ref[at, N:], entering_ref[...], ((1,), (1,)))
        y = inside_ref[at] + growth_ref[at] * carried
        squares = left_dot(y * y, spread, ((1,), (1,))) * (1.0 / HEAD)
        scale = left_dot(lax.rsqrt(squares + EPSILON), spread, ((1,), (0,)))
        normed = y * scale * gain
        part = block * GROUP // local
        on = slice(block * GROUP - part * local, (block + 1) * GROUP - part * local)

        @pl.when(mine == part)
        def _():
            keep_ref[on] = normed

        @pl.when(mine != part)
        def _():
            send_ref[on] = normed.astype(jnp.bfloat16)

        terms = normed * steer
        folded = terms[:, 0:128]
        for lane in range(128, channels, 128):
            folded = folded + terms[:, lane : lane + 128]
        dot_ref[part, :, on] = jnp.sum(folded.T, axis=0, keepdims=True)


def steer_kernel(factor, mine_ref, keep_ref, other_ref, dots_ref, chan_ref, out_ref):
    first = mine_ref[0] == 0
    half = keep_ref.shape[1]
    dots = dots_ref[...]
    for lane in range(0, half, 256):
        at = slice(lane, lane + 256)
        later = slice(half + lane, half + lane + 256)
        own, other = keep_ref[:, at], other_ref[:, at].astype(jnp.float32)
        left, right = jnp.where(first, own, other), jnp.where(first, other, own)
        for on, normed in ((at, left), (later, right)):
            steer = jnp.broadcast_to(chan_ref[2:3, on], (dots.shape[0], 256))
            penalty = dot(dots, steer, ((0,), (0,)), HIGHEST)
            out_ref[:, on] = (normed - penalty * factor).astype(jnp.bfloat16)


def ring(block, axis):
    count = SIZES[axis]
    forward = [(i, (i + 1) % count) for i in range(count)]
    backward = [(i, (i - 1) % count) for i in range(count)]
    pieces, offsets = [block], [0]
    ahead = behind = block
    for hop in range(1, count // 2):
        ahead = lax.ppermute(ahead, axis, forward)
        behind = lax.ppermute(behind, axis, backward)
        ahead, behind = lax.optimization_barrier((ahead, behind))
        pieces += [ahead, behind]
        offsets += [-hop, hop]
    cut = (block.shape[0] // 2 + 15) // 16 * 16
    pieces.append(lax.ppermute(ahead[:cut], axis, forward))
    pieces.append(lax.ppermute(behind[cut:], axis, backward))
    offsets.append(count // 2)
    return pieces, offsets


def per_device(
    tokens, x_weight, bc_weight, dt_weight, conv_x, conv_bc, dt_bias, decay_rate, d_skip,
    norm_gain, initial_state, steer,
):
    local, width = tokens.shape
    k_rows, channels = x_weight.shape
    half = channels // 2
    heads = dt_weight.shape[1] // 2
    bc_rows = bc_weight.shape[1] // 2
    small = bc_rows + heads
    seq_count = SIZES["z"] * SIZES["x"] * SIZES["yl"]
    tp_count = SIZES["yh"] * SIZES["c"]
    z = lax.axis_index("z")
    mine = lax.axis_index("yl").astype(jnp.int32).reshape(1)
    f32, bf16 = jnp.float32, jnp.bfloat16

    earlier = lax.ppermute(
        tokens[local - HALO :], SEQ, [(i, i + 1) for i in range(seq_count - 1)]
    )
    extended = jnp.concatenate([earlier, tokens], 0)
    feats = lax.all_gather(extended, ("yh", "yl", "c"), axis=0, tiled=False).reshape(
        SIZES["yh"], 2, SIZES["c"], local + HALO, width
    )

    quarter = half // 2
    fan = SIZES["x"] * SIZES["yl"]
    panel, side = pl.pallas_call(
        panel_kernel,
        out_shape=[
            jax.ShapeDtypeStruct((fan, k_rows + small, quarter), bf16),
            jax.ShapeDtypeStruct((2 * SIZES["z"], k_rows, quarter), bf16),
        ],
        compiler_params=pltpu.CompilerParams(vmem_limit_bytes=ALL_VMEM),
    )(x_weight, bc_weight, dt_weight)
    got = lax.all_to_all(panel, ("x", "yl"), 0, 0)
    tall = got[:, :k_rows].reshape(fan * k_rows, quarter)
    flat = got[:, k_rows:, :k_rows].reshape(2, fan // 2, small, k_rows)
    flat = flat.transpose(0, 2, 1, 3).reshape(2 * small, quarter)
    block = jnp.concatenate([tall, flat], 0)
    pieces, offsets = ring(block, "z")
    side = lax.optimization_barrier((side, block))[0]
    side = lax.all_to_all(side, ("z", "yl"), 0, 0).reshape(SIZES["z"], 2 * k_rows, quarter)
    side = lax.optimization_barrier((side, pieces[1], pieces[2]))[0]
    side = lax.all_to_all(
        jnp.broadcast_to(side[None], (SIZES["x"],) + side.shape), "x", 0, 0
    )
    channel_rows = jnp.concatenate(
        [
            jnp.repeat(d_skip, HEAD)[None], norm_gain[None], steer[None],
            jnp.zeros((5, channels), f32),
        ],
        0,
    )
    head_columns = jnp.stack([dt_bias, decay_rate], 1)
    channel_rows, head_columns, _ = lax.optimization_barrier(
        (channel_rows, head_columns, pieces[3])
    )
    source = (z + jnp.array(offsets, jnp.int32)) % SIZES["z"]
    x_pre, bc_pre, dt_raw = project(source, feats, side, pieces, bc_rows, heads)
    bc_all = lax.all_to_all(
        jnp.broadcast_to(
            bc_pre.reshape(1, bc_rows, -1), (2 * tp_count, bc_rows, 2 * (local + HALO))
        ),
        ("yh", "c", "yl"), 0, 0,
    )
    bc_all = bc_all.reshape(2 * N, -1).T.reshape(2, local + HALO, 2 * N)

    pair = 2 * local
    plane = SIZES["z"] * SIZES["x"]
    share = half // plane
    x_conv, cumulative, step_size, scaled = call(
        conv_kernel,
        [
            jax.ShapeDtypeStruct((pair, half), bf16),
            jax.ShapeDtypeStruct((heads, pair), f32),
            jax.ShapeDtypeStruct((heads, pair), f32),
            jax.ShapeDtypeStruct((half, pair), bf16),
        ],
        mine, x_pre, dt_raw, conv_x, head_columns,
        blocks={
            2: ((conv_x.shape[0], half), lambda i, s: (0, s[0])),
            3: ((heads, 2), lambda i, s: (s[0], 0)),
        },
        flops=10**9, bytes_accessed=8 * pair * half,
    )
    bc_conv, payload, locals_ = call(
        state_kernel,
        [
            jax.ShapeDtypeStruct((pair, 2 * N), bf16),
            jax.ShapeDtypeStruct((plane, share + 8, N), bf16),
            jax.ShapeDtypeStruct((pair // GROUP, half, N), f32),
        ],
        mine, bc_all, conv_bc, cumulative, scaled,
    )
    states = lax.all_to_all(payload, ("z", "x"), 0, 0)
    place = mine * plane + lax.axis_index(("z", "x")).astype(jnp.int32)
    (prefixes,) = call(
        prefix_kernel,
        [jax.ShapeDtypeStruct((plane, share, N), bf16)],
        place, states, initial_state.reshape(channels, N),
        blocks={1: ((share, N), lambda i, s: (s[0], 0))},
    )
    entering = lax.all_to_all(prefixes, ("z", "x"), 0, 0).reshape(half, N)

    lanes = ((8, half), lambda i, s: (0, s[0]))
    inside, growth = call(
        inside_kernel,
        [jax.ShapeDtypeStruct((pair, half), f32), jax.ShapeDtypeStruct((pair, half), f32)],
        mine, x_conv, bc_conv, cumulative, step_size, locals_, channel_rows,
        blocks={5: lanes},
        flops=10**9, bytes_accessed=12 * pair * half,
    )
    keep, send, dots = call(
        output_kernel,
        [
            jax.ShapeDtypeStruct((local, half), f32),
            jax.ShapeDtypeStruct((local, half), bf16),
            jax.ShapeDtypeStruct((2, 1, local), f32),
        ],
        mine, inside, growth, bc_conv, entering, channel_rows,
        blocks={4: lanes},
    )
    swapped = lax.ppermute(send, "yl", [(0, 1), (1, 0)])
    shape = (SIZES["yh"], 2, SIZES["c"], 1, local)
    partials = lax.all_to_all(
        jnp.broadcast_to(dots[None, :, None], shape).reshape(2 * tp_count, 1, local),
        ("yh", "yl", "c"), 0, 0,
    )
    factor = 1.0 / math.sqrt(channels * tp_count)
    (out,) = call(
        functools.partial(steer_kernel, factor),
        [jax.ShapeDtypeStruct((local, channels), bf16)],
        mine, keep, swapped, partials.reshape(2 * tp_count, local),
        channel_rows,
    )
    return out


def solution(mesh):
    fine = Mesh(mesh.devices.reshape(tuple(SIZES.values())), tuple(SIZES))
    both = P(SEQ, TP)
    placed = (
        both, both, both, both, P(None, TP), P(), P(TP), P(TP), P(TP), P(TP),
        P(TP, None, None), P(TP),
    )
    return jax.shard_map(
        per_device, mesh=fine, in_specs=placed, out_specs=both, check_vma=False
    )
```

```python
import functools
import math

import jax
import jax.numpy as jnp
from jax import lax
from jax.experimental import pallas as pl
from jax.experimental.pallas import tpu as pltpu
from jax.sharding import Mesh, PartitionSpec as P

EPSILON = 1e-05
GROUP = 128
N = 128
HALO = 16
HEAD = 64
ALL_VMEM = 67043328
HIGHEST = lax.Precision.HIGHEST

SEQ = ("z", "x", "yl")
TP = ("yh", "c")
SIZES = {"z": 8, "x": 4, "yl": 2, "yh": 4, "c": 2}


def call(kernel, outs, scalars, *args, blocks=None, scratch=(), flops=0, bytes_accessed=0):
    blocks = blocks or {}
    specs = [
        pl.BlockSpec(*blocks[at])
        if at in blocks
        else pl.BlockSpec(arg.shape, functools.partial(lambda rank, i, s: (0,) * rank, arg.ndim))
        for at, arg in enumerate(args)
    ]
    whole = [
        pl.BlockSpec(out.shape, functools.partial(lambda rank, i, s: (0,) * rank, len(out.shape)))
        for out in outs
    ]
    return pl.pallas_call(
        kernel,
        grid_spec=pltpu.PrefetchScalarGridSpec(
            num_scalar_prefetch=1,
            grid=(1,),
            in_specs=specs,
            out_specs=whole,
            scratch_shapes=list(scratch),
        ),
        out_shape=outs,
        compiler_params=pltpu.CompilerParams(vmem_limit_bytes=ALL_VMEM),
        cost_estimate=pl.CostEstimate(
            flops=flops, bytes_accessed=bytes_accessed, transcendentals=0
        ),
    )(scalars, *args)


def dot(a, b, dims, precision=None):
    return lax.dot_general(
        a, b, (dims, ((), ())), precision=precision, preferred_element_type=jnp.float32
    )


def parts(value):
    high = value.astype(jnp.bfloat16)
    rest = value - high.astype(jnp.float32)
    middle = rest.astype(jnp.bfloat16)
    low = (rest - middle.astype(jnp.float32)).astype(jnp.bfloat16)
    return high, middle, low


def left_dot(value, exact, dims):
    return sum(dot(part, exact, dims) for part in parts(value))


def right_dot(exact, value, dims):
    return sum(dot(exact, part, dims) for part in parts(value))


def expander(heads, channels):
    row = lax.broadcasted_iota(jnp.int32, (heads, channels), 0)
    column = lax.broadcasted_iota(jnp.int32, (heads, channels), 1)
    return jnp.where(column // (channels // heads) == row, 1.0, 0.0).astype(jnp.bfloat16)


def fetch_tokens(where_ref, own_ref, other_ref, feats, sem):
    for step in range(feats.shape[0]):
        line, mine = where_ref[step], where_ref[feats.shape[0] + step] == 1

        @pl.when(mine)
        def _():
            pltpu.make_async_copy(own_ref.at[line], feats.at[step], sem.at[step]).start()

        @pl.when(jnp.logical_not(mine))
        def _():
            pltpu.make_async_copy(other_ref.at[line], feats.at[step], sem.at[step]).start()


def narrow_kernel(
    where_ref, own_ref, other_ref, w0, w1, w2, w3, w4, w5, w6, w7,
    bc_ref, dt_ref, feats, weights, small, sem, weight_sem,
):
    bc_rows, dt_rows = bc_ref.shape[0], dt_ref.shape[0]
    flat = bc_rows + dt_rows
    rows = feats.shape[2]
    tokens = rows - HALO
    blocks = feats.shape[0]
    fetch_tokens(where_ref, own_ref, other_ref, feats, sem)
    copies = []
    for at, ref in enumerate((w0, w1, w2, w3, w4, w5, w6, w7)):
        tall = ref.shape[0] - flat
        copies.append(
            pltpu.make_async_copy(
                ref.at[tall : tall + flat], weights.at[at], weight_sem.at[at]
            )
        )
        copies[at].start()
    small[...] = jnp.zeros_like(small)
    for step in range(blocks):
        pltpu.make_async_copy(own_ref.at[0], feats.at[step], sem.at[step]).wait()
        copies[step].wait()
        for part in range(2):
            small[part, 0:rows, 0:flat] += dot(
                feats[step, part], weights[step], ((1,), (1,))
            )
    for part in range(2):
        turned = small[part].T
        bc_ref[:, part, :] = turned[0:bc_rows, 0:rows].astype(jnp.bfloat16)
        turned = small[part, HALO:rows].T
        dt_ref[:, part * tokens : (part + 1) * tokens] = turned[bc_rows:flat]


def project_kernel(
    where_ref, own_ref, other_ref, w0, w1, w2, w3, w4, w5, w6, w7, w8,
    x_ref, feats, weights, acc, sem, weight_sem,
):
    blocks, depth = weights.shape[0], weights.shape[1]
    cut = w7.shape[0]
    fetch_tokens(where_ref, own_ref, other_ref, feats, sem)
    copies = [
        [pltpu.make_async_copy(ref.at[0:depth], weights.at[at], weight_sem.at[at])]
        for at, ref in enumerate((w0, w1, w2, w3, w4, w5, w6))
    ]
    copies.append(
        [
            pltpu.make_async_copy(w7, weights.at[7, 0:cut], weight_sem.at[7]),
            pltpu.make_async_copy(w8, weights.at[7, cut:], weight_sem.at[8]),
        ]
    )
    for group in copies:
        for copy in group:
            copy.start()
    for step in range(blocks):
        pltpu.make_async_copy(own_ref.at[0], feats.at[step], sem.at[step]).wait()
        for copy in copies[step]:
            copy.wait()
        for part in range(2):
            found = dot(feats[step, part], weights[step], ((1,), (0,)))
            if step == 0:
                acc[part] = found
            elif step < blocks - 1:
                acc[part] += found
            else:
                x_ref[part] = (acc[part] + found).astype(jnp.bfloat16)


def narrow_project(where, own, other, weights, bc_rows, dt_rows):
    _, _, rows, depth = own.shape
    blocks = len(weights)
    flat = bc_rows + dt_rows
    return pl.pallas_call(
        narrow_kernel,
        in_specs=[pl.BlockSpec(memory_space=pltpu.SMEM)]
        + [pl.BlockSpec(memory_space=pl.ANY)] * (blocks + 2),
        out_specs=[pl.BlockSpec(memory_space=pltpu.VMEM)] * 2,
        scratch_shapes=[
            pltpu.VMEM((blocks, 2, rows, depth), jnp.bfloat16),
            pltpu.VMEM((blocks, flat, depth), jnp.bfloat16),
            pltpu.VMEM((2, (rows + 127) // 128 * 128, 128), jnp.float32),
            pltpu.SemaphoreType.DMA((blocks,)),
            pltpu.SemaphoreType.DMA((blocks,)),
        ],
        out_shape=[
            jax.ShapeDtypeStruct((bc_rows, 2, rows), jnp.bfloat16),
            jax.ShapeDtypeStruct((dt_rows, 2 * (rows - HALO)), jnp.float32),
        ],
        compiler_params=pltpu.CompilerParams(vmem_limit_bytes=ALL_VMEM),
        cost_estimate=pl.CostEstimate(flops=10**9, bytes_accessed=10**7, transcendentals=0),
    )(where, own, other, *weights)


def project(where, own, other, weights):
    _, _, rows, depth = own.shape
    channels = weights[0].shape[1]
    blocks = len(weights) - 1
    return pl.pallas_call(
        project_kernel,
        in_specs=[pl.BlockSpec(memory_space=pltpu.SMEM)]
        + [pl.BlockSpec(memory_space=pl.ANY)] * (len(weights) + 2),
        out_specs=pl.BlockSpec(memory_space=pltpu.VMEM),
        scratch_shapes=[
            pltpu.VMEM((blocks, 2, rows, depth), jnp.bfloat16),
            pltpu.VMEM((blocks, depth, channels), jnp.bfloat16),
            pltpu.VMEM((2, rows, channels), jnp.float32),
            pltpu.SemaphoreType.DMA((blocks,)),
            pltpu.SemaphoreType.DMA((blocks + 1,)),
        ],
        out_shape=jax.ShapeDtypeStruct((2, rows, channels), jnp.bfloat16),
        compiler_params=pltpu.CompilerParams(vmem_limit_bytes=ALL_VMEM),
        cost_estimate=pl.CostEstimate(
            flops=3 * 10**9, bytes_accessed=10**7, transcendentals=0
        ),
    )(where, own, other, *weights)


def convolved(values, taps, tokens):
    summed = taps[0:1] * values[HALO - 3 : HALO - 3 + tokens]
    for k in range(1, 4):
        summed = summed + taps[k : k + 1] * values[HALO - 3 + k : HALO - 3 + k + tokens]
    return (summed / (1.0 + jnp.exp(-summed))).astype(jnp.bfloat16)


def conv_kernel(
    mine_ref, pre_ref, dt_ref, conv_ref, head_ref, x_ref, cum_ref, step_ref, scaled_ref
):
    tokens, channels = x_ref.shape
    halves, rows, _ = pre_ref.shape
    local = tokens // halves
    heads = dt_ref.shape[0]
    for part in range(halves):
        at = slice(part * local, (part + 1) * local)
        for lane in range(0, channels, 128):
            on = slice(lane, lane + 128)
            values = pre_ref[part, :, on].astype(jnp.float32)
            x_ref[at, on] = convolved(values, conv_ref[:, on], local)
    raw = dt_ref[...] + head_ref[:, 0:1]
    step_size = jnp.maximum(raw, 0.0) + jnp.log1p(jnp.exp(-jnp.abs(raw)))
    log_decay = -step_size * head_ref[:, 1:2]
    step_ref[...] = step_size
    upper = jnp.where(
        lax.broadcasted_iota(jnp.int32, (GROUP, GROUP), 0)
        <= lax.broadcasted_iota(jnp.int32, (GROUP, GROUP), 1),
        1.0,
        0.0,
    ).astype(jnp.bfloat16)
    spread = expander(heads, channels)
    for block in range(tokens // GROUP):
        at = slice(block * GROUP, (block + 1) * GROUP)
        cumulative = left_dot(log_decay[:, at], upper, ((1,), (0,)))
        cum_ref[:, at] = cumulative
        to_end = jnp.exp(cumulative[:, GROUP - 1 : GROUP] - cumulative) * step_size[:, at]
        wide = left_dot(to_end.T, spread, ((1,), (0,)))
        scaled = x_ref[at, :].astype(jnp.float32) * wide
        scaled_ref[:, at] = scaled.T.astype(jnp.bfloat16)


def state_kernel(
    mine_ref, bc_ref, conv_ref, cum_ref, scaled_ref, bconv_ref, pay_ref, local_ref
):
    halves, rows, _ = bc_ref.shape
    channels, tokens = scaled_ref.shape
    local = tokens // halves
    heads = cum_ref.shape[0]
    for part in range(halves):
        at = slice(part * local, (part + 1) * local)
        for lane in range(0, 2 * N, 128):
            on = slice(lane, lane + 128)
            values = bc_ref[part, :, on].astype(jnp.float32)
            bconv_ref[at, on] = convolved(values, conv_ref[:, on], local)
    total = jnp.zeros((heads, 1), jnp.float32)
    blocks = tokens // GROUP
    for block in range(blocks):
        at = slice(block * GROUP, (block + 1) * GROUP)
        added = dot(scaled_ref[:, at], bconv_ref[at, 0:N], ((1,), (0,)))
        end = cum_ref[:, (block + 1) * GROUP - 1 : (block + 1) * GROUP]
        total = total + end
        growth = jnp.exp(end)
        for head in range(heads):
            on = slice(head * HEAD, (head + 1) * HEAD)
            if block:
                local_ref[block, on] = (
                    local_ref[block - 1, on] * growth[head : head + 1] + added[on]
                )
            else:
                local_ref[block, on] = added[on]
    total = jnp.exp(total)
    high = total.astype(jnp.bfloat16).astype(jnp.float32)
    low = total - high
    share = pay_ref.shape[0] // heads
    tail_rows = pay_ref.shape[1] - 16
    row = lax.broadcasted_iota(jnp.int32, (tail_rows, N), 0)
    for head in range(heads):
        tail = jnp.where(
            row == 0, high[head : head + 1], jnp.where(row == 1, low[head : head + 1], 0.0)
        ).astype(jnp.bfloat16)
        for part in range(head * share, (head + 1) * share):
            pay_ref[part, 0:16] = local_ref[blocks - 1, part * 16 : (part + 1) * 16].astype(
                jnp.bfloat16
            )
            pay_ref[part, 16:] = tail


def block_kernel(
    mine_ref, pre_ref, bc_ref, dt_ref, conv_x_ref, conv_bc_ref, head_ref,
    x_ref, bconv_ref, cum_ref, step_ref, pay_ref, local_ref, scaled_ref,
):
    conv_kernel(
        mine_ref, pre_ref, dt_ref, conv_x_ref, head_ref, x_ref, cum_ref, step_ref, scaled_ref
    )
    state_kernel(
        mine_ref, bc_ref, conv_bc_ref, cum_ref, scaled_ref, bconv_ref, pay_ref, local_ref
    )


def prefix_kernel(at_ref, got_ref, start_ref, out_ref):
    running = start_ref[...]
    for source in range(got_ref.shape[0]):
        out_ref[source] = running.astype(jnp.bfloat16)
        tail = got_ref[source, 16:].astype(jnp.float32)
        running = (tail[0:1] + tail[1:2]) * running + got_ref[source, 0:16].astype(jnp.float32)


def inside_kernel(
    mine_ref, x_ref, bc_ref, cum_ref, step_ref, local_ref, chan_ref, out_ref, growth_ref
):
    tokens, channels = x_ref.shape
    heads = cum_ref.shape[0]
    spread = expander(heads, channels)
    causal = lax.broadcasted_iota(jnp.int32, (GROUP, GROUP), 0) >= lax.broadcasted_iota(
        jnp.int32, (GROUP, GROUP), 1
    )
    before = jnp.zeros((heads, 1), jnp.float32)
    for block in range(tokens // GROUP):
        at = slice(block * GROUP, (block + 1) * GROUP)
        c_block = bc_ref[at, N:]
        scores = dot(c_block, bc_ref[at, 0:N], ((1,), (1,)))
        cumulative = cum_ref[:, at]
        columns = cumulative.T
        growth_ref[at] = left_dot(jnp.exp(cumulative + before).T, spread, ((1,), (0,)))
        before = before + cumulative[:, GROUP - 1 : GROUP]
        rest = chan_ref[0:1] * x_ref[at].astype(jnp.float32)
        if block:
            carried = right_dot(c_block, local_ref[block - 1], ((1,), (1,)))
            rest = rest + left_dot(jnp.exp(columns), spread, ((1,), (0,))) * carried
        for pair in range(0, heads, 2):
            found = []
            for head in (pair, pair + 1):
                differ = columns[:, head : head + 1] - cumulative[head : head + 1]
                decays = jnp.exp(jnp.where(causal, differ, -1e30))
                mixing = (scores * decays * step_ref[head : head + 1, at]).astype(jnp.bfloat16)
                found.append(
                    dot(mixing, x_ref[at, head * HEAD : (head + 1) * HEAD], ((1,), (0,)))
                )
            on = slice(pair * HEAD, (pair + 2) * HEAD)
            out_ref[at, on] = jnp.concatenate(found, 1) + rest[:, on]


def output_kernel(
    mine_ref, inside_ref, growth_ref, bc_ref, entering_ref, chan_ref, keep_ref, send_ref, dot_ref
):
    mine = mine_ref[0]
    tokens, channels = inside_ref.shape
    local = tokens // 2
    spread = expander(channels // HEAD, channels)
    gain, steer = chan_ref[1:2], chan_ref[2:3]
    for block in range(tokens // GROUP):
        at = slice(block * GROUP, (block + 1) * GROUP)
        carried = dot(bc_ref[at, N:], entering_ref[...], ((1,), (1,)))
        y = inside_ref[at] + growth_ref[at] * carried
        squares = left_dot(y * y, spread, ((1,), (1,))) * (1.0 / HEAD)
        scale = left_dot(lax.rsqrt(squares + EPSILON), spread, ((1,), (0,)))
        normed = y * scale * gain
        part = block * GROUP // local
        on = slice(block * GROUP - part * local, (block + 1) * GROUP - part * local)

        @pl.when(mine == part)
        def _():
            keep_ref[on] = normed

        @pl.when(mine != part)
        def _():
            send_ref[on] = normed.astype(jnp.bfloat16)

        terms = normed * steer
        folded = terms[:, 0:128]
        for lane in range(128, channels, 128):
            folded = folded + terms[:, lane : lane + 128]
        dot_ref[part, :, on] = jnp.sum(folded.T, axis=0, keepdims=True)


def steer_kernel(factor, mine_ref, keep_ref, other_ref, dots_ref, chan_ref, out_ref):
    first = mine_ref[0] == 0
    half = keep_ref.shape[1]
    dots = dots_ref[...]
    for lane in range(0, half, 256):
        at = slice(lane, lane + 256)
        later = slice(half + lane, half + lane + 256)
        own, other = keep_ref[:, at], other_ref[:, at].astype(jnp.float32)
        left, right = jnp.where(first, own, other), jnp.where(first, other, own)
        for on, normed in ((at, left), (later, right)):
            steer = jnp.broadcast_to(chan_ref[2:3, on], (dots.shape[0], 256))
            penalty = dot(dots, steer, ((0,), (0,)), HIGHEST)
            out_ref[:, on] = (normed - penalty * factor).astype(jnp.bfloat16)


def ring(block, depth, axis):
    count = SIZES[axis]
    forward = [(i, (i + 1) % count) for i in range(count)]
    backward = [(i, (i - 1) % count) for i in range(count)]
    across = [(i, (i + count // 2) % count) for i in range(count)]
    pieces, offsets = [block], [0]
    ahead = behind = block
    far = None
    for hop in range(1, count // 2):
        ahead = lax.ppermute(ahead, axis, forward)
        behind = lax.ppermute(behind, axis, backward)
        if far is None:
            far = lax.ppermute(block[depth:], axis, across)
            ahead, behind, far = lax.optimization_barrier((ahead, behind, far))
        else:
            ahead, behind = lax.optimization_barrier((ahead, behind))
        pieces += [ahead, behind]
        offsets += [-hop, hop]
    cut = (depth // 2 + 15) // 16 * 16
    last = [
        lax.ppermute(ahead[:cut], axis, forward),
        lax.ppermute(behind[cut:depth], axis, backward),
    ]
    offsets.append(count // 2)
    return pieces, far, last, offsets


def per_device(
    tokens, x_weight, bc_weight, dt_weight, conv_x, conv_bc, dt_bias, decay_rate, d_skip,
    norm_gain, initial_state, steer,
):
    local, width = tokens.shape
    k_rows, channels = x_weight.shape
    half = channels // 2
    heads = dt_weight.shape[1] // 2
    bc_rows = bc_weight.shape[1] // 2
    small = bc_rows + heads
    seq_count = SIZES["z"] * SIZES["x"] * SIZES["yl"]
    tp_count = SIZES["yh"] * SIZES["c"]
    z, core = lax.axis_index("z"), lax.axis_index("c")
    mine = lax.axis_index("yl").astype(jnp.int32).reshape(1)
    f32, bf16 = jnp.float32, jnp.bfloat16

    earlier = lax.ppermute(
        tokens[local - HALO :], SEQ, [(i, i + 1) for i in range(seq_count - 1)]
    )
    extended = jnp.concatenate([earlier, tokens], 0)
    line = SIZES["yh"] * 2
    copies = jnp.broadcast_to(extended[None], (line,) + extended.shape)

    fan = SIZES["x"] * SIZES["yl"]
    packed_rows = small * k_rows // half
    packed = jnp.concatenate(
        [
            bc_weight.reshape(k_rows, 2, bc_rows).transpose(1, 2, 0),
            dt_weight.reshape(k_rows, 2, heads).transpose(1, 2, 0),
        ],
        1,
    ).reshape(2, packed_rows, half)
    panel = jnp.concatenate(
        [
            x_weight.reshape(k_rows, 2, half).transpose(1, 0, 2),
            packed,
            jnp.zeros((2, -packed_rows % 8, half), bf16),
        ],
        1,
    )
    panel = jnp.broadcast_to(panel[None], (SIZES["x"],) + panel.shape).reshape(
        fan, panel.shape[1], half
    )
    got = lax.all_to_all(panel, ("x", "yl"), 0, 0)
    tall = got[:, :k_rows].reshape(fan * k_rows, half)
    flat = got[:, k_rows : k_rows + packed_rows].reshape(
        fan, packed_rows, half // k_rows, k_rows
    )
    flat = flat.transpose(1, 2, 0, 3).reshape(small, fan * k_rows)
    pieces, far, last, offsets = ring(jnp.concatenate([tall, flat], 0), fan * k_rows, "z")

    copies = lax.optimization_barrier((copies, got))[0]
    own = lax.all_to_all(copies, ("yh", "yl"), 0, 0).reshape(
        SIZES["yh"], 2, local + HALO, width
    )
    own = lax.optimization_barrier((own, pieces[5], pieces[6]))[0]
    other = lax.ppermute(own, "c", [(0, 1), (1, 0)])

    channel_rows = jnp.concatenate(
        [
            jnp.repeat(d_skip, HEAD)[None], norm_gain[None], steer[None],
            jnp.zeros((5, channels), f32),
        ],
        0,
    )
    head_columns = jnp.stack([dt_bias, decay_rate], 1)
    channel_rows, head_columns, _ = lax.optimization_barrier(
        (channel_rows, head_columns, pieces[3])
    )
    source = (z + jnp.array(offsets, jnp.int32)) % SIZES["z"]
    where = jnp.concatenate([source // 2, (source % 2 == core).astype(jnp.int32)])

    bc_pre, dt_raw = narrow_project(where, own, other, pieces + [far], bc_rows, heads)
    last[0] = lax.optimization_barrier((last[0], bc_pre))[0]
    x_pre = project(where, own, other, pieces + last)
    bc_all = lax.all_to_all(
        jnp.broadcast_to(
            bc_pre.reshape(1, bc_rows, -1), (2 * tp_count, bc_rows, 2 * (local + HALO))
        ),
        ("yh", "c", "yl"), 0, 0,
    )
    bc_all = bc_all.reshape(2 * N, -1).T.reshape(2, local + HALO, 2 * N)

    pair = 2 * local
    plane = SIZES["z"] * SIZES["x"]
    share = half // plane
    x_conv, bc_conv, cumulative, step_size, payload, locals_ = call(
        block_kernel,
        [
            jax.ShapeDtypeStruct((pair, half), bf16),
            jax.ShapeDtypeStruct((pair, 2 * N), bf16),
            jax.ShapeDtypeStruct((heads, pair), f32),
            jax.ShapeDtypeStruct((heads, pair), f32),
            jax.ShapeDtypeStruct((plane, share + 8, N), bf16),
            jax.ShapeDtypeStruct((pair // GROUP, half, N), f32),
        ],
        mine, x_pre, bc_all, dt_raw, conv_x, conv_bc, head_columns,
        blocks={
            3: ((conv_x.shape[0], half), lambda i, s: (0, s[0])),
            5: ((heads, 2), lambda i, s: (s[0], 0)),
        },
        scratch=[pltpu.VMEM((half, pair), bf16)],
    )
    states = lax.all_to_all(payload, ("z", "x"), 0, 0)
    place = mine * plane + lax.axis_index(("z", "x")).astype(jnp.int32)
    (prefixes,) = call(
        prefix_kernel,
        [jax.ShapeDtypeStruct((plane, share, N), bf16)],
        place, states, initial_state.reshape(channels, N),
        blocks={1: ((share, N), lambda i, s: (s[0], 0))},
    )
    entering = lax.all_to_all(prefixes, ("z", "x"), 0, 0).reshape(half, N)

    lanes = ((8, half), lambda i, s: (0, s[0]))
    inside, growth = call(
        inside_kernel,
        [jax.ShapeDtypeStruct((pair, half), f32), jax.ShapeDtypeStruct((pair, half), f32)],
        mine, x_conv, bc_conv, cumulative, step_size, locals_, channel_rows,
        blocks={5: lanes},
        flops=10**9, bytes_accessed=12 * pair * half,
    )
    keep, send, dots = call(
        output_kernel,
        [
            jax.ShapeDtypeStruct((local, half), f32),
            jax.ShapeDtypeStruct((local, half), bf16),
            jax.ShapeDtypeStruct((2, 1, local), f32),
        ],
        mine, inside, growth, bc_conv, entering, channel_rows,
        blocks={4: lanes},
    )
    swapped = lax.ppermute(send, "yl", [(0, 1), (1, 0)])
    shape = (SIZES["yh"], 2, SIZES["c"], 1, local)
    partials = lax.all_to_all(
        jnp.broadcast_to(dots[None, :, None], shape).reshape(2 * tp_count, 1, local),
        ("yh", "yl", "c"), 0, 0,
    )
    factor = 1.0 / math.sqrt(channels * tp_count)
    (out,) = call(
        functools.partial(steer_kernel, factor),
        [jax.ShapeDtypeStruct((local, channels), bf16)],
        mine, keep, swapped, partials.reshape(2 * tp_count, local),
        channel_rows,
    )
    return out


def solution(mesh):
    fine = Mesh(mesh.devices.reshape(tuple(SIZES.values())), tuple(SIZES))
    both = P(SEQ, TP)
    placed = (
        both, both, both, both, P(None, TP), P(), P(TP), P(TP), P(TP), P(TP),
        P(TP, None, None), P(TP),
    )
    return jax.shard_map(
        per_device, mesh=fine, in_specs=placed, out_specs=both, check_vma=False
    )
```

```python
import functools
import math

import jax
import jax.numpy as jnp
from jax import lax
from jax.experimental import pallas as pl
from jax.experimental.pallas import tpu as pltpu
from jax.sharding import Mesh, PartitionSpec as P

EPSILON = 1e-05
GROUP = 128
N = 128
HALO = 16
HEAD = 64
ALL_VMEM = 67043328
HIGHEST = lax.Precision.HIGHEST

SEQ = ("z", "x", "yl")
TP = ("yh", "c")
OFFSETS = (0, -1, 1, -2, 2, -3, 3, 4)
SIZES = {"z": 8, "x": 4, "yl": 2, "yh": 4, "c": 2}


def call(
    kernel, outs, scalars, *args, blocks=None, scratch=(), flops=0, bytes_accessed=0,
    grant=20 * 1024 * 1024,
):
    blocks = blocks or {}
    specs = [
        pl.BlockSpec(*blocks[at])
        if at in blocks
        else pl.BlockSpec(arg.shape, functools.partial(lambda rank, i, s: (0,) * rank, arg.ndim))
        for at, arg in enumerate(args)
    ]
    whole = [
        pl.BlockSpec(out.shape, functools.partial(lambda rank, i, s: (0,) * rank, len(out.shape)))
        for out in outs
    ]
    return pl.pallas_call(
        kernel,
        grid_spec=pltpu.PrefetchScalarGridSpec(
            num_scalar_prefetch=1,
            grid=(1,),
            in_specs=specs,
            out_specs=whole,
            scratch_shapes=list(scratch),
        ),
        out_shape=outs,
        compiler_params=pltpu.CompilerParams(vmem_limit_bytes=grant),
        cost_estimate=pl.CostEstimate(
            flops=flops, bytes_accessed=bytes_accessed, transcendentals=0
        ),
    )(scalars, *args)


def dot(a, b, dims, precision=None):
    return lax.dot_general(
        a, b, (dims, ((), ())), precision=precision, preferred_element_type=jnp.float32
    )


def parts(value):
    high = value.astype(jnp.bfloat16)
    rest = value - high.astype(jnp.float32)
    middle = rest.astype(jnp.bfloat16)
    low = (rest - middle.astype(jnp.float32)).astype(jnp.bfloat16)
    return high, middle, low


def left_dot(value, exact, dims):
    return sum(dot(part, exact, dims) for part in parts(value))


def right_dot(exact, value, dims):
    return sum(dot(exact, part, dims) for part in parts(value))


def expander(heads, channels):
    row = lax.broadcasted_iota(jnp.int32, (heads, channels), 0)
    column = lax.broadcasted_iota(jnp.int32, (heads, channels), 1)
    return jnp.where(column // (channels // heads) == row, 1.0, 0.0).astype(jnp.bfloat16)


def fetch_tokens(where_ref, own_ref, other_ref, feats, sem):
    for step in range(feats.shape[0]):
        line, mine = where_ref[step], where_ref[feats.shape[0] + step] == 1

        @pl.when(mine)
        def _():
            pltpu.make_async_copy(own_ref.at[line], feats.at[step], sem.at[step]).start()

        @pl.when(jnp.logical_not(mine))
        def _():
            pltpu.make_async_copy(other_ref.at[line], feats.at[step], sem.at[step]).start()


def narrow_kernel(
    where_ref, own_ref, other_ref, w0, w1, w2, w3, w4, w5, w6, w7,
    bc_ref, dt_ref, feats, weights, small, sem, weight_sem,
):
    bc_rows, dt_rows = bc_ref.shape[0], dt_ref.shape[0]
    flat = bc_rows + dt_rows
    rows = feats.shape[2]
    tokens = rows - HALO
    blocks = feats.shape[0]
    fetch_tokens(where_ref, own_ref, other_ref, feats, sem)
    copies = []
    for at, ref in enumerate((w0, w1, w2, w3, w4, w5, w6, w7)):
        tall = ref.shape[0] - flat
        copies.append(
            pltpu.make_async_copy(
                ref.at[tall : tall + flat], weights.at[at], weight_sem.at[at]
            )
        )
        copies[at].start()
    small[...] = jnp.zeros_like(small)
    for step in range(blocks):
        pltpu.make_async_copy(own_ref.at[0], feats.at[step], sem.at[step]).wait()
        copies[step].wait()
        for part in range(2):
            small[part, 0:rows, 0:flat] += dot(
                feats[step, part], weights[step], ((1,), (1,))
            )
    for part in range(2):
        turned = small[part].T
        bc_ref[:, part, :] = turned[0:bc_rows, 0:rows].astype(jnp.bfloat16)
        turned = small[part, HALO:rows].T
        dt_ref[:, part * tokens : (part + 1) * tokens] = turned[bc_rows:flat]


def project_kernel(
    where_ref, own_ref, other_ref, w0, w1, w2, w3, w4, w5, w6, w7,
    x_ref, feats, weights, acc, sem, weight_sem,
):
    blocks, depth = weights.shape[0], weights.shape[1]
    fetch_tokens(where_ref, own_ref, other_ref, feats, sem)
    copies = [
        pltpu.make_async_copy(ref.at[0:depth], weights.at[at], weight_sem.at[at])
        for at, ref in enumerate((w0, w1, w2, w3, w4, w5, w6, w7))
    ]
    for copy in copies:
        copy.start()
    for step in range(blocks):
        pltpu.make_async_copy(own_ref.at[0], feats.at[step], sem.at[step]).wait()
        copies[step].wait()
        for part in range(2):
            found = dot(feats[step, part], weights[step], ((1,), (0,)))
            if step == 0:
                acc[part] = found
            elif step < blocks - 1:
                acc[part] += found
            else:
                x_ref[part] = (acc[part] + found).astype(jnp.bfloat16)


def narrow_project(where, own, other, weights, bc_rows, dt_rows):
    _, _, rows, depth = own.shape
    blocks = len(weights)
    flat = bc_rows + dt_rows
    return pl.pallas_call(
        narrow_kernel,
        in_specs=[pl.BlockSpec(memory_space=pltpu.SMEM)]
        + [pl.BlockSpec(memory_space=pl.ANY)] * (blocks + 2),
        out_specs=[pl.BlockSpec(memory_space=pltpu.VMEM)] * 2,
        scratch_shapes=[
            pltpu.VMEM((blocks, 2, rows, depth), jnp.bfloat16),
            pltpu.VMEM((blocks, flat, depth), jnp.bfloat16),
            pltpu.VMEM((2, (rows + 127) // 128 * 128, 128), jnp.float32),
            pltpu.SemaphoreType.DMA((blocks,)),
            pltpu.SemaphoreType.DMA((blocks,)),
        ],
        out_shape=[
            jax.ShapeDtypeStruct((bc_rows, 2, rows), jnp.bfloat16),
            jax.ShapeDtypeStruct((dt_rows, 2 * (rows - HALO)), jnp.float32),
        ],
        compiler_params=pltpu.CompilerParams(vmem_limit_bytes=ALL_VMEM),
        cost_estimate=pl.CostEstimate(flops=10**9, bytes_accessed=10**7, transcendentals=0),
    )(where, own, other, *weights)


def project(where, own, other, weights):
    _, _, rows, depth = own.shape
    channels = weights[0].shape[1]
    blocks = len(weights)
    return pl.pallas_call(
        project_kernel,
        in_specs=[pl.BlockSpec(memory_space=pltpu.SMEM)]
        + [pl.BlockSpec(memory_space=pl.ANY)] * (len(weights) + 2),
        out_specs=pl.BlockSpec(memory_space=pltpu.VMEM),
        scratch_shapes=[
            pltpu.VMEM((blocks, 2, rows, depth), jnp.bfloat16),
            pltpu.VMEM((blocks, depth, channels), jnp.bfloat16),
            pltpu.VMEM((2, rows, channels), jnp.float32),
            pltpu.SemaphoreType.DMA((blocks,)),
            pltpu.SemaphoreType.DMA((blocks,)),
        ],
        out_shape=jax.ShapeDtypeStruct((2, rows, channels), jnp.bfloat16),
        compiler_params=pltpu.CompilerParams(vmem_limit_bytes=ALL_VMEM),
        cost_estimate=pl.CostEstimate(
            flops=3 * 10**9, bytes_accessed=10**7, transcendentals=0
        ),
    )(where, own, other, *weights)


def convolved(values, taps, tokens):
    summed = taps[0:1] * values[HALO - 3 : HALO - 3 + tokens]
    for k in range(1, 4):
        summed = summed + taps[k : k + 1] * values[HALO - 3 + k : HALO - 3 + k + tokens]
    return (summed / (1.0 + jnp.exp(-summed))).astype(jnp.bfloat16)


def conv_kernel(
    mine_ref, pre_ref, dt_ref, conv_ref, head_ref, x_ref, cum_ref, step_ref, scaled_ref
):
    tokens, channels = x_ref.shape
    halves, rows, _ = pre_ref.shape
    local = tokens // halves
    heads = dt_ref.shape[0]
    for part in range(halves):
        at = slice(part * local, (part + 1) * local)
        for lane in range(0, channels, 128):
            on = slice(lane, lane + 128)
            values = pre_ref[part, :, on].astype(jnp.float32)
            x_ref[at, on] = convolved(values, conv_ref[:, on], local)
    raw = dt_ref[...] + head_ref[:, 0:1]
    step_size = jnp.maximum(raw, 0.0) + jnp.log1p(jnp.exp(-jnp.abs(raw)))
    log_decay = -step_size * head_ref[:, 1:2]
    step_ref[...] = step_size
    upper = jnp.where(
        lax.broadcasted_iota(jnp.int32, (GROUP, GROUP), 0)
        <= lax.broadcasted_iota(jnp.int32, (GROUP, GROUP), 1),
        1.0,
        0.0,
    ).astype(jnp.bfloat16)
    spread = expander(heads, channels)
    for block in range(tokens // GROUP):
        at = slice(block * GROUP, (block + 1) * GROUP)
        cumulative = left_dot(log_decay[:, at], upper, ((1,), (0,)))
        cum_ref[:, at] = cumulative
        to_end = jnp.exp(cumulative[:, GROUP - 1 : GROUP] - cumulative) * step_size[:, at]
        wide = left_dot(to_end.T, spread, ((1,), (0,)))
        scaled = x_ref[at, :].astype(jnp.float32) * wide
        scaled_ref[:, at] = scaled.T.astype(jnp.bfloat16)


def state_kernel(
    mine_ref, bc_ref, conv_ref, cum_ref, scaled_ref, bconv_ref, pay_ref, local_ref
):
    halves, rows, _ = bc_ref.shape
    channels, tokens = scaled_ref.shape
    local = tokens // halves
    heads = cum_ref.shape[0]
    for part in range(halves):
        at = slice(part * local, (part + 1) * local)
        for lane in range(0, 2 * N, 128):
            on = slice(lane, lane + 128)
            values = bc_ref[part, :, on].astype(jnp.float32)
            bconv_ref[at, on] = convolved(values, conv_ref[:, on], local)
    total = jnp.zeros((heads, 1), jnp.float32)
    blocks = tokens // GROUP
    for block in range(blocks):
        at = slice(block * GROUP, (block + 1) * GROUP)
        added = dot(scaled_ref[:, at], bconv_ref[at, 0:N], ((1,), (0,)))
        end = cum_ref[:, (block + 1) * GROUP - 1 : (block + 1) * GROUP]
        total = total + end
        growth = jnp.exp(end)
        for head in range(heads):
            on = slice(head * HEAD, (head + 1) * HEAD)
            if block:
                local_ref[block, on] = (
                    local_ref[block - 1, on] * growth[head : head + 1] + added[on]
                )
            else:
                local_ref[block, on] = added[on]
    total = jnp.exp(total)
    high = total.astype(jnp.bfloat16).astype(jnp.float32)
    low = total - high
    share = pay_ref.shape[0] // heads
    tail_rows = pay_ref.shape[1] - 16
    row = lax.broadcasted_iota(jnp.int32, (tail_rows, N), 0)
    for head in range(heads):
        tail = jnp.where(
            row == 0, high[head : head + 1], jnp.where(row == 1, low[head : head + 1], 0.0)
        ).astype(jnp.bfloat16)
        for part in range(head * share, (head + 1) * share):
            pay_ref[part, 0:16] = local_ref[blocks - 1, part * 16 : (part + 1) * 16].astype(
                jnp.bfloat16
            )
            pay_ref[part, 16:] = tail


def block_kernel(
    mine_ref, pre_ref, bc_ref, dt_ref, conv_x_ref, conv_bc_ref, head_ref,
    x_ref, bconv_ref, cum_ref, step_ref, pay_ref, local_ref, scaled_ref,
):
    conv_kernel(
        mine_ref, pre_ref, dt_ref, conv_x_ref, head_ref, x_ref, cum_ref, step_ref, scaled_ref
    )
    state_kernel(
        mine_ref, bc_ref, conv_bc_ref, cum_ref, scaled_ref, bconv_ref, pay_ref, local_ref
    )


def prefix_kernel(at_ref, got_ref, start_ref, out_ref):
    running = start_ref[...]
    for source in range(got_ref.shape[0]):
        out_ref[source] = running.astype(jnp.bfloat16)
        tail = got_ref[source, 16:].astype(jnp.float32)
        running = (tail[0:1] + tail[1:2]) * running + got_ref[source, 0:16].astype(jnp.float32)


def inside_kernel(
    mine_ref, x_ref, bc_ref, cum_ref, step_ref, local_ref, chan_ref, out_ref, growth_ref
):
    tokens, channels = x_ref.shape
    heads = cum_ref.shape[0]
    spread = expander(heads, channels)
    causal = lax.broadcasted_iota(jnp.int32, (GROUP, GROUP), 0) >= lax.broadcasted_iota(
        jnp.int32, (GROUP, GROUP), 1
    )
    before = jnp.zeros((heads, 1), jnp.float32)
    for block in range(tokens // GROUP):
        at = slice(block * GROUP, (block + 1) * GROUP)
        c_block = bc_ref[at, N:]
        scores = dot(c_block, bc_ref[at, 0:N], ((1,), (1,)))
        cumulative = cum_ref[:, at]
        columns = cumulative.T
        growth_ref[at] = left_dot(jnp.exp(cumulative + before).T, spread, ((1,), (0,)))
        before = before + cumulative[:, GROUP - 1 : GROUP]
        rest = chan_ref[0:1] * x_ref[at].astype(jnp.float32)
        if block:
            carried = right_dot(c_block, local_ref[block - 1], ((1,), (1,)))
            rest = rest + left_dot(jnp.exp(columns), spread, ((1,), (0,))) * carried
        for pair in range(0, heads, 2):
            found = []
            for head in (pair, pair + 1):
                differ = columns[:, head : head + 1] - cumulative[head : head + 1]
                decays = jnp.exp(jnp.where(causal, differ, -1e30))
                mixing = (scores * decays * step_ref[head : head + 1, at]).astype(jnp.bfloat16)
                found.append(
                    dot(mixing, x_ref[at, head * HEAD : (head + 1) * HEAD], ((1,), (0,)))
                )
            on = slice(pair * HEAD, (pair + 2) * HEAD)
            out_ref[at, on] = jnp.concatenate(found, 1) + rest[:, on]


def output_kernel(
    mine_ref, inside_ref, growth_ref, bc_ref, entering_ref, chan_ref, keep_ref, send_ref, dot_ref
):
    mine = mine_ref[0]
    tokens, channels = inside_ref.shape
    local = tokens // 2
    spread = expander(channels // HEAD, channels)
    gain, steer = chan_ref[1:2], chan_ref[2:3]
    for block in range(tokens // GROUP):
        at = slice(block * GROUP, (block + 1) * GROUP)
        carried = dot(bc_ref[at, N:], entering_ref[...], ((1,), (1,)))
        y = inside_ref[at] + growth_ref[at] * carried
        squares = left_dot(y * y, spread, ((1,), (1,))) * (1.0 / HEAD)
        scale = left_dot(lax.rsqrt(squares + EPSILON), spread, ((1,), (0,)))
        normed = y * scale * gain
        part = block * GROUP // local
        on = slice(block * GROUP - part * local, (block + 1) * GROUP - part * local)

        @pl.when(mine == part)
        def _():
            keep_ref[on] = normed

        @pl.when(mine != part)
        def _():
            send_ref[on] = normed.astype(jnp.bfloat16)

        terms = normed * steer
        folded = terms[:, 0:128]
        for lane in range(128, channels, 128):
            folded = folded + terms[:, lane : lane + 128]
        dot_ref[part, :, on] = jnp.sum(folded.T, axis=0, keepdims=True)


def steer_kernel(factor, mine_ref, keep_ref, other_ref, dots_ref, chan_ref, out_ref):
    first = mine_ref[0] == 0
    half = keep_ref.shape[1]
    dots = dots_ref[...]
    for lane in range(0, half, 256):
        at = slice(lane, lane + 256)
        later = slice(half + lane, half + lane + 256)
        own, other = keep_ref[:, at], other_ref[:, at].astype(jnp.float32)
        left, right = jnp.where(first, own, other), jnp.where(first, other, own)
        for on, normed in ((at, left), (later, right)):
            steer = jnp.broadcast_to(chan_ref[2:3, on], (dots.shape[0], 256))
            penalty = dot(dots, steer, ((0,), (0,)), HIGHEST)
            out_ref[:, on] = (normed - penalty * factor).astype(jnp.bfloat16)


def prepare_parameters(d_skip, norm_gain, steer, dt_bias, decay_rate, z):
    channel_rows = jnp.concatenate(
        [
            jnp.repeat(d_skip, HEAD)[None], norm_gain[None], steer[None],
            jnp.zeros((5, steer.shape[0]), jnp.float32),
        ],
        0,
    )
    head_columns = jnp.stack([dt_bias, decay_rate], 1)
    source = (z + jnp.array(OFFSETS, jnp.int32)) % SIZES["z"]
    where = jnp.concatenate(
        [source // 2, (source % 2 == lax.axis_index("c")).astype(jnp.int32)]
    )
    return channel_rows, head_columns, where


def ring(block, depth, axis, prepare, raw):
    count = SIZES[axis]
    forward = [(i, (i + 1) % count) for i in range(count)]
    backward = [(i, (i - 1) % count) for i in range(count)]
    across = [(i, (i + count // 2) % count) for i in range(count)]
    pieces = [block]
    ahead = behind = block
    for hop in range(1, count // 2):
        ahead = lax.ppermute(ahead, axis, forward)
        behind = lax.ppermute(behind, axis, backward)
        if hop == 1:
            far = lax.ppermute(block[depth:], axis, across)
            ready = prepare(*lax.optimization_barrier((raw, far))[0])
            ahead, behind, far = lax.optimization_barrier((ahead, behind, far))
        elif hop == 2:
            ahead, behind, ready = lax.optimization_barrier((ahead, behind, ready))
        else:
            ahead, behind = lax.optimization_barrier((ahead, behind))
        pieces += [ahead, behind]
    pieces.append(lax.ppermute(ahead, axis, forward))
    return pieces, far, ready


def per_device(
    tokens, x_weight, bc_weight, dt_weight, conv_x, conv_bc, dt_bias, decay_rate, d_skip,
    norm_gain, initial_state, steer,
):
    local, width = tokens.shape
    k_rows, channels = x_weight.shape
    half = channels // 2
    heads = dt_weight.shape[1] // 2
    bc_rows = bc_weight.shape[1] // 2
    small = bc_rows + heads
    seq_count = SIZES["z"] * SIZES["x"] * SIZES["yl"]
    tp_count = SIZES["yh"] * SIZES["c"]
    z = lax.axis_index("z")
    mine = lax.axis_index("yl").astype(jnp.int32).reshape(1)
    f32, bf16 = jnp.float32, jnp.bfloat16

    earlier = lax.ppermute(
        tokens[local - HALO :], SEQ, [(i, i + 1) for i in range(seq_count - 1)]
    )
    extended = jnp.concatenate([earlier, tokens], 0)
    line = SIZES["yh"] * 2
    copies = jnp.broadcast_to(extended[None], (line,) + extended.shape)

    fan = SIZES["x"] * SIZES["yl"]
    packed_rows = small * k_rows // half
    packed = jnp.concatenate(
        [
            bc_weight.reshape(k_rows, 2, bc_rows).transpose(1, 2, 0),
            dt_weight.reshape(k_rows, 2, heads).transpose(1, 2, 0),
        ],
        1,
    ).reshape(2, packed_rows, half)
    panel = jnp.concatenate(
        [
            x_weight.reshape(k_rows, 2, half).transpose(1, 0, 2),
            packed,
            jnp.zeros((2, -packed_rows % 8, half), bf16),
        ],
        1,
    )
    panel = jnp.broadcast_to(panel[None], (SIZES["x"],) + panel.shape).reshape(
        fan, panel.shape[1], half
    )
    got = lax.all_to_all(panel, ("x", "yl"), 0, 0)
    tall = got[:, :k_rows].reshape(fan * k_rows, half)
    flat = got[:, k_rows : k_rows + packed_rows].reshape(
        fan, packed_rows, half // k_rows, k_rows
    )
    flat = flat.transpose(1, 2, 0, 3).reshape(small, fan * k_rows)
    block = jnp.concatenate([tall, flat], 0)
    pieces, far, ready = ring(
        block, fan * k_rows, "z", prepare_parameters,
        (d_skip, norm_gain, steer, dt_bias, decay_rate, z.astype(jnp.int32)),
    )
    channel_rows, head_columns, where = ready

    copies = lax.optimization_barrier((copies, got))[0]
    own = lax.all_to_all(copies, ("yh", "yl"), 0, 0).reshape(
        SIZES["yh"], 2, local + HALO, width
    )
    own = lax.optimization_barrier((own, pieces[5], pieces[6]))[0]
    other = lax.ppermute(own, "c", [(0, 1), (1, 0)])

    bc_pre, dt_raw = narrow_project(where, own, other, pieces[:-1] + [far], bc_rows, heads)
    pieces[-1] = lax.optimization_barrier((pieces[-1], bc_pre))[0]
    x_pre = project(where, own, other, pieces)
    bc_all = lax.all_to_all(
        jnp.broadcast_to(
            bc_pre.reshape(1, bc_rows, -1), (2 * tp_count, bc_rows, 2 * (local + HALO))
        ),
        ("yh", "c", "yl"), 0, 0,
    )
    bc_all = bc_all.reshape(2 * N, -1).T.reshape(2, local + HALO, 2 * N)

    pair = 2 * local
    plane = SIZES["z"] * SIZES["x"]
    share = half // plane
    x_conv, bc_conv, cumulative, step_size, payload, locals_ = call(
        block_kernel,
        [
            jax.ShapeDtypeStruct((pair, half), bf16),
            jax.ShapeDtypeStruct((pair, 2 * N), bf16),
            jax.ShapeDtypeStruct((heads, pair), f32),
            jax.ShapeDtypeStruct((heads, pair), f32),
            jax.ShapeDtypeStruct((plane, share + 8, N), bf16),
            jax.ShapeDtypeStruct((pair // GROUP, half, N), f32),
        ],
        mine, x_pre, bc_all, dt_raw, conv_x, conv_bc, head_columns,
        blocks={
            3: ((conv_x.shape[0], half), lambda i, s: (0, s[0])),
            5: ((heads, 2), lambda i, s: (s[0], 0)),
        },
        scratch=[pltpu.VMEM((half, pair), bf16)],
        grant=ALL_VMEM,
    )
    states = lax.all_to_all(payload, ("z", "x"), 0, 0)
    place = mine * plane + lax.axis_index(("z", "x")).astype(jnp.int32)
    (prefixes,) = call(
        prefix_kernel,
        [jax.ShapeDtypeStruct((plane, share, N), bf16)],
        place, states, initial_state.reshape(channels, N),
        blocks={1: ((share, N), lambda i, s: (s[0], 0))},
    )
    entering = lax.all_to_all(prefixes, ("z", "x"), 0, 0).reshape(half, N)

    lanes = ((8, half), lambda i, s: (0, s[0]))
    inside, growth = call(
        inside_kernel,
        [jax.ShapeDtypeStruct((pair, half), f32), jax.ShapeDtypeStruct((pair, half), f32)],
        mine, x_conv, bc_conv, cumulative, step_size, locals_, channel_rows,
        blocks={5: lanes},
        flops=10**9, bytes_accessed=12 * pair * half,
    )
    keep, send, dots = call(
        output_kernel,
        [
            jax.ShapeDtypeStruct((local, half), f32),
            jax.ShapeDtypeStruct((local, half), bf16),
            jax.ShapeDtypeStruct((2, 1, local), f32),
        ],
        mine, inside, growth, bc_conv, entering, channel_rows,
        blocks={4: lanes},
    )
    swapped = lax.ppermute(send, "yl", [(0, 1), (1, 0)])
    shape = (SIZES["yh"], 2, SIZES["c"], 1, local)
    partials = lax.all_to_all(
        jnp.broadcast_to(dots[None, :, None], shape).reshape(2 * tp_count, 1, local),
        ("yh", "yl", "c"), 0, 0,
    )
    factor = 1.0 / math.sqrt(channels * tp_count)
    (out,) = call(
        functools.partial(steer_kernel, factor),
        [jax.ShapeDtypeStruct((local, channels), bf16)],
        mine, keep, swapped, partials.reshape(2 * tp_count, local),
        channel_rows,
    )
    return out


def solution(mesh):
    fine = Mesh(mesh.devices.reshape(tuple(SIZES.values())), tuple(SIZES))
    both = P(SEQ, TP)
    placed = (
        both, both, both, both, P(None, TP), P(), P(TP), P(TP), P(TP), P(TP),
        P(TP, None, None), P(TP),
    )
    return jax.shard_map(
        per_device, mesh=fine, in_specs=placed, out_specs=both, check_vma=False
    )
```

```python
import functools
import math

import jax
import jax.numpy as jnp
from jax import lax
from jax.experimental import pallas as pl
from jax.experimental.pallas import tpu as pltpu
from jax.sharding import Mesh, PartitionSpec as P

EPSILON = 1e-05
GROUP = 128
N = 128
HALO = 16
HEAD = 64
ALL_VMEM = 67043328
HIGHEST = lax.Precision.HIGHEST

SEQ = ("z", "x", "yl")
TP = ("yh", "c")
SHARES = 64
OFFSETS = (0, -1, 1, -2, 2, -3, 3, 4)
SIZES = {"z": 8, "x": 4, "yl": 2, "yh": 4, "c": 2}


def call(
    kernel, outs, scalars, *args, blocks=None, scratch=(), flops=0, bytes_accessed=0,
    grant=20 * 1024 * 1024,
):
    blocks = blocks or {}
    specs = [
        pl.BlockSpec(*blocks[at])
        if at in blocks
        else pl.BlockSpec(arg.shape, functools.partial(lambda rank, i, s: (0,) * rank, arg.ndim))
        for at, arg in enumerate(args)
    ]
    whole = [
        pl.BlockSpec(out.shape, functools.partial(lambda rank, i, s: (0,) * rank, len(out.shape)))
        for out in outs
    ]
    return pl.pallas_call(
        kernel,
        grid_spec=pltpu.PrefetchScalarGridSpec(
            num_scalar_prefetch=1,
            grid=(1,),
            in_specs=specs,
            out_specs=whole,
            scratch_shapes=list(scratch),
        ),
        out_shape=outs,
        compiler_params=pltpu.CompilerParams(vmem_limit_bytes=grant),
        cost_estimate=pl.CostEstimate(
            flops=flops, bytes_accessed=bytes_accessed, transcendentals=0
        ),
    )(scalars, *args)


def dot(a, b, dims, precision=None):
    return lax.dot_general(
        a, b, (dims, ((), ())), precision=precision, preferred_element_type=jnp.float32
    )


def parts(value):
    high = value.astype(jnp.bfloat16)
    rest = value - high.astype(jnp.float32)
    middle = rest.astype(jnp.bfloat16)
    low = (rest - middle.astype(jnp.float32)).astype(jnp.bfloat16)
    return high, middle, low


def left_dot(value, exact, dims):
    return sum(dot(part, exact, dims) for part in parts(value))


def right_dot(exact, value, dims):
    return sum(dot(exact, part, dims) for part in parts(value))


def expander(heads, channels):
    row = lax.broadcasted_iota(jnp.int32, (heads, channels), 0)
    column = lax.broadcasted_iota(jnp.int32, (heads, channels), 1)
    return jnp.where(column // (channels // heads) == row, 1.0, 0.0).astype(jnp.bfloat16)


def fetch_tokens(where_ref, own_ref, other_ref, feats, sem):
    for step in range(feats.shape[0]):
        line, mine = where_ref[step], where_ref[feats.shape[0] + step] == 1

        @pl.when(mine)
        def _():
            pltpu.make_async_copy(own_ref.at[line], feats.at[step], sem.at[step]).start()

        @pl.when(jnp.logical_not(mine))
        def _():
            pltpu.make_async_copy(other_ref.at[line], feats.at[step], sem.at[step]).start()


def narrow_kernel(
    where_ref, own_ref, other_ref, w0, w1, w2, w3, w4, w5, w6, w7,
    bc_ref, dt_ref, feats, weights, small, sem, weight_sem,
):
    bc_rows, dt_rows = bc_ref.shape[1], dt_ref.shape[0]
    flat = bc_rows + dt_rows
    rows = feats.shape[2]
    tokens = rows - HALO
    blocks = feats.shape[0]
    fetch_tokens(where_ref, own_ref, other_ref, feats, sem)
    copies = []
    for at, ref in enumerate((w0, w1, w2, w3, w4, w5, w6, w7)):
        tall = ref.shape[0] - flat
        copies.append(
            pltpu.make_async_copy(
                ref.at[tall : tall + flat], weights.at[at], weight_sem.at[at]
            )
        )
        copies[at].start()
    small[...] = jnp.zeros_like(small)
    for step in range(blocks):
        pltpu.make_async_copy(own_ref.at[0], feats.at[step], sem.at[step]).wait()
        copies[step].wait()
        for part in range(2):
            small[part * rows : (part + 1) * rows, 0:flat] += dot(
                feats[step, part], weights[step], ((1,), (1,))
            )
    turned = small[...].T[0:bc_rows, 0 : 2 * rows].astype(jnp.bfloat16)
    for at in range(bc_ref.shape[0]):
        bc_ref[at] = turned
    for part in range(2):
        turned = small[part * rows + HALO : (part + 1) * rows].T
        dt_ref[:, part * tokens : (part + 1) * tokens] = turned[bc_rows:flat]


def project_kernel(
    where_ref, own_ref, other_ref, w0, w1, w2, w3, w4, w5, w6, w7,
    x_ref, feats, weights, acc, sem, weight_sem,
):
    blocks, depth = weights.shape[0], weights.shape[1]
    fetch_tokens(where_ref, own_ref, other_ref, feats, sem)
    copies = [
        pltpu.make_async_copy(ref.at[0:depth], weights.at[at], weight_sem.at[at])
        for at, ref in enumerate((w0, w1, w2, w3, w4, w5, w6, w7))
    ]
    for copy in copies:
        copy.start()
    for step in range(blocks):
        pltpu.make_async_copy(own_ref.at[0], feats.at[step], sem.at[step]).wait()
        copies[step].wait()
        for part in range(2):
            found = dot(feats[step, part], weights[step], ((1,), (0,)))
            if step == 0:
                acc[part] = found
            elif step < blocks - 1:
                acc[part] += found
            else:
                x_ref[part] = (acc[part] + found).astype(jnp.bfloat16)


def narrow_project(where, own, other, weights, bc_rows, dt_rows, copies):
    _, _, rows, depth = own.shape
    blocks = len(weights)
    flat = bc_rows + dt_rows
    return pl.pallas_call(
        narrow_kernel,
        in_specs=[pl.BlockSpec(memory_space=pltpu.SMEM)]
        + [pl.BlockSpec(memory_space=pl.ANY)] * (blocks + 2),
        out_specs=[pl.BlockSpec(memory_space=pltpu.VMEM)] * 2,
        scratch_shapes=[
            pltpu.VMEM((blocks, 2, rows, depth), jnp.bfloat16),
            pltpu.VMEM((blocks, flat, depth), jnp.bfloat16),
            pltpu.VMEM(((2 * rows + 127) // 128 * 128, 128), jnp.float32),
            pltpu.SemaphoreType.DMA((blocks,)),
            pltpu.SemaphoreType.DMA((blocks,)),
        ],
        out_shape=[
            jax.ShapeDtypeStruct((copies, bc_rows, 2 * rows), jnp.bfloat16),
            jax.ShapeDtypeStruct((dt_rows, 2 * (rows - HALO)), jnp.float32),
        ],
        compiler_params=pltpu.CompilerParams(vmem_limit_bytes=ALL_VMEM),
        cost_estimate=pl.CostEstimate(flops=10**9, bytes_accessed=10**7, transcendentals=0),
    )(where, own, other, *weights)


def project(where, own, other, weights):
    _, _, rows, depth = own.shape
    channels = weights[0].shape[1]
    blocks = len(weights)
    return pl.pallas_call(
        project_kernel,
        in_specs=[pl.BlockSpec(memory_space=pltpu.SMEM)]
        + [pl.BlockSpec(memory_space=pl.ANY)] * (len(weights) + 2),
        out_specs=pl.BlockSpec(memory_space=pltpu.VMEM),
        scratch_shapes=[
            pltpu.VMEM((blocks, 2, rows, depth), jnp.bfloat16),
            pltpu.VMEM((blocks, depth, channels), jnp.bfloat16),
            pltpu.VMEM((2, rows, channels), jnp.float32),
            pltpu.SemaphoreType.DMA((blocks,)),
            pltpu.SemaphoreType.DMA((blocks,)),
        ],
        out_shape=jax.ShapeDtypeStruct((2, rows, channels), jnp.bfloat16),
        compiler_params=pltpu.CompilerParams(vmem_limit_bytes=ALL_VMEM),
        cost_estimate=pl.CostEstimate(
            flops=3 * 10**9, bytes_accessed=10**7, transcendentals=0
        ),
    )(where, own, other, *weights)


def convolved(values, taps, tokens):
    summed = taps[0:1] * values[HALO - 3 : HALO - 3 + tokens]
    for k in range(1, 4):
        summed = summed + taps[k : k + 1] * values[HALO - 3 + k : HALO - 3 + k + tokens]
    return (summed / (1.0 + jnp.exp(-summed))).astype(jnp.bfloat16)


def conv_kernel(
    mine_ref, pre_ref, dt_ref, conv_ref, head_ref, x_ref, cum_ref, step_ref, scaled_ref
):
    tokens, channels = x_ref.shape
    halves, rows, _ = pre_ref.shape
    local = tokens // halves
    heads = dt_ref.shape[0]
    for part in range(halves):
        at = slice(part * local, (part + 1) * local)
        for lane in range(0, channels, 128):
            on = slice(lane, lane + 128)
            values = pre_ref[part, :, on].astype(jnp.float32)
            x_ref[at, on] = convolved(values, conv_ref[:, on], local)
    raw = dt_ref[...] + head_ref[:, 0:1]
    step_size = jnp.maximum(raw, 0.0) + jnp.log1p(jnp.exp(-jnp.abs(raw)))
    log_decay = -step_size * head_ref[:, 64:65]
    step_ref[...] = step_size
    upper = jnp.where(
        lax.broadcasted_iota(jnp.int32, (GROUP, GROUP), 0)
        <= lax.broadcasted_iota(jnp.int32, (GROUP, GROUP), 1),
        1.0,
        0.0,
    ).astype(jnp.bfloat16)
    spread = expander(heads, channels)
    for block in range(tokens // GROUP):
        at = slice(block * GROUP, (block + 1) * GROUP)
        cumulative = left_dot(log_decay[:, at], upper, ((1,), (0,)))
        cum_ref[:, at] = cumulative
        to_end = jnp.exp(cumulative[:, GROUP - 1 : GROUP] - cumulative) * step_size[:, at]
        wide = left_dot(to_end.T, spread, ((1,), (0,)))
        scaled = x_ref[at, :].astype(jnp.float32) * wide
        scaled_ref[:, at] = scaled.T.astype(jnp.bfloat16)


def state_kernel(
    mine_ref, bc_ref, conv_ref, cum_ref, scaled_ref, bconv_ref, pay_ref, local_ref
):
    rows = bc_ref.shape[1] // 2
    channels, tokens = scaled_ref.shape
    local = tokens // 2
    heads = cum_ref.shape[0]
    row = lax.broadcasted_iota(jnp.int32, (128, 128), 0)
    column = lax.broadcasted_iota(jnp.int32, (128, 128), 1)
    same = jnp.where(row == column, 1.0, 0.0).astype(jnp.bfloat16)
    for lane in range(0, 2 * N, 128):
        on = slice(lane, lane + 128)
        turned = dot(bc_ref[on], same, ((0,), (0,)))
        for part in range(2):
            at = slice(part * local, (part + 1) * local)
            values = turned[part * rows : (part + 1) * rows]
            bconv_ref[at, on] = convolved(values, conv_ref[:, on], local)
    total = jnp.zeros((heads, 1), jnp.float32)
    blocks = tokens // GROUP
    for block in range(blocks):
        at = slice(block * GROUP, (block + 1) * GROUP)
        added = dot(scaled_ref[:, at], bconv_ref[at, 0:N], ((1,), (0,)))
        end = cum_ref[:, (block + 1) * GROUP - 1 : (block + 1) * GROUP]
        total = total + end
        growth = jnp.exp(end)
        for head in range(heads):
            on = slice(head * HEAD, (head + 1) * HEAD)
            if block:
                local_ref[block, on] = (
                    local_ref[block - 1, on] * growth[head : head + 1] + added[on]
                )
            else:
                local_ref[block, on] = added[on]
    total = jnp.exp(total)
    high = total.astype(jnp.bfloat16).astype(jnp.float32)
    low = total - high
    share = pay_ref.shape[0] // heads
    tail_rows = pay_ref.shape[1] - 16
    row = lax.broadcasted_iota(jnp.int32, (tail_rows, N), 0)
    for head in range(heads):
        tail = jnp.where(
            row == 0, high[head : head + 1], jnp.where(row == 1, low[head : head + 1], 0.0)
        ).astype(jnp.bfloat16)
        for part in range(head * share, (head + 1) * share):
            pay_ref[part, 0:16] = local_ref[blocks - 1, part * 16 : (part + 1) * 16].astype(
                jnp.bfloat16
            )
            pay_ref[part, 16:] = tail


def prefix_kernel(at_ref, got_ref, start_ref, out_ref):
    running = start_ref[...]
    for source in range(got_ref.shape[0]):
        out_ref[source] = running.astype(jnp.bfloat16)
        tail = got_ref[source, 16:].astype(jnp.float32)
        running = (tail[0:1] + tail[1:2]) * running + got_ref[source, 0:16].astype(jnp.float32)


def inside_kernel(
    mine_ref, x_ref, bc_ref, cum_ref, step_ref, local_ref, chan_ref, out_ref, growth_ref
):
    tokens, channels = x_ref.shape
    heads = cum_ref.shape[0]
    spread = expander(heads, channels)
    causal = lax.broadcasted_iota(jnp.int32, (GROUP, GROUP), 0) >= lax.broadcasted_iota(
        jnp.int32, (GROUP, GROUP), 1
    )
    before = jnp.zeros((heads, 1), jnp.float32)
    for block in range(tokens // GROUP):
        at = slice(block * GROUP, (block + 1) * GROUP)
        c_block = bc_ref[at, N:]
        scores = dot(c_block, bc_ref[at, 0:N], ((1,), (1,)))
        cumulative = cum_ref[:, at]
        columns = cumulative.T
        growth_ref[at] = left_dot(jnp.exp(cumulative + before).T, spread, ((1,), (0,)))
        before = before + cumulative[:, GROUP - 1 : GROUP]
        rest = chan_ref[0:1] * x_ref[at].astype(jnp.float32)
        if block:
            carried = right_dot(c_block, local_ref[block - 1], ((1,), (1,)))
            rest = rest + left_dot(jnp.exp(columns), spread, ((1,), (0,))) * carried
        for pair in range(0, heads, 2):
            found = []
            for head in (pair, pair + 1):
                differ = columns[:, head : head + 1] - cumulative[head : head + 1]
                decays = jnp.exp(jnp.where(causal, differ, -1e30))
                mixing = (scores * decays * step_ref[head : head + 1, at]).astype(jnp.bfloat16)
                found.append(
                    dot(mixing, x_ref[at, head * HEAD : (head + 1) * HEAD], ((1,), (0,)))
                )
            on = slice(pair * HEAD, (pair + 2) * HEAD)
            out_ref[at, on] = jnp.concatenate(found, 1) + rest[:, on]


def output_kernel(
    mine_ref, inside_ref, growth_ref, bc_ref, entering_ref, chan_ref, keep_ref, send_ref, dot_ref
):
    mine = mine_ref[0]
    tokens, channels = inside_ref.shape
    local = tokens // 2
    spread = expander(channels // HEAD, channels)
    gain, steer = chan_ref[1:2], chan_ref[2:3]
    for block in range(tokens // GROUP):
        at = slice(block * GROUP, (block + 1) * GROUP)
        carried = dot(bc_ref[at, N:], entering_ref[...], ((1,), (1,)))
        y = inside_ref[at] + growth_ref[at] * carried
        squares = left_dot(y * y, spread, ((1,), (1,))) * (1.0 / HEAD)
        scale = left_dot(lax.rsqrt(squares + EPSILON), spread, ((1,), (0,)))
        normed = y * scale * gain
        part = block * GROUP // local
        on = slice(block * GROUP - part * local, (block + 1) * GROUP - part * local)

        @pl.when(mine == part)
        def _():
            keep_ref[on] = normed

        @pl.when(mine != part)
        def _():
            send_ref[on] = normed.astype(jnp.bfloat16)

        terms = normed * steer
        folded = terms[:, 0:128]
        for lane in range(128, channels, 128):
            folded = folded + terms[:, lane : lane + 128]
        dot_ref[part, :, on] = jnp.sum(folded.T, axis=0, keepdims=True)


def steer_kernel(factor, mine_ref, keep_ref, other_ref, dots_ref, chan_ref, out_ref):
    first = mine_ref[0] == 0
    half = keep_ref.shape[1]
    dots = dots_ref[...]
    for lane in range(0, half, 256):
        at = slice(lane, lane + 256)
        later = slice(half + lane, half + lane + 256)
        own, other = keep_ref[:, at], other_ref[:, at].astype(jnp.float32)
        left, right = jnp.where(first, own, other), jnp.where(first, other, own)
        for on, normed in ((at, left), (later, right)):
            steer = jnp.broadcast_to(chan_ref[2:3, on], (dots.shape[0], 256))
            penalty = dot(dots, steer, ((0,), (0,)), HIGHEST)
            out_ref[:, on] = (normed - penalty * factor).astype(jnp.bfloat16)


def prepare_parameters(d_skip, norm_gain, steer, dt_bias, decay_rate, z, start, at):
    channel_rows = jnp.concatenate(
        [
            jnp.repeat(d_skip, HEAD)[None], norm_gain[None], steer[None],
            jnp.zeros((5, steer.shape[0]), jnp.float32),
        ],
        0,
    )
    wide = (dt_bias.shape[0], 64)
    head_columns = jnp.concatenate(
        [jnp.broadcast_to(dt_bias[:, None], wide), jnp.broadcast_to(decay_rate[:, None], wide)], 1
    )
    source = (z + jnp.array(OFFSETS, jnp.int32)) % SIZES["z"]
    where = jnp.concatenate(
        [source // 2, (source % 2 == lax.axis_index("c")).astype(jnp.int32)]
    )
    start = lax.dynamic_slice_in_dim(start, at, start.shape[0] // SHARES, 0)
    return channel_rows, head_columns, where, start


def ring(block, depth, axis, prepare, raw):
    count = SIZES[axis]
    forward = [(i, (i + 1) % count) for i in range(count)]
    backward = [(i, (i - 1) % count) for i in range(count)]
    across = [(i, (i + count // 2) % count) for i in range(count)]
    pieces = [block]
    ahead = behind = block
    for hop in range(1, count // 2):
        ahead = lax.ppermute(ahead, axis, forward)
        behind = lax.ppermute(behind, axis, backward)
        if hop == 1:
            far = lax.ppermute(block[depth:], axis, across)
            ready = prepare(*lax.optimization_barrier((raw, far))[0])
            ahead, behind, far = lax.optimization_barrier((ahead, behind, far))
        elif hop == 2:
            ahead, behind, ready = lax.optimization_barrier((ahead, behind, ready))
        else:
            ahead, behind = lax.optimization_barrier((ahead, behind))
        pieces += [ahead, behind]
    pieces.append(lax.ppermute(ahead, axis, forward))
    return pieces, far, ready


def per_device(
    tokens, x_weight, bc_weight, dt_weight, conv_x, conv_bc, dt_bias, decay_rate, d_skip,
    norm_gain, initial_state, steer,
):
    local, width = tokens.shape
    k_rows, channels = x_weight.shape
    half = channels // 2
    heads = dt_weight.shape[1] // 2
    bc_rows = bc_weight.shape[1] // 2
    small = bc_rows + heads
    seq_count = SIZES["z"] * SIZES["x"] * SIZES["yl"]
    tp_count = SIZES["yh"] * SIZES["c"]
    z = lax.axis_index("z")
    mine = lax.axis_index("yl").astype(jnp.int32).reshape(1)
    f32, bf16 = jnp.float32, jnp.bfloat16

    earlier = lax.ppermute(
        tokens[local - HALO :], SEQ, [(i, i + 1) for i in range(seq_count - 1)]
    )
    extended = jnp.concatenate([earlier, tokens], 0)
    line = SIZES["yh"] * 2
    copies = jnp.broadcast_to(extended[None], (line,) + extended.shape)

    fan = SIZES["x"] * SIZES["yl"]
    packed_rows = small * k_rows // half
    packed = jnp.concatenate(
        [
            bc_weight.reshape(k_rows, 2, bc_rows).transpose(1, 2, 0),
            dt_weight.reshape(k_rows, 2, heads).transpose(1, 2, 0),
        ],
        1,
    ).reshape(2, packed_rows, half)
    panel = jnp.concatenate(
        [
            x_weight.reshape(k_rows, 2, half).transpose(1, 0, 2),
            packed,
            jnp.zeros((2, -packed_rows % 8, half), bf16),
        ],
        1,
    )
    panel = jnp.broadcast_to(panel[None], (SIZES["x"],) + panel.shape).reshape(
        fan, panel.shape[1], half
    )
    got = lax.all_to_all(panel, ("x", "yl"), 0, 0)
    copies, got = lax.optimization_barrier((copies, got))
    tall = got[:, :k_rows].reshape(fan * k_rows, half)
    flat = got[:, k_rows : k_rows + packed_rows].reshape(
        fan, packed_rows, half // k_rows, k_rows
    )
    flat = flat.transpose(1, 2, 0, 3).reshape(small, fan * k_rows)
    block = jnp.concatenate([tall, flat], 0)
    pieces, far, ready = ring(
        block, fan * k_rows, "z", prepare_parameters,
        (
            d_skip, norm_gain, steer, dt_bias, decay_rate, z.astype(jnp.int32),
            initial_state.reshape(channels, N),
            (lax.axis_index(("yl", "z", "x")) * (channels // SHARES)).astype(jnp.int32),
        ),
    )
    channel_rows, head_columns, where, start = ready

    own = lax.all_to_all(copies, ("yh", "yl"), 0, 0).reshape(
        SIZES["yh"], 2, local + HALO, width
    )
    own = lax.optimization_barrier((own, pieces[5]))[0]
    other = lax.ppermute(own, "c", [(0, 1), (1, 0)])

    bc_pre, dt_raw = narrow_project(where, own, other, pieces[:-1] + [far], bc_rows, heads, 2 * tp_count)
    pieces[-1] = lax.optimization_barrier((pieces[-1], bc_pre))[0]
    x_pre = project(where, own, other, pieces)
    bc_all = lax.all_to_all(bc_pre, ("yh", "c", "yl"), 0, 0).reshape(2 * N, -1)

    pair = 2 * local
    plane = SIZES["z"] * SIZES["x"]
    share = half // plane
    x_conv, cumulative, step_size, scaled = call(
        conv_kernel,
        [
            jax.ShapeDtypeStruct((pair, half), bf16),
            jax.ShapeDtypeStruct((heads, pair), f32),
            jax.ShapeDtypeStruct((heads, pair), f32),
            jax.ShapeDtypeStruct((half, pair), bf16),
        ],
        mine, x_pre, dt_raw, conv_x, head_columns,
        blocks={
            2: ((conv_x.shape[0], half), lambda i, s: (0, s[0])),
            3: ((heads, 128), lambda i, s: (s[0], 0)),
        },
        flops=10**9, bytes_accessed=8 * pair * half, grant=ALL_VMEM,
    )
    bc_conv, payload, locals_ = call(
        state_kernel,
        [
            jax.ShapeDtypeStruct((pair, 2 * N), bf16),
            jax.ShapeDtypeStruct((plane, share + 8, N), bf16),
            jax.ShapeDtypeStruct((pair // GROUP, half, N), f32),
        ],
        mine, bc_all, conv_bc, cumulative, scaled,
        grant=ALL_VMEM,
    )
    states = lax.all_to_all(payload, ("z", "x"), 0, 0)
    (prefixes,) = call(
        prefix_kernel,
        [jax.ShapeDtypeStruct((plane, share, N), bf16)],
        mine, states, start,
    )
    entering = lax.all_to_all(prefixes, ("z", "x"), 0, 0).reshape(half, N)

    lanes = ((8, half), lambda i, s: (0, s[0]))
    inside, growth = call(
        inside_kernel,
        [jax.ShapeDtypeStruct((pair, half), f32), jax.ShapeDtypeStruct((pair, half), f32)],
        mine, x_conv, bc_conv, cumulative, step_size, locals_, channel_rows,
        blocks={5: lanes},
        flops=10**9, bytes_accessed=12 * pair * half,
    )
    keep, send, dots = call(
        output_kernel,
        [
            jax.ShapeDtypeStruct((local, half), f32),
            jax.ShapeDtypeStruct((local, half), bf16),
            jax.ShapeDtypeStruct((2, 1, local), f32),
        ],
        mine, inside, growth, bc_conv, entering, channel_rows,
        blocks={4: lanes},
    )
    shape = (SIZES["yh"], 2, SIZES["c"], 1, local)
    partials = lax.all_to_all(
        jnp.broadcast_to(dots[None, :, None], shape).reshape(2 * tp_count, 1, local),
        ("yh", "yl", "c"), 0, 0,
    )
    swapped = lax.ppermute(send, "yl", [(0, 1), (1, 0)])
    factor = 1.0 / math.sqrt(channels * tp_count)
    (out,) = call(
        functools.partial(steer_kernel, factor),
        [jax.ShapeDtypeStruct((local, channels), bf16)],
        mine, keep, swapped, partials.reshape(2 * tp_count, local),
        channel_rows,
    )
    return out


def solution(mesh):
    fine = Mesh(mesh.devices.reshape(tuple(SIZES.values())), tuple(SIZES))
    both = P(SEQ, TP)
    placed = (
        both, both, both, both, P(None, TP), P(), P(TP), P(TP), P(TP), P(TP),
        P(TP, None, None), P(TP),
    )
    return jax.shard_map(
        per_device, mesh=fine, in_specs=placed, out_specs=both, check_vma=False
    )
```

```python
import functools
import math

import jax
import jax.numpy as jnp
from jax import lax
from jax.experimental import pallas as pl
from jax.experimental.pallas import tpu as pltpu
from jax.sharding import Mesh, PartitionSpec as P

EPSILON = 1e-05
GROUP = 128
N = 128
HALO = 16
HEAD = 64
ALL_VMEM = 67043328
HIGHEST = lax.Precision.HIGHEST

SEQ = ("z", "x", "yl")
TP = ("yh", "c")
SHARES = 64
OFFSETS = (0, -1, 1, -2, 2, -3, 3, 4)
SIZES = {"z": 8, "x": 4, "yl": 2, "yh": 4, "c": 2}


def call(
    kernel, outs, scalars, *args, blocks=None, scratch=(), flops=0, bytes_accessed=0,
    grant=20 * 1024 * 1024,
):
    blocks = blocks or {}
    specs = [
        pl.BlockSpec(*blocks[at])
        if at in blocks
        else pl.BlockSpec(arg.shape, functools.partial(lambda rank, i, s: (0,) * rank, arg.ndim))
        for at, arg in enumerate(args)
    ]
    whole = [
        pl.BlockSpec(out.shape, functools.partial(lambda rank, i, s: (0,) * rank, len(out.shape)))
        for out in outs
    ]
    return pl.pallas_call(
        kernel,
        grid_spec=pltpu.PrefetchScalarGridSpec(
            num_scalar_prefetch=1,
            grid=(1,),
            in_specs=specs,
            out_specs=whole,
            scratch_shapes=list(scratch),
        ),
        out_shape=outs,
        compiler_params=pltpu.CompilerParams(vmem_limit_bytes=grant),
        cost_estimate=pl.CostEstimate(
            flops=flops, bytes_accessed=bytes_accessed, transcendentals=0
        ),
    )(scalars, *args)


def dot(a, b, dims, precision=None):
    return lax.dot_general(
        a, b, (dims, ((), ())), precision=precision, preferred_element_type=jnp.float32
    )


def parts(value):
    high = value.astype(jnp.bfloat16)
    rest = value - high.astype(jnp.float32)
    middle = rest.astype(jnp.bfloat16)
    low = (rest - middle.astype(jnp.float32)).astype(jnp.bfloat16)
    return high, middle, low


def left_dot(value, exact, dims):
    return sum(dot(part, exact, dims) for part in parts(value))


def right_dot(exact, value, dims):
    return sum(dot(exact, part, dims) for part in parts(value))


def expander(heads, channels):
    row = lax.broadcasted_iota(jnp.int32, (heads, channels), 0)
    column = lax.broadcasted_iota(jnp.int32, (heads, channels), 1)
    return jnp.where(column // (channels // heads) == row, 1.0, 0.0).astype(jnp.bfloat16)


def fetch_tokens(where_ref, own_ref, other_ref, feats, sem):
    for step in range(feats.shape[0]):
        line, mine = where_ref[step], where_ref[feats.shape[0] + step] == 1

        @pl.when(mine)
        def _():
            pltpu.make_async_copy(own_ref.at[line], feats.at[step], sem.at[step]).start()

        @pl.when(jnp.logical_not(mine))
        def _():
            pltpu.make_async_copy(other_ref.at[line], feats.at[step], sem.at[step]).start()


def narrow_kernel(
    where_ref, own_ref, other_ref, w0, w1, w2, w3, w4, w5, w6, w7,
    bc_ref, dt_ref, feats, weights, small, sem, weight_sem,
):
    bc_rows, dt_rows = bc_ref.shape[1], dt_ref.shape[0]
    flat = bc_rows + dt_rows
    rows = feats.shape[2]
    tokens = rows - HALO
    blocks = feats.shape[0]
    fetch_tokens(where_ref, own_ref, other_ref, feats, sem)
    copies = []
    for at, ref in enumerate((w0, w1, w2, w3, w4, w5, w6, w7)):
        tall = ref.shape[0] - flat
        copies.append(
            pltpu.make_async_copy(
                ref.at[tall : tall + flat], weights.at[at], weight_sem.at[at]
            )
        )
        copies[at].start()
    small[...] = jnp.zeros_like(small)
    for step in range(blocks):
        pltpu.make_async_copy(own_ref.at[0], feats.at[step], sem.at[step]).wait()
        copies[step].wait()
        for part in range(2):
            small[part * rows : (part + 1) * rows, 0:flat] += dot(
                feats[step, part], weights[step], ((1,), (1,))
            )
    turned = small[...].T[0:bc_rows, 0 : 2 * rows].astype(jnp.bfloat16)
    for at in range(bc_ref.shape[0]):
        bc_ref[at] = turned
    for part in range(2):
        turned = small[part * rows + HALO : (part + 1) * rows].T
        dt_ref[:, part * tokens : (part + 1) * tokens] = turned[bc_rows:flat]


def project_kernel(
    where_ref, dt_ref, conv_ref, head_ref, own_ref, other_ref, w0, w1, w2, w3, w4, w5, w6, w7,
    x_ref, cum_ref, step_ref, scaled_ref, feats, weights, acc, pre, sem, weight_sem,
):
    blocks, depth = weights.shape[0], weights.shape[1]
    fetch_tokens(where_ref, own_ref, other_ref, feats, sem)
    copies = [
        pltpu.make_async_copy(ref.at[0:depth], weights.at[at], weight_sem.at[at])
        for at, ref in enumerate((w0, w1, w2, w3, w4, w5, w6, w7))
    ]
    for copy in copies:
        copy.start()
    for step in range(blocks):
        pltpu.make_async_copy(own_ref.at[0], feats.at[step], sem.at[step]).wait()
        copies[step].wait()
        for part in range(2):
            found = dot(feats[step, part], weights[step], ((1,), (0,)))
            if step == 0:
                acc[part] = found
            elif step < blocks - 1:
                acc[part] += found
            else:
                pre[part] = (acc[part] + found).astype(jnp.bfloat16)
    mine = where_ref[2 * blocks]
    heads, channels = dt_ref.shape[0], x_ref.shape[1]
    convolve_block(
        pre, dt_ref,
        conv_ref.at[:, pl.ds(pl.multiple_of(mine * channels, channels), channels)],
        head_ref.at[pl.ds(pl.multiple_of(mine * heads, heads), heads)],
        x_ref, cum_ref, step_ref, scaled_ref,
    )


def narrow_project(where, own, other, weights, bc_rows, dt_rows, copies):
    _, _, rows, depth = own.shape
    blocks = len(weights)
    flat = bc_rows + dt_rows
    return pl.pallas_call(
        narrow_kernel,
        in_specs=[pl.BlockSpec(memory_space=pltpu.SMEM)]
        + [pl.BlockSpec(memory_space=pl.ANY)] * (blocks + 2),
        out_specs=[pl.BlockSpec(memory_space=pltpu.VMEM)] * 2,
        scratch_shapes=[
            pltpu.VMEM((blocks, 2, rows, depth), jnp.bfloat16),
            pltpu.VMEM((blocks, flat, depth), jnp.bfloat16),
            pltpu.VMEM(((2 * rows + 127) // 128 * 128, 128), jnp.float32),
            pltpu.SemaphoreType.DMA((blocks,)),
            pltpu.SemaphoreType.DMA((blocks,)),
        ],
        out_shape=[
            jax.ShapeDtypeStruct((copies, bc_rows, 2 * rows), jnp.bfloat16),
            jax.ShapeDtypeStruct((dt_rows, 2 * (rows - HALO)), jnp.float32),
        ],
        compiler_params=pltpu.CompilerParams(vmem_limit_bytes=ALL_VMEM),
        cost_estimate=pl.CostEstimate(flops=10**9, bytes_accessed=10**7, transcendentals=0),
    )(where, own, other, *weights)


def project(where, dt_raw, conv_x, head_columns, own, other, weights):
    _, _, rows, depth = own.shape
    channels = weights[0].shape[1]
    blocks = len(weights)
    heads, tokens = dt_raw.shape
    vmem = pl.BlockSpec(memory_space=pltpu.VMEM)
    return pl.pallas_call(
        project_kernel,
        in_specs=[pl.BlockSpec(memory_space=pltpu.SMEM), vmem, vmem, vmem]
        + [pl.BlockSpec(memory_space=pl.ANY)] * (len(weights) + 2),
        out_specs=[vmem] * 4,
        scratch_shapes=[
            pltpu.VMEM((blocks, 2, rows, depth), jnp.bfloat16),
            pltpu.VMEM((blocks, depth, channels), jnp.bfloat16),
            pltpu.VMEM((2, rows, channels), jnp.float32),
            pltpu.VMEM((2, rows, channels), jnp.bfloat16),
            pltpu.SemaphoreType.DMA((blocks,)),
            pltpu.SemaphoreType.DMA((blocks,)),
        ],
        out_shape=[
            jax.ShapeDtypeStruct((tokens, channels), jnp.bfloat16),
            jax.ShapeDtypeStruct((heads, tokens), jnp.float32),
            jax.ShapeDtypeStruct((heads, tokens), jnp.float32),
            jax.ShapeDtypeStruct((channels, tokens), jnp.bfloat16),
        ],
        compiler_params=pltpu.CompilerParams(vmem_limit_bytes=ALL_VMEM),
        cost_estimate=pl.CostEstimate(
            flops=3 * 10**9, bytes_accessed=10**7, transcendentals=0
        ),
    )(where, dt_raw, conv_x, head_columns, own, other, *weights)


def convolved(values, taps, tokens):
    summed = taps[0:1] * values[HALO - 3 : HALO - 3 + tokens]
    for k in range(1, 4):
        summed = summed + taps[k : k + 1] * values[HALO - 3 + k : HALO - 3 + k + tokens]
    return (summed / (1.0 + jnp.exp(-summed))).astype(jnp.bfloat16)


def convolve_block(pre_ref, dt_ref, conv_ref, head_ref, x_ref, cum_ref, step_ref, scaled_ref):
    tokens, channels = x_ref.shape
    halves, rows, _ = pre_ref.shape
    local = tokens // halves
    heads = dt_ref.shape[0]
    for part in range(halves):
        at = slice(part * local, (part + 1) * local)
        for lane in range(0, channels, 128):
            on = slice(lane, lane + 128)
            values = pre_ref[part, :, on].astype(jnp.float32)
            x_ref[at, on] = convolved(values, conv_ref[:, on], local)
    raw = dt_ref[...] + head_ref[:, 0:1]
    step_size = jnp.maximum(raw, 0.0) + jnp.log1p(jnp.exp(-jnp.abs(raw)))
    log_decay = -step_size * head_ref[:, 64:65]
    step_ref[...] = step_size
    upper = jnp.where(
        lax.broadcasted_iota(jnp.int32, (GROUP, GROUP), 0)
        <= lax.broadcasted_iota(jnp.int32, (GROUP, GROUP), 1),
        1.0,
        0.0,
    ).astype(jnp.bfloat16)
    spread = expander(heads, channels)
    for block in range(tokens // GROUP):
        at = slice(block * GROUP, (block + 1) * GROUP)
        cumulative = left_dot(log_decay[:, at], upper, ((1,), (0,)))
        cum_ref[:, at] = cumulative
        to_end = jnp.exp(cumulative[:, GROUP - 1 : GROUP] - cumulative) * step_size[:, at]
        wide = left_dot(to_end.T, spread, ((1,), (0,)))
        scaled = x_ref[at, :].astype(jnp.float32) * wide
        scaled_ref[:, at] = scaled.T.astype(jnp.bfloat16)


def state_kernel(
    mine_ref, bc_ref, conv_ref, cum_ref, scaled_ref, bconv_ref, pay_ref, local_ref
):
    rows = bc_ref.shape[1] // 2
    channels, tokens = scaled_ref.shape
    local = tokens // 2
    heads = cum_ref.shape[0]
    row = lax.broadcasted_iota(jnp.int32, (128, 128), 0)
    column = lax.broadcasted_iota(jnp.int32, (128, 128), 1)
    same = jnp.where(row == column, 1.0, 0.0).astype(jnp.bfloat16)
    for lane in range(0, 2 * N, 128):
        on = slice(lane, lane + 128)
        turned = dot(bc_ref[on], same, ((0,), (0,)))
        for part in range(2):
            at = slice(part * local, (part + 1) * local)
            values = turned[part * rows : (part + 1) * rows]
            bconv_ref[at, on] = convolved(values, conv_ref[:, on], local)
    total = jnp.zeros((heads, 1), jnp.float32)
    blocks = tokens // GROUP
    for block in range(blocks):
        at = slice(block * GROUP, (block + 1) * GROUP)
        added = dot(scaled_ref[:, at], bconv_ref[at, 0:N], ((1,), (0,)))
        end = cum_ref[:, (block + 1) * GROUP - 1 : (block + 1) * GROUP]
        total = total + end
        growth = jnp.exp(end)
        for head in range(heads):
            on = slice(head * HEAD, (head + 1) * HEAD)
            if block:
                local_ref[block, on] = (
                    local_ref[block - 1, on] * growth[head : head + 1] + added[on]
                )
            else:
                local_ref[block, on] = added[on]
    total = jnp.exp(total)
    high = total.astype(jnp.bfloat16).astype(jnp.float32)
    low = total - high
    share = pay_ref.shape[0] // heads
    tail_rows = pay_ref.shape[1] - 16
    row = lax.broadcasted_iota(jnp.int32, (tail_rows, N), 0)
    for head in range(heads):
        tail = jnp.where(
            row == 0, high[head : head + 1], jnp.where(row == 1, low[head : head + 1], 0.0)
        ).astype(jnp.bfloat16)
        for part in range(head * share, (head + 1) * share):
            pay_ref[part, 0:16] = local_ref[blocks - 1, part * 16 : (part + 1) * 16].astype(
                jnp.bfloat16
            )
            pay_ref[part, 16:] = tail


def prefix_kernel(at_ref, got_ref, start_ref, out_ref):
    running = start_ref[...]
    for source in range(got_ref.shape[0]):
        out_ref[source] = running.astype(jnp.bfloat16)
        tail = got_ref[source, 16:].astype(jnp.float32)
        running = (tail[0:1] + tail[1:2]) * running + got_ref[source, 0:16].astype(jnp.float32)


def inside_kernel(
    mine_ref, x_ref, bc_ref, cum_ref, step_ref, local_ref, chan_ref, out_ref, growth_ref
):
    tokens, channels = x_ref.shape
    heads = cum_ref.shape[0]
    spread = expander(heads, channels)
    causal = lax.broadcasted_iota(jnp.int32, (GROUP, GROUP), 0) >= lax.broadcasted_iota(
        jnp.int32, (GROUP, GROUP), 1
    )
    before = jnp.zeros((heads, 1), jnp.float32)
    for block in range(tokens // GROUP):
        at = slice(block * GROUP, (block + 1) * GROUP)
        c_block = bc_ref[at, N:]
        scores = dot(c_block, bc_ref[at, 0:N], ((1,), (1,)))
        cumulative = cum_ref[:, at]
        columns = cumulative.T
        growth_ref[at] = left_dot(jnp.exp(cumulative + before).T, spread, ((1,), (0,)))
        before = before + cumulative[:, GROUP - 1 : GROUP]
        rest = chan_ref[0:1] * x_ref[at].astype(jnp.float32)
        if block:
            carried = right_dot(c_block, local_ref[block - 1], ((1,), (1,)))
            rest = rest + left_dot(jnp.exp(columns), spread, ((1,), (0,))) * carried
        for pair in range(0, heads, 2):
            found = []
            for head in (pair, pair + 1):
                differ = columns[:, head : head + 1] - cumulative[head : head + 1]
                decays = jnp.exp(jnp.where(causal, differ, -1e30))
                mixing = (scores * decays * step_ref[head : head + 1, at]).astype(jnp.bfloat16)
                found.append(
                    dot(mixing, x_ref[at, head * HEAD : (head + 1) * HEAD], ((1,), (0,)))
                )
            on = slice(pair * HEAD, (pair + 2) * HEAD)
            out_ref[at, on] = jnp.concatenate(found, 1) + rest[:, on]


def output_kernel(
    mine_ref, inside_ref, growth_ref, bc_ref, entering_ref, chan_ref, keep_ref, send_ref, dot_ref
):
    mine = mine_ref[0]
    tokens, channels = inside_ref.shape
    local = tokens // 2
    spread = expander(channels // HEAD, channels)
    gain, steer = chan_ref[1:2], chan_ref[2:3]
    for block in range(tokens // GROUP):
        at = slice(block * GROUP, (block + 1) * GROUP)
        carried = dot(bc_ref[at, N:], entering_ref[...], ((1,), (1,)))
        y = inside_ref[at] + growth_ref[at] * carried
        squares = left_dot(y * y, spread, ((1,), (1,))) * (1.0 / HEAD)
        scale = left_dot(lax.rsqrt(squares + EPSILON), spread, ((1,), (0,)))
        normed = y * scale * gain
        part = block * GROUP // local
        on = slice(block * GROUP - part * local, (block + 1) * GROUP - part * local)

        @pl.when(mine == part)
        def _():
            keep_ref[on] = normed

        @pl.when(mine != part)
        def _():
            send_ref[on] = normed.astype(jnp.bfloat16)

        terms = normed * steer
        folded = terms[:, 0:128]
        for lane in range(128, channels, 128):
            folded = folded + terms[:, lane : lane + 128]
        dot_ref[part, :, on] = jnp.sum(folded.T, axis=0, keepdims=True)


def steer_kernel(factor, mine_ref, keep_ref, other_ref, dots_ref, chan_ref, out_ref):
    first = mine_ref[0] == 0
    half = keep_ref.shape[1]
    dots = dots_ref[...]
    for lane in range(0, half, 256):
        at = slice(lane, lane + 256)
        later = slice(half + lane, half + lane + 256)
        own, other = keep_ref[:, at], other_ref[:, at].astype(jnp.float32)
        left, right = jnp.where(first, own, other), jnp.where(first, other, own)
        for on, normed in ((at, left), (later, right)):
            steer = jnp.broadcast_to(chan_ref[2:3, on], (dots.shape[0], 256))
            penalty = dot(dots, steer, ((0,), (0,)), HIGHEST)
            out_ref[:, on] = (normed - penalty * factor).astype(jnp.bfloat16)


def prepare_parameters(d_skip, norm_gain, steer, dt_bias, decay_rate, z, start, at):
    channel_rows = jnp.concatenate(
        [
            jnp.repeat(d_skip, HEAD)[None], norm_gain[None], steer[None],
            jnp.zeros((5, steer.shape[0]), jnp.float32),
        ],
        0,
    )
    wide = (dt_bias.shape[0], 64)
    head_columns = jnp.concatenate(
        [jnp.broadcast_to(dt_bias[:, None], wide), jnp.broadcast_to(decay_rate[:, None], wide)], 1
    )
    source = (z + jnp.array(OFFSETS, jnp.int32)) % SIZES["z"]
    where = jnp.concatenate(
        [
            source // 2, (source % 2 == lax.axis_index("c")).astype(jnp.int32),
            lax.axis_index("yl").astype(jnp.int32).reshape(1),
        ]
    )
    start = lax.dynamic_slice_in_dim(start, at, start.shape[0] // SHARES, 0)
    return channel_rows, head_columns, where, start


def ring(block, depth, axis, prepare, raw):
    count = SIZES[axis]
    forward = [(i, (i + 1) % count) for i in range(count)]
    backward = [(i, (i - 1) % count) for i in range(count)]
    across = [(i, (i + count // 2) % count) for i in range(count)]
    pieces = [block]
    ahead = behind = block
    for hop in range(1, count // 2):
        ahead = lax.ppermute(ahead, axis, forward)
        behind = lax.ppermute(behind, axis, backward)
        if hop == 1:
            far = lax.ppermute(block[depth:], axis, across)
            ready = prepare(*lax.optimization_barrier((raw, far))[0])
            ahead, behind, far = lax.optimization_barrier((ahead, behind, far))
        elif hop == 2:
            ahead, behind, ready = lax.optimization_barrier((ahead, behind, ready))
        else:
            ahead, behind = lax.optimization_barrier((ahead, behind))
        pieces += [ahead, behind]
    pieces.append(lax.ppermute(ahead, axis, forward))
    return pieces, far, ready


def per_device(
    tokens, x_weight, bc_weight, dt_weight, conv_x, conv_bc, dt_bias, decay_rate, d_skip,
    norm_gain, initial_state, steer,
):
    local, width = tokens.shape
    k_rows, channels = x_weight.shape
    half = channels // 2
    heads = dt_weight.shape[1] // 2
    bc_rows = bc_weight.shape[1] // 2
    small = bc_rows + heads
    seq_count = SIZES["z"] * SIZES["x"] * SIZES["yl"]
    tp_count = SIZES["yh"] * SIZES["c"]
    z = lax.axis_index("z")
    mine = lax.axis_index("yl").astype(jnp.int32).reshape(1)
    f32, bf16 = jnp.float32, jnp.bfloat16

    earlier = lax.ppermute(
        tokens[local - HALO :], SEQ, [(i, i + 1) for i in range(seq_count - 1)]
    )
    extended = jnp.concatenate([earlier, tokens], 0)
    line = SIZES["yh"] * 2
    copies = jnp.broadcast_to(extended[None], (line,) + extended.shape)

    fan = SIZES["x"] * SIZES["yl"]
    packed_rows = small * k_rows // half
    packed = jnp.concatenate(
        [
            bc_weight.reshape(k_rows, 2, bc_rows).transpose(1, 2, 0),
            dt_weight.reshape(k_rows, 2, heads).transpose(1, 2, 0),
        ],
        1,
    ).reshape(2, packed_rows, half)
    panel = jnp.concatenate(
        [
            jnp.stack([x_weight[:, :half], x_weight[:, half:]]),
            packed,
            jnp.zeros((2, -packed_rows % 8, half), bf16),
        ],
        1,
    )
    panel = jnp.broadcast_to(panel[None], (SIZES["x"],) + panel.shape).reshape(
        fan, panel.shape[1], half
    )
    got = lax.all_to_all(panel, ("x", "yl"), 0, 0)
    copies, got = lax.optimization_barrier((copies, got))
    tall = got[:, :k_rows].reshape(fan * k_rows, half)
    flat = got[:, k_rows : k_rows + packed_rows].reshape(
        fan, packed_rows, half // k_rows, k_rows
    )
    flat = flat.transpose(1, 2, 0, 3).reshape(small, fan * k_rows)
    block = jnp.concatenate([tall, flat], 0)
    pieces, far, ready = ring(
        block, fan * k_rows, "z", prepare_parameters,
        (
            d_skip, norm_gain, steer, dt_bias, decay_rate, z.astype(jnp.int32),
            initial_state.reshape(channels, N),
            (lax.axis_index(("yl", "z", "x")) * (channels // SHARES)).astype(jnp.int32),
        ),
    )
    channel_rows, head_columns, where, start = ready

    own = lax.all_to_all(copies, ("yh", "yl"), 0, 0).reshape(
        SIZES["yh"], 2, local + HALO, width
    )
    own = lax.optimization_barrier((own, pieces[5]))[0]
    other = lax.ppermute(own, "c", [(0, 1), (1, 0)])

    bc_pre, dt_raw = narrow_project(where, own, other, pieces[:-1] + [far], bc_rows, heads, 2 * tp_count)
    pieces[-1] = lax.optimization_barrier((pieces[-1], bc_pre))[0]
    x_conv, cumulative, step_size, scaled = project(
        where, dt_raw, conv_x, head_columns, own, other, pieces
    )
    bc_all = lax.all_to_all(bc_pre, ("yh", "c", "yl"), 0, 0).reshape(2 * N, -1)

    pair = 2 * local
    plane = SIZES["z"] * SIZES["x"]
    share = half // plane
    bc_conv, payload, locals_ = call(
        state_kernel,
        [
            jax.ShapeDtypeStruct((pair, 2 * N), bf16),
            jax.ShapeDtypeStruct((plane, share + 8, N), bf16),
            jax.ShapeDtypeStruct((pair // GROUP, half, N), f32),
        ],
        mine, bc_all, conv_bc, cumulative, scaled,
        grant=ALL_VMEM,
    )
    states = lax.all_to_all(payload, ("z", "x"), 0, 0)
    (prefixes,) = call(
        prefix_kernel,
        [jax.ShapeDtypeStruct((plane, share, N), bf16)],
        mine, states, start,
    )
    entering = lax.all_to_all(prefixes, ("z", "x"), 0, 0).reshape(half, N)

    lanes = ((8, half), lambda i, s: (0, s[0]))
    inside, growth = call(
        inside_kernel,
        [jax.ShapeDtypeStruct((pair, half), f32), jax.ShapeDtypeStruct((pair, half), f32)],
        mine, x_conv, bc_conv, cumulative, step_size, locals_, channel_rows,
        blocks={5: lanes},
        flops=10**9, bytes_accessed=12 * pair * half,
    )
    keep, send, dots = call(
        output_kernel,
        [
            jax.ShapeDtypeStruct((local, half), f32),
            jax.ShapeDtypeStruct((local, half), bf16),
            jax.ShapeDtypeStruct((2, 1, local), f32),
        ],
        mine, inside, growth, bc_conv, entering, channel_rows,
        blocks={4: lanes},
    )
    shape = (SIZES["yh"], 2, SIZES["c"], 1, local)
    partials = lax.all_to_all(
        jnp.broadcast_to(dots[None, :, None], shape).reshape(2 * tp_count, 1, local),
        ("yh", "yl", "c"), 0, 0,
    )
    swapped = lax.ppermute(send, "yl", [(0, 1), (1, 0)])
    factor = 1.0 / math.sqrt(channels * tp_count)
    (out,) = call(
        functools.partial(steer_kernel, factor),
        [jax.ShapeDtypeStruct((local, channels), bf16)],
        mine, keep, swapped, partials.reshape(2 * tp_count, local),
        channel_rows,
    )
    return out


def solution(mesh):
    fine = Mesh(mesh.devices.reshape(tuple(SIZES.values())), tuple(SIZES))
    both = P(SEQ, TP)
    placed = (
        both, both, both, both, P(None, TP), P(), P(TP), P(TP), P(TP), P(TP),
        P(TP, None, None), P(TP),
    )
    return jax.shard_map(
        per_device, mesh=fine, in_specs=placed, out_specs=both, check_vma=False
    )
```

```python
import functools
import math

import jax
import jax.numpy as jnp
from jax import lax
from jax.experimental import pallas as pl
from jax.experimental.pallas import tpu as pltpu
from jax.sharding import Mesh, PartitionSpec as P

EPSILON = 1e-05
GROUP = 128
N = 128
HALO = 16
HEAD = 64
ALL_VMEM = 67043328
HIGHEST = lax.Precision.HIGHEST

SEQ = ("z", "x", "yl")
TP = ("yh", "c")
SHARES = 64
OFFSETS = (0, -1, 1, -2, 2, -3, 3, 4)
SIZES = {"z": 8, "x": 4, "yl": 2, "yh": 4, "c": 2}


def call(
    kernel, outs, scalars, *args, blocks=None, scratch=(), flops=0, bytes_accessed=0,
    grant=20 * 1024 * 1024,
):
    blocks = blocks or {}
    specs = [
        pl.BlockSpec(*blocks[at])
        if at in blocks
        else pl.BlockSpec(arg.shape, functools.partial(lambda rank, i, s: (0,) * rank, arg.ndim))
        for at, arg in enumerate(args)
    ]
    whole = [
        pl.BlockSpec(out.shape, functools.partial(lambda rank, i, s: (0,) * rank, len(out.shape)))
        for out in outs
    ]
    return pl.pallas_call(
        kernel,
        grid_spec=pltpu.PrefetchScalarGridSpec(
            num_scalar_prefetch=1,
            grid=(1,),
            in_specs=specs,
            out_specs=whole,
            scratch_shapes=list(scratch),
        ),
        out_shape=outs,
        compiler_params=pltpu.CompilerParams(vmem_limit_bytes=grant),
        cost_estimate=pl.CostEstimate(
            flops=flops, bytes_accessed=bytes_accessed, transcendentals=0
        ),
    )(scalars, *args)


def dot(a, b, dims, precision=None):
    return lax.dot_general(
        a, b, (dims, ((), ())), precision=precision, preferred_element_type=jnp.float32
    )


def parts(value):
    high = value.astype(jnp.bfloat16)
    rest = value - high.astype(jnp.float32)
    middle = rest.astype(jnp.bfloat16)
    low = (rest - middle.astype(jnp.float32)).astype(jnp.bfloat16)
    return high, middle, low


def left_dot(value, exact, dims):
    return sum(dot(part, exact, dims) for part in parts(value))


def right_dot(exact, value, dims):
    return sum(dot(exact, part, dims) for part in parts(value))


def expander(heads, channels):
    row = lax.broadcasted_iota(jnp.int32, (heads, channels), 0)
    column = lax.broadcasted_iota(jnp.int32, (heads, channels), 1)
    return jnp.where(column // (channels // heads) == row, 1.0, 0.0).astype(jnp.bfloat16)


def fetch_tokens(where_ref, own_ref, other_ref, feats, sem):
    for step in range(feats.shape[0]):
        line, mine = where_ref[step], where_ref[feats.shape[0] + step] == 1

        @pl.when(mine)
        def _():
            pltpu.make_async_copy(own_ref.at[line], feats.at[step], sem.at[step]).start()

        @pl.when(jnp.logical_not(mine))
        def _():
            pltpu.make_async_copy(other_ref.at[line], feats.at[step], sem.at[step]).start()


def narrow_kernel(
    where_ref, own_ref, other_ref, w0, w1, w2, w3, w4, w5, w6, w7,
    bc_ref, dt_ref, feats, weights, small, sem, weight_sem,
):
    bc_rows, dt_rows = bc_ref.shape[1], dt_ref.shape[0]
    flat = bc_rows + dt_rows
    rows = feats.shape[2]
    tokens = rows - HALO
    blocks = feats.shape[0]
    fetch_tokens(where_ref, own_ref, other_ref, feats, sem)
    copies = []
    for at, ref in enumerate((w0, w1, w2, w3, w4, w5, w6, w7)):
        tall = ref.shape[0] - flat
        copies.append(
            pltpu.make_async_copy(
                ref.at[tall : tall + flat], weights.at[at], weight_sem.at[at]
            )
        )
        copies[at].start()
    small[...] = jnp.zeros_like(small)
    for step in range(blocks):
        pltpu.make_async_copy(own_ref.at[0], feats.at[step], sem.at[step]).wait()
        copies[step].wait()
        for part in range(2):
            small[part * rows : (part + 1) * rows, 0:flat] += dot(
                feats[step, part], weights[step], ((1,), (1,))
            )
    turned = small[...].T[0:bc_rows, 0 : 2 * rows].astype(jnp.bfloat16)
    for at in range(bc_ref.shape[0]):
        bc_ref[at] = turned
    for part in range(2):
        turned = small[part * rows + HALO : (part + 1) * rows].T
        dt_ref[:, part * tokens : (part + 1) * tokens] = turned[bc_rows:flat]


def project_kernel(
    where_ref, dt_ref, conv_ref, head_ref, own_ref, other_ref, w0, w1, w2, w3, w4, w5, w6, w7,
    x_ref, cum_ref, step_ref, scaled_ref, feats, weights, acc, pre, sem, weight_sem,
):
    blocks, depth = weights.shape[0], weights.shape[1]
    fetch_tokens(where_ref, own_ref, other_ref, feats, sem)
    copies = [
        pltpu.make_async_copy(ref.at[0:depth], weights.at[at], weight_sem.at[at])
        for at, ref in enumerate((w0, w1, w2, w3, w4, w5, w6, w7))
    ]
    for copy in copies:
        copy.start()
    for step in range(blocks):
        pltpu.make_async_copy(own_ref.at[0], feats.at[step], sem.at[step]).wait()
        copies[step].wait()
        for part in range(2):
            found = dot(feats[step, part], weights[step], ((1,), (0,)))
            if step == 0:
                acc[part] = found
            elif step < blocks - 1:
                acc[part] += found
            else:
                pre[part] = (acc[part] + found).astype(jnp.bfloat16)
    mine = where_ref[2 * blocks]
    heads, channels = dt_ref.shape[0], x_ref.shape[1]
    convolve_block(
        pre, dt_ref,
        conv_ref.at[:, pl.ds(pl.multiple_of(mine * channels, channels), channels)],
        head_ref.at[pl.ds(pl.multiple_of(mine * heads, heads), heads)],
        x_ref, cum_ref, step_ref, scaled_ref,
    )


def narrow_project(where, own, other, weights, bc_rows, dt_rows, copies):
    _, _, rows, depth = own.shape
    blocks = len(weights)
    flat = bc_rows + dt_rows
    return pl.pallas_call(
        narrow_kernel,
        in_specs=[pl.BlockSpec(memory_space=pltpu.SMEM)]
        + [pl.BlockSpec(memory_space=pl.ANY)] * (blocks + 2),
        out_specs=[pl.BlockSpec(memory_space=pltpu.VMEM)] * 2,
        scratch_shapes=[
            pltpu.VMEM((blocks, 2, rows, depth), jnp.bfloat16),
            pltpu.VMEM((blocks, flat, depth), jnp.bfloat16),
            pltpu.VMEM(((2 * rows + 127) // 128 * 128, 128), jnp.float32),
            pltpu.SemaphoreType.DMA((blocks,)),
            pltpu.SemaphoreType.DMA((blocks,)),
        ],
        out_shape=[
            jax.ShapeDtypeStruct((copies, bc_rows, 2 * rows), jnp.bfloat16),
            jax.ShapeDtypeStruct((dt_rows, 2 * (rows - HALO)), jnp.float32),
        ],
        compiler_params=pltpu.CompilerParams(vmem_limit_bytes=64000000),
        cost_estimate=pl.CostEstimate(flops=10**9, bytes_accessed=10**7, transcendentals=0),
    )(where, own, other, *weights)


def project(where, dt_raw, conv_x, head_columns, own, other, weights):
    _, _, rows, depth = own.shape
    channels = weights[0].shape[1]
    blocks = len(weights)
    heads, tokens = dt_raw.shape
    vmem = pl.BlockSpec(memory_space=pltpu.VMEM)
    return pl.pallas_call(
        project_kernel,
        in_specs=[pl.BlockSpec(memory_space=pltpu.SMEM), vmem, vmem, vmem]
        + [pl.BlockSpec(memory_space=pl.ANY)] * (len(weights) + 2),
        out_specs=[vmem] * 4,
        scratch_shapes=[
            pltpu.VMEM((blocks, 2, rows, depth), jnp.bfloat16),
            pltpu.VMEM((blocks, depth, channels), jnp.bfloat16),
            pltpu.VMEM((2, rows, channels), jnp.float32),
            pltpu.VMEM((2, rows, channels), jnp.bfloat16),
            pltpu.SemaphoreType.DMA((blocks,)),
            pltpu.SemaphoreType.DMA((blocks,)),
        ],
        out_shape=[
            jax.ShapeDtypeStruct((tokens, channels), jnp.bfloat16),
            jax.ShapeDtypeStruct((heads, tokens), jnp.float32),
            jax.ShapeDtypeStruct((heads, tokens), jnp.float32),
            jax.ShapeDtypeStruct((channels, tokens), jnp.bfloat16),
        ],
        compiler_params=pltpu.CompilerParams(vmem_limit_bytes=64000000),
        cost_estimate=pl.CostEstimate(
            flops=3 * 10**9, bytes_accessed=10**7, transcendentals=0
        ),
    )(where, dt_raw, conv_x, head_columns, own, other, *weights)


def convolved(values, taps, tokens):
    summed = taps[0:1] * values[HALO - 3 : HALO - 3 + tokens]
    for k in range(1, 4):
        summed = summed + taps[k : k + 1] * values[HALO - 3 + k : HALO - 3 + k + tokens]
    return (summed / (1.0 + jnp.exp(-summed))).astype(jnp.bfloat16)


def convolve_block(pre_ref, dt_ref, conv_ref, head_ref, x_ref, cum_ref, step_ref, scaled_ref):
    tokens, channels = x_ref.shape
    halves, rows, _ = pre_ref.shape
    local = tokens // halves
    heads = dt_ref.shape[0]
    for part in range(halves):
        at = slice(part * local, (part + 1) * local)
        for lane in range(0, channels, 128):
            on = slice(lane, lane + 128)
            values = pre_ref[part, :, on].astype(jnp.float32)
            x_ref[at, on] = convolved(values, conv_ref[:, on], local)
    raw = dt_ref[...] + head_ref[:, 0:1]
    step_size = jnp.maximum(raw, 0.0) + jnp.log1p(jnp.exp(-jnp.abs(raw)))
    log_decay = -step_size * head_ref[:, 64:65]
    step_ref[...] = step_size
    upper = jnp.where(
        lax.broadcasted_iota(jnp.int32, (GROUP, GROUP), 0)
        <= lax.broadcasted_iota(jnp.int32, (GROUP, GROUP), 1),
        1.0,
        0.0,
    ).astype(jnp.bfloat16)
    spread = expander(heads, channels)
    for block in range(tokens // GROUP):
        at = slice(block * GROUP, (block + 1) * GROUP)
        cumulative = left_dot(log_decay[:, at], upper, ((1,), (0,)))
        cum_ref[:, at] = cumulative
        to_end = jnp.exp(cumulative[:, GROUP - 1 : GROUP] - cumulative) * step_size[:, at]
        wide = left_dot(to_end.T, spread, ((1,), (0,)))
        scaled = x_ref[at, :].astype(jnp.float32) * wide
        scaled_ref[:, at] = scaled.T.astype(jnp.bfloat16)


def state_kernel(
    mine_ref, bc_ref, conv_ref, cum_ref, scaled_ref, bconv_ref, pay_ref, local_ref
):
    rows = bc_ref.shape[1] // 2
    channels, tokens = scaled_ref.shape
    local = tokens // 2
    heads = cum_ref.shape[0]
    row = lax.broadcasted_iota(jnp.int32, (128, 128), 0)
    column = lax.broadcasted_iota(jnp.int32, (128, 128), 1)
    same = jnp.where(row == column, 1.0, 0.0).astype(jnp.bfloat16)
    for lane in range(0, 2 * N, 128):
        on = slice(lane, lane + 128)
        turned = dot(bc_ref[on], same, ((0,), (0,)))
        for part in range(2):
            at = slice(part * local, (part + 1) * local)
            values = turned[part * rows : (part + 1) * rows]
            bconv_ref[at, on] = convolved(values, conv_ref[:, on], local)
    total = jnp.zeros((heads, 1), jnp.float32)
    blocks = tokens // GROUP
    for block in range(blocks):
        at = slice(block * GROUP, (block + 1) * GROUP)
        added = dot(scaled_ref[:, at], bconv_ref[at, 0:N], ((1,), (0,)))
        end = cum_ref[:, (block + 1) * GROUP - 1 : (block + 1) * GROUP]
        total = total + end
        growth = jnp.exp(end)
        for head in range(heads):
            on = slice(head * HEAD, (head + 1) * HEAD)
            if block:
                local_ref[block, on] = (
                    local_ref[block - 1, on] * growth[head : head + 1] + added[on]
                )
            else:
                local_ref[block, on] = added[on]
    total = jnp.exp(total)
    high = total.astype(jnp.bfloat16).astype(jnp.float32)
    low = total - high
    share = pay_ref.shape[0] // heads
    tail_rows = pay_ref.shape[1] - 16
    row = lax.broadcasted_iota(jnp.int32, (tail_rows, N), 0)
    for head in range(heads):
        tail = jnp.where(
            row == 0, high[head : head + 1], jnp.where(row == 1, low[head : head + 1], 0.0)
        ).astype(jnp.bfloat16)
        for part in range(head * share, (head + 1) * share):
            pay_ref[part, 0:16] = local_ref[blocks - 1, part * 16 : (part + 1) * 16].astype(
                jnp.bfloat16
            )
            pay_ref[part, 16:] = tail


def prefix_kernel(at_ref, got_ref, start_ref, out_ref):
    running = start_ref[...]
    for source in range(got_ref.shape[0]):
        out_ref[source] = running.astype(jnp.bfloat16)
        tail = got_ref[source, 16:].astype(jnp.float32)
        running = (tail[0:1] + tail[1:2]) * running + got_ref[source, 0:16].astype(jnp.float32)


def inside_kernel(
    mine_ref, x_ref, bc_ref, cum_ref, step_ref, local_ref, chan_ref, out_ref, growth_ref
):
    tokens, channels = x_ref.shape
    heads = cum_ref.shape[0]
    spread = expander(heads, channels)
    causal = lax.broadcasted_iota(jnp.int32, (GROUP, GROUP), 0) >= lax.broadcasted_iota(
        jnp.int32, (GROUP, GROUP), 1
    )
    before = jnp.zeros((heads, 1), jnp.float32)
    for block in range(tokens // GROUP):
        at = slice(block * GROUP, (block + 1) * GROUP)
        c_block = bc_ref[at, N:]
        scores = dot(c_block, bc_ref[at, 0:N], ((1,), (1,)))
        cumulative = cum_ref[:, at]
        columns = cumulative.T
        growth_ref[at] = left_dot(jnp.exp(cumulative + before).T, spread, ((1,), (0,)))
        before = before + cumulative[:, GROUP - 1 : GROUP]
        rest = chan_ref[0:1] * x_ref[at].astype(jnp.float32)
        if block:
            carried = right_dot(c_block, local_ref[block - 1], ((1,), (1,)))
            rest = rest + left_dot(jnp.exp(columns), spread, ((1,), (0,))) * carried
        for pair in range(0, heads, 2):
            found = []
            for head in (pair, pair + 1):
                differ = columns[:, head : head + 1] - cumulative[head : head + 1]
                decays = jnp.exp(jnp.where(causal, differ, -1e30))
                mixing = (scores * decays * step_ref[head : head + 1, at]).astype(jnp.bfloat16)
                found.append(
                    dot(mixing, x_ref[at, head * HEAD : (head + 1) * HEAD], ((1,), (0,)))
                )
            on = slice(pair * HEAD, (pair + 2) * HEAD)
            out_ref[at, on] = jnp.concatenate(found, 1) + rest[:, on]


def output_kernel(
    mine_ref, inside_ref, growth_ref, bc_ref, entering_ref, chan_ref, keep_ref, send_ref, dot_ref
):
    mine = mine_ref[0]
    tokens, channels = inside_ref.shape
    local = tokens // 2
    spread = expander(channels // HEAD, channels)
    gain, steer = chan_ref[1:2], chan_ref[2:3]
    for block in range(tokens // GROUP):
        at = slice(block * GROUP, (block + 1) * GROUP)
        carried = dot(bc_ref[at, N:], entering_ref[...], ((1,), (1,)))
        y = inside_ref[at] + growth_ref[at] * carried
        squares = left_dot(y * y, spread, ((1,), (1,))) * (1.0 / HEAD)
        scale = left_dot(lax.rsqrt(squares + EPSILON), spread, ((1,), (0,)))
        normed = y * scale * gain
        part = block * GROUP // local
        on = slice(block * GROUP - part * local, (block + 1) * GROUP - part * local)

        @pl.when(mine == part)
        def _():
            keep_ref[on] = normed

        @pl.when(mine != part)
        def _():
            send_ref[on] = normed.astype(jnp.bfloat16)

        terms = normed * steer
        folded = terms[:, 0:128]
        for lane in range(128, channels, 128):
            folded = folded + terms[:, lane : lane + 128]
        dot_ref[part, :, on] = jnp.sum(folded.T, axis=0, keepdims=True)


def steer_kernel(factor, mine_ref, keep_ref, other_ref, dots_ref, chan_ref, out_ref):
    first = mine_ref[0] == 0
    half = keep_ref.shape[1]
    dots = dots_ref[...]
    for lane in range(0, half, 256):
        at = slice(lane, lane + 256)
        later = slice(half + lane, half + lane + 256)
        own, other = keep_ref[:, at], other_ref[:, at].astype(jnp.float32)
        left, right = jnp.where(first, own, other), jnp.where(first, other, own)
        for on, normed in ((at, left), (later, right)):
            steer = jnp.broadcast_to(chan_ref[2:3, on], (dots.shape[0], 256))
            penalty = dot(dots, steer, ((0,), (0,)), HIGHEST)
            out_ref[:, on] = (normed - penalty * factor).astype(jnp.bfloat16)


def prepare_parameters(d_skip, norm_gain, steer, dt_bias, decay_rate, z, start, at):
    channel_rows = jnp.concatenate(
        [
            jnp.repeat(d_skip, HEAD)[None], norm_gain[None], steer[None],
            jnp.zeros((5, steer.shape[0]), jnp.float32),
        ],
        0,
    )
    wide = (dt_bias.shape[0], 64)
    head_columns = jnp.concatenate(
        [jnp.broadcast_to(dt_bias[:, None], wide), jnp.broadcast_to(decay_rate[:, None], wide)], 1
    )
    source = (z + jnp.array(OFFSETS, jnp.int32)) % SIZES["z"]
    where = jnp.concatenate(
        [
            source // 2, (source % 2 == lax.axis_index("c")).astype(jnp.int32),
            lax.axis_index("yl").astype(jnp.int32).reshape(1),
        ]
    )
    start = lax.dynamic_slice_in_dim(start, at, start.shape[0] // SHARES, 0)
    return channel_rows, head_columns, where, start


def ring(block, depth, axis, prepare, raw):
    count = SIZES[axis]
    forward = [(i, (i + 1) % count) for i in range(count)]
    backward = [(i, (i - 1) % count) for i in range(count)]
    across = [(i, (i + count // 2) % count) for i in range(count)]
    pieces = [block]
    ahead = behind = block
    for hop in range(1, count // 2):
        ahead = lax.ppermute(ahead, axis, forward)
        behind = lax.ppermute(behind, axis, backward)
        if hop == 2:
            ready = prepare(*raw)
            far = lax.ppermute(small, axis, across)
            ahead, behind, ready, far = lax.optimization_barrier((ahead, behind, ready, far))
        elif hop == 1:
            ahead, behind = lax.optimization_barrier((ahead, behind))
            small, raw = lax.optimization_barrier((block[depth:], raw, ahead))[:2]
        else:
            ahead, behind = lax.optimization_barrier((ahead, behind))
        pieces += [ahead, behind]
    pieces.append(lax.ppermute(ahead, axis, forward))
    return pieces, far, ready


def per_device(
    tokens, x_weight, bc_weight, dt_weight, conv_x, conv_bc, dt_bias, decay_rate, d_skip,
    norm_gain, initial_state, steer,
):
    local, width = tokens.shape
    k_rows, channels = x_weight.shape
    half = channels // 2
    heads = dt_weight.shape[1] // 2
    bc_rows = bc_weight.shape[1] // 2
    small = bc_rows + heads
    seq_count = SIZES["z"] * SIZES["x"] * SIZES["yl"]
    tp_count = SIZES["yh"] * SIZES["c"]
    z = lax.axis_index("z")
    mine = lax.axis_index("yl").astype(jnp.int32).reshape(1)
    f32, bf16 = jnp.float32, jnp.bfloat16

    earlier = lax.ppermute(
        tokens[local - HALO :], SEQ, [(i, i + 1) for i in range(seq_count - 1)]
    )
    extended = jnp.concatenate([earlier, tokens], 0)
    line = SIZES["yh"] * 2
    copies = jnp.broadcast_to(extended[None], (line,) + extended.shape)

    fan = SIZES["x"] * SIZES["yl"]
    packed_rows = small * k_rows // half
    packed = jnp.concatenate(
        [
            bc_weight.reshape(k_rows, 2, bc_rows).transpose(1, 2, 0),
            dt_weight.reshape(k_rows, 2, heads).transpose(1, 2, 0),
        ],
        1,
    ).reshape(2, packed_rows, half)
    panel = jnp.concatenate(
        [
            jnp.stack([x_weight[:, :half], x_weight[:, half:]]),
            packed,
            jnp.zeros((2, -packed_rows % 8, half), bf16),
        ],
        1,
    )
    panel = jnp.broadcast_to(panel[None], (SIZES["x"],) + panel.shape).reshape(
        fan, panel.shape[1], half
    )
    got = lax.all_to_all(panel, ("x", "yl"), 0, 0)
    copies, got = lax.optimization_barrier((copies, got))
    tall = got[:, :k_rows].reshape(fan * k_rows, half)
    flat = got[:, k_rows : k_rows + packed_rows].reshape(
        fan, packed_rows, half // k_rows, k_rows
    )
    flat = flat.transpose(1, 2, 0, 3).reshape(small, fan * k_rows)
    block = jnp.concatenate([tall, flat], 0)
    pieces, far, ready = ring(
        block, fan * k_rows, "z", prepare_parameters,
        (
            d_skip, norm_gain, steer, dt_bias, decay_rate, z.astype(jnp.int32),
            initial_state.reshape(channels, N),
            (lax.axis_index(("yl", "z", "x")) * (channels // SHARES)).astype(jnp.int32),
        ),
    )
    channel_rows, head_columns, where, start = ready

    own = lax.all_to_all(copies, ("yh", "yl"), 0, 0).reshape(
        SIZES["yh"], 2, local + HALO, width
    )
    own = lax.optimization_barrier((own, pieces[5]))[0]
    other = lax.ppermute(own, "c", [(0, 1), (1, 0)])

    bc_pre, dt_raw = narrow_project(where, own, other, pieces[:-1] + [far], bc_rows, heads, 2 * tp_count)
    pieces[-1] = lax.optimization_barrier((pieces[-1], bc_pre))[0]
    x_conv, cumulative, step_size, scaled = project(
        where, dt_raw, conv_x, head_columns, own, other, pieces
    )
    bc_all = lax.all_to_all(bc_pre, ("yh", "c", "yl"), 0, 0).reshape(2 * N, -1)

    pair = 2 * local
    plane = SIZES["z"] * SIZES["x"]
    share = half // plane
    bc_conv, payload, locals_ = call(
        state_kernel,
        [
            jax.ShapeDtypeStruct((pair, 2 * N), bf16),
            jax.ShapeDtypeStruct((plane, share + 8, N), bf16),
            jax.ShapeDtypeStruct((pair // GROUP, half, N), f32),
        ],
        mine, bc_all, conv_bc, cumulative, scaled,
        grant=ALL_VMEM,
    )
    states = lax.all_to_all(payload, ("z", "x"), 0, 0)
    (prefixes,) = call(
        prefix_kernel,
        [jax.ShapeDtypeStruct((plane, share, N), bf16)],
        mine, states, start,
    )
    entering = lax.all_to_all(prefixes, ("z", "x"), 0, 0).reshape(half, N)

    lanes = ((8, half), lambda i, s: (0, s[0]))
    inside, growth = call(
        inside_kernel,
        [jax.ShapeDtypeStruct((pair, half), f32), jax.ShapeDtypeStruct((pair, half), f32)],
        mine, x_conv, bc_conv, cumulative, step_size, locals_, channel_rows,
        blocks={5: lanes},
        flops=10**9, bytes_accessed=12 * pair * half,
    )
    keep, send, dots = call(
        output_kernel,
        [
            jax.ShapeDtypeStruct((local, half), f32),
            jax.ShapeDtypeStruct((local, half), bf16),
            jax.ShapeDtypeStruct((2, 1, local), f32),
        ],
        mine, inside, growth, bc_conv, entering, channel_rows,
        blocks={4: lanes},
    )
    shape = (SIZES["yh"], 2, SIZES["c"], 1, local)
    partials = lax.all_to_all(
        jnp.broadcast_to(dots[None, :, None], shape).reshape(2 * tp_count, 1, local),
        ("yh", "yl", "c"), 0, 0,
    )
    swapped = lax.ppermute(send, "yl", [(0, 1), (1, 0)])
    factor = 1.0 / math.sqrt(channels * tp_count)
    (out,) = call(
        functools.partial(steer_kernel, factor),
        [jax.ShapeDtypeStruct((local, channels), bf16)],
        mine, keep, swapped, partials.reshape(2 * tp_count, local),
        channel_rows,
    )
    return out


def solution(mesh):
    fine = Mesh(mesh.devices.reshape(tuple(SIZES.values())), tuple(SIZES))
    both = P(SEQ, TP)
    placed = (
        both, both, both, both, P(None, TP), P(), P(TP), P(TP), P(TP), P(TP),
        P(TP, None, None), P(TP),
    )
    return jax.shard_map(
        per_device, mesh=fine, in_specs=placed, out_specs=both, check_vma=False
    )
```

```python
import functools
import math

import jax
import jax.numpy as jnp
from jax import lax
from jax.experimental import pallas as pl
from jax.experimental.pallas import tpu as pltpu
from jax.sharding import Mesh, PartitionSpec as P

EPSILON = 1e-05
GROUP = 128
N = 128
HALO = 16
HEAD = 64
ALL_VMEM = 67043328
HIGHEST = lax.Precision.HIGHEST

SEQ = ("z", "x", "yl")
TP = ("yh", "c")
SHARES = 64
OFFSETS = (0, -1, 1, -2, 2, -3, 3, 4)
SIZES = {"z": 8, "x": 4, "yl": 2, "yh": 4, "c": 2}


def call(
    kernel, outs, scalars, *args, blocks=None, scratch=(), flops=0, bytes_accessed=0,
    grant=20 * 1024 * 1024,
):
    blocks = blocks or {}
    specs = [
        pl.BlockSpec(*blocks[at])
        if at in blocks
        else pl.BlockSpec(arg.shape, functools.partial(lambda rank, i, s: (0,) * rank, arg.ndim))
        for at, arg in enumerate(args)
    ]
    whole = [
        pl.BlockSpec(out.shape, functools.partial(lambda rank, i, s: (0,) * rank, len(out.shape)))
        for out in outs
    ]
    return pl.pallas_call(
        kernel,
        grid_spec=pltpu.PrefetchScalarGridSpec(
            num_scalar_prefetch=1,
            grid=(1,),
            in_specs=specs,
            out_specs=whole,
            scratch_shapes=list(scratch),
        ),
        out_shape=outs,
        compiler_params=pltpu.CompilerParams(vmem_limit_bytes=grant),
        cost_estimate=pl.CostEstimate(
            flops=flops, bytes_accessed=bytes_accessed, transcendentals=0
        ),
    )(scalars, *args)


def dot(a, b, dims, precision=None):
    return lax.dot_general(
        a, b, (dims, ((), ())), precision=precision, preferred_element_type=jnp.float32
    )


def parts(value):
    high = value.astype(jnp.bfloat16)
    rest = value - high.astype(jnp.float32)
    middle = rest.astype(jnp.bfloat16)
    low = (rest - middle.astype(jnp.float32)).astype(jnp.bfloat16)
    return high, middle, low


def left_dot(value, exact, dims):
    return sum(dot(part, exact, dims) for part in parts(value))


def right_dot(exact, value, dims):
    return sum(dot(exact, part, dims) for part in parts(value))


def expander(heads, channels):
    row = lax.broadcasted_iota(jnp.int32, (heads, channels), 0)
    column = lax.broadcasted_iota(jnp.int32, (heads, channels), 1)
    return jnp.where(column // (channels // heads) == row, 1.0, 0.0).astype(jnp.bfloat16)


def fetch_tokens(where_ref, own_ref, other_ref, feats, sem):
    for step in range(feats.shape[0]):
        line, mine = where_ref[step], where_ref[feats.shape[0] + step] == 1

        @pl.when(mine)
        def _():
            pltpu.make_async_copy(own_ref.at[line], feats.at[step], sem.at[step]).start()

        @pl.when(jnp.logical_not(mine))
        def _():
            pltpu.make_async_copy(other_ref.at[line], feats.at[step], sem.at[step]).start()


def token_kernel(earlier_ref, tokens_ref, out_ref):
    for at in range(out_ref.shape[0]):
        out_ref[at, 0:HALO] = earlier_ref[...]
        out_ref[at, HALO:] = tokens_ref[...]


def narrow_kernel(
    where_ref, own_ref, other_ref, w0, w1, w2, w3, w4, w5, w6, w7,
    bc_ref, dt_ref, feats, weights, small, sem, weight_sem,
):
    bc_rows, dt_rows = bc_ref.shape[1], dt_ref.shape[0]
    flat = bc_rows + dt_rows
    rows = feats.shape[2]
    tokens = rows - HALO
    blocks = feats.shape[0]
    fetch_tokens(where_ref, own_ref, other_ref, feats, sem)
    copies = []
    for at, ref in enumerate((w0, w1, w2, w3, w4, w5, w6, w7)):
        tall = ref.shape[0] - flat
        copies.append(
            pltpu.make_async_copy(
                ref.at[tall : tall + flat], weights.at[at], weight_sem.at[at]
            )
        )
        copies[at].start()
    small[...] = jnp.zeros_like(small)
    for step in range(blocks):
        pltpu.make_async_copy(own_ref.at[0], feats.at[step], sem.at[step]).wait()
        copies[step].wait()
        for part in range(2):
            small[part * rows : (part + 1) * rows, 0:flat] += dot(
                feats[step, part], weights[step], ((1,), (1,))
            )
    turned = small[...].T[0:bc_rows, 0 : 2 * rows].astype(jnp.bfloat16)
    for at in range(bc_ref.shape[0]):
        bc_ref[at] = turned
    for part in range(2):
        turned = small[part * rows + HALO : (part + 1) * rows].T
        dt_ref[:, part * tokens : (part + 1) * tokens] = turned[bc_rows:flat]


def project_kernel(
    where_ref, dt_ref, conv_ref, head_ref, own_ref, other_ref, w0, w1, w2, w3, w4, w5, w6, w7,
    x_ref, cum_ref, step_ref, scaled_ref, feats, weights, acc, pre, sem, weight_sem,
):
    blocks, depth = weights.shape[0], weights.shape[1]
    fetch_tokens(where_ref, own_ref, other_ref, feats, sem)
    copies = [
        pltpu.make_async_copy(ref.at[0:depth], weights.at[at], weight_sem.at[at])
        for at, ref in enumerate((w0, w1, w2, w3, w4, w5, w6, w7))
    ]
    for copy in copies:
        copy.start()
    for step in range(blocks):
        pltpu.make_async_copy(own_ref.at[0], feats.at[step], sem.at[step]).wait()
        copies[step].wait()
        for part in range(2):
            found = dot(feats[step, part], weights[step], ((1,), (0,)))
            if step == 0:
                acc[part] = found
            elif step < blocks - 1:
                acc[part] += found
            else:
                pre[part] = (acc[part] + found).astype(jnp.bfloat16)
    mine = where_ref[2 * blocks]
    heads, channels = dt_ref.shape[0], x_ref.shape[1]
    convolve_block(
        pre, dt_ref,
        conv_ref.at[:, pl.ds(pl.multiple_of(mine * channels, channels), channels)],
        head_ref.at[pl.ds(pl.multiple_of(mine * heads, heads), heads)],
        x_ref, cum_ref, step_ref, scaled_ref,
    )


def narrow_project(where, own, other, weights, bc_rows, dt_rows, copies):
    _, _, rows, depth = own.shape
    blocks = len(weights)
    flat = bc_rows + dt_rows
    return pl.pallas_call(
        narrow_kernel,
        in_specs=[pl.BlockSpec(memory_space=pltpu.SMEM)]
        + [pl.BlockSpec(memory_space=pl.ANY)] * (blocks + 2),
        out_specs=[pl.BlockSpec(memory_space=pltpu.VMEM)] * 2,
        scratch_shapes=[
            pltpu.VMEM((blocks, 2, rows, depth), jnp.bfloat16),
            pltpu.VMEM((blocks, flat, depth), jnp.bfloat16),
            pltpu.VMEM(((2 * rows + 127) // 128 * 128, 128), jnp.float32),
            pltpu.SemaphoreType.DMA((blocks,)),
            pltpu.SemaphoreType.DMA((blocks,)),
        ],
        out_shape=[
            jax.ShapeDtypeStruct((copies, bc_rows, 2 * rows), jnp.bfloat16),
            jax.ShapeDtypeStruct((dt_rows, 2 * (rows - HALO)), jnp.float32),
        ],
        compiler_params=pltpu.CompilerParams(vmem_limit_bytes=ALL_VMEM),
        cost_estimate=pl.CostEstimate(flops=10**9, bytes_accessed=10**7, transcendentals=0),
    )(where, own, other, *weights)


def project(where, dt_raw, conv_x, head_columns, own, other, weights):
    _, _, rows, depth = own.shape
    channels = weights[0].shape[1]
    blocks = len(weights)
    heads, tokens = dt_raw.shape
    vmem = pl.BlockSpec(memory_space=pltpu.VMEM)
    return pl.pallas_call(
        project_kernel,
        in_specs=[pl.BlockSpec(memory_space=pltpu.SMEM), vmem, vmem, vmem]
        + [pl.BlockSpec(memory_space=pl.ANY)] * (len(weights) + 2),
        out_specs=[vmem] * 4,
        scratch_shapes=[
            pltpu.VMEM((blocks, 2, rows, depth), jnp.bfloat16),
            pltpu.VMEM((blocks, depth, channels), jnp.bfloat16),
            pltpu.VMEM((2, rows, channels), jnp.float32),
            pltpu.VMEM((2, rows, channels), jnp.bfloat16),
            pltpu.SemaphoreType.DMA((blocks,)),
            pltpu.SemaphoreType.DMA((blocks,)),
        ],
        out_shape=[
            jax.ShapeDtypeStruct((tokens, channels), jnp.bfloat16),
            jax.ShapeDtypeStruct((heads, tokens), jnp.float32),
            jax.ShapeDtypeStruct((heads, tokens), jnp.float32),
            jax.ShapeDtypeStruct((channels, tokens), jnp.bfloat16),
        ],
        compiler_params=pltpu.CompilerParams(vmem_limit_bytes=ALL_VMEM),
        cost_estimate=pl.CostEstimate(
            flops=3 * 10**9, bytes_accessed=10**7, transcendentals=0
        ),
    )(where, dt_raw, conv_x, head_columns, own, other, *weights)


def convolved(values, taps, tokens):
    summed = taps[0:1] * values[HALO - 3 : HALO - 3 + tokens]
    for k in range(1, 4):
        summed = summed + taps[k : k + 1] * values[HALO - 3 + k : HALO - 3 + k + tokens]
    return (summed / (1.0 + jnp.exp(-summed))).astype(jnp.bfloat16)


def convolve_block(pre_ref, dt_ref, conv_ref, head_ref, x_ref, cum_ref, step_ref, scaled_ref):
    tokens, channels = x_ref.shape
    halves, rows, _ = pre_ref.shape
    local = tokens // halves
    heads = dt_ref.shape[0]
    for part in range(halves):
        at = slice(part * local, (part + 1) * local)
        for lane in range(0, channels, 128):
            on = slice(lane, lane + 128)
            values = pre_ref[part, :, on].astype(jnp.float32)
            x_ref[at, on] = convolved(values, conv_ref[:, on], local)
    raw = dt_ref[...] + head_ref[:, 0:1]
    step_size = jnp.maximum(raw, 0.0) + jnp.log1p(jnp.exp(-jnp.abs(raw)))
    log_decay = -step_size * head_ref[:, 64:65]
    step_ref[...] = step_size
    upper = jnp.where(
        lax.broadcasted_iota(jnp.int32, (GROUP, GROUP), 0)
        <= lax.broadcasted_iota(jnp.int32, (GROUP, GROUP), 1),
        1.0,
        0.0,
    ).astype(jnp.bfloat16)
    spread = expander(heads, channels)
    for block in range(tokens // GROUP):
        at = slice(block * GROUP, (block + 1) * GROUP)
        cumulative = left_dot(log_decay[:, at], upper, ((1,), (0,)))
        cum_ref[:, at] = cumulative
        to_end = jnp.exp(cumulative[:, GROUP - 1 : GROUP] - cumulative) * step_size[:, at]
        wide = left_dot(to_end.T, spread, ((1,), (0,)))
        scaled = x_ref[at, :].astype(jnp.float32) * wide
        scaled_ref[:, at] = scaled.T.astype(jnp.bfloat16)


def state_kernel(
    mine_ref, bc_ref, conv_ref, cum_ref, scaled_ref, bconv_ref, pay_ref, local_ref
):
    rows = bc_ref.shape[1] // 2
    channels, tokens = scaled_ref.shape
    local = tokens // 2
    heads = cum_ref.shape[0]
    row = lax.broadcasted_iota(jnp.int32, (128, 128), 0)
    column = lax.broadcasted_iota(jnp.int32, (128, 128), 1)
    same = jnp.where(row == column, 1.0, 0.0).astype(jnp.bfloat16)
    for lane in range(0, 2 * N, 128):
        on = slice(lane, lane + 128)
        turned = dot(bc_ref[on], same, ((0,), (0,)))
        for part in range(2):
            at = slice(part * local, (part + 1) * local)
            values = turned[part * rows : (part + 1) * rows]
            bconv_ref[at, on] = convolved(values, conv_ref[:, on], local)
    total = jnp.zeros((heads, 1), jnp.float32)
    blocks = tokens // GROUP
    for block in range(blocks):
        at = slice(block * GROUP, (block + 1) * GROUP)
        added = dot(scaled_ref[:, at], bconv_ref[at, 0:N], ((1,), (0,)))
        end = cum_ref[:, (block + 1) * GROUP - 1 : (block + 1) * GROUP]
        total = total + end
        growth = jnp.exp(end)
        for head in range(heads):
            on = slice(head * HEAD, (head + 1) * HEAD)
            if block:
                local_ref[block, on] = (
                    local_ref[block - 1, on] * growth[head : head + 1] + added[on]
                )
            else:
                local_ref[block, on] = added[on]
    total = jnp.exp(total)
    high = total.astype(jnp.bfloat16).astype(jnp.float32)
    low = total - high
    share = pay_ref.shape[0] // heads
    tail_rows = pay_ref.shape[1] - 16
    row = lax.broadcasted_iota(jnp.int32, (tail_rows, N), 0)
    for head in range(heads):
        tail = jnp.where(
            row == 0, high[head : head + 1], jnp.where(row == 1, low[head : head + 1], 0.0)
        ).astype(jnp.bfloat16)
        for part in range(head * share, (head + 1) * share):
            pay_ref[part, 0:16] = local_ref[blocks - 1, part * 16 : (part + 1) * 16].astype(
                jnp.bfloat16
            )
            pay_ref[part, 16:] = tail


def prefix_kernel(at_ref, got_ref, start_ref, out_ref):
    running = start_ref[...]
    for source in range(got_ref.shape[0]):
        out_ref[source] = running.astype(jnp.bfloat16)
        tail = got_ref[source, 16:].astype(jnp.float32)
        running = (tail[0:1] + tail[1:2]) * running + got_ref[source, 0:16].astype(jnp.float32)


def inside_kernel(
    mine_ref, x_ref, bc_ref, cum_ref, step_ref, local_ref, chan_ref, out_ref, growth_ref
):
    tokens, channels = x_ref.shape
    heads = cum_ref.shape[0]
    spread = expander(heads, channels)
    causal = lax.broadcasted_iota(jnp.int32, (GROUP, GROUP), 0) >= lax.broadcasted_iota(
        jnp.int32, (GROUP, GROUP), 1
    )
    before = jnp.zeros((heads, 1), jnp.float32)
    for block in range(tokens // GROUP):
        at = slice(block * GROUP, (block + 1) * GROUP)
        c_block = bc_ref[at, N:]
        scores = dot(c_block, bc_ref[at, 0:N], ((1,), (1,)))
        cumulative = cum_ref[:, at]
        columns = cumulative.T
        growth_ref[at] = left_dot(jnp.exp(cumulative + before).T, spread, ((1,), (0,)))
        before = before + cumulative[:, GROUP - 1 : GROUP]
        rest = chan_ref[0:1] * x_ref[at].astype(jnp.float32)
        if block:
            carried = right_dot(c_block, local_ref[block - 1], ((1,), (1,)))
            rest = rest + left_dot(jnp.exp(columns), spread, ((1,), (0,))) * carried
        for pair in range(0, heads, 2):
            found = []
            for head in (pair, pair + 1):
                differ = columns[:, head : head + 1] - cumulative[head : head + 1]
                decays = jnp.exp(jnp.where(causal, differ, -1e30))
                mixing = (scores * decays * step_ref[head : head + 1, at]).astype(jnp.bfloat16)
                found.append(
                    dot(mixing, x_ref[at, head * HEAD : (head + 1) * HEAD], ((1,), (0,)))
                )
            on = slice(pair * HEAD, (pair + 2) * HEAD)
            out_ref[at, on] = jnp.concatenate(found, 1) + rest[:, on]


def output_kernel(
    mine_ref, inside_ref, growth_ref, bc_ref, entering_ref, chan_ref, keep_ref, send_ref, dot_ref
):
    mine = mine_ref[0]
    tokens, channels = inside_ref.shape
    local = tokens // 2
    spread = expander(channels // HEAD, channels)
    gain, steer = chan_ref[1:2], chan_ref[2:3]
    for block in range(tokens // GROUP):
        at = slice(block * GROUP, (block + 1) * GROUP)
        carried = dot(bc_ref[at, N:], entering_ref[...], ((1,), (1,)))
        y = inside_ref[at] + growth_ref[at] * carried
        squares = left_dot(y * y, spread, ((1,), (1,))) * (1.0 / HEAD)
        scale = left_dot(lax.rsqrt(squares + EPSILON), spread, ((1,), (0,)))
        normed = y * scale * gain
        part = block * GROUP // local
        on = slice(block * GROUP - part * local, (block + 1) * GROUP - part * local)

        @pl.when(mine == part)
        def _():
            keep_ref[on] = normed

        @pl.when(mine != part)
        def _():
            send_ref[on] = normed.astype(jnp.bfloat16)

        terms = normed * steer
        folded = terms[:, 0:128]
        for lane in range(128, channels, 128):
            folded = folded + terms[:, lane : lane + 128]
        dot_ref[part, :, on] = jnp.sum(folded.T, axis=0, keepdims=True)


def steer_kernel(factor, mine_ref, keep_ref, other_ref, dots_ref, chan_ref, out_ref):
    first = mine_ref[0] == 0
    half = keep_ref.shape[1]
    dots = dots_ref[...]
    for lane in range(0, half, 256):
        at = slice(lane, lane + 256)
        later = slice(half + lane, half + lane + 256)
        own, other = keep_ref[:, at], other_ref[:, at].astype(jnp.float32)
        left, right = jnp.where(first, own, other), jnp.where(first, other, own)
        for on, normed in ((at, left), (later, right)):
            steer = jnp.broadcast_to(chan_ref[2:3, on], (dots.shape[0], 256))
            penalty = dot(dots, steer, ((0,), (0,)), HIGHEST)
            out_ref[:, on] = (normed - penalty * factor).astype(jnp.bfloat16)


def prepare_parameters(d_skip, norm_gain, steer, dt_bias, decay_rate, z, start, at):
    channel_rows = jnp.concatenate(
        [
            jnp.repeat(d_skip, HEAD)[None], norm_gain[None], steer[None],
            jnp.zeros((5, steer.shape[0]), jnp.float32),
        ],
        0,
    )
    wide = (dt_bias.shape[0], 64)
    head_columns = jnp.concatenate(
        [jnp.broadcast_to(dt_bias[:, None], wide), jnp.broadcast_to(decay_rate[:, None], wide)], 1
    )
    source = (z + jnp.array(OFFSETS, jnp.int32)) % SIZES["z"]
    where = jnp.concatenate(
        [
            source // 2, (source % 2 == lax.axis_index("c")).astype(jnp.int32),
            lax.axis_index("yl").astype(jnp.int32).reshape(1),
        ]
    )
    start = lax.dynamic_slice_in_dim(start, at, start.shape[0] // SHARES, 0)
    return channel_rows, head_columns, where, start


def ring(block, depth, axis, prepare, raw):
    count = SIZES[axis]
    forward = [(i, (i + 1) % count) for i in range(count)]
    backward = [(i, (i - 1) % count) for i in range(count)]
    across = [(i, (i + count // 2) % count) for i in range(count)]
    pieces = [block]
    ahead = behind = block
    for hop in range(1, count // 2):
        ahead = lax.ppermute(ahead, axis, forward)
        behind = lax.ppermute(behind, axis, backward)
        if hop == 1:
            far = lax.ppermute(block[depth:], axis, across)
            ready = prepare(*lax.optimization_barrier((raw, far))[0])
            ahead, behind, far = lax.optimization_barrier((ahead, behind, far))
        elif hop == 2:
            ahead, behind, ready = lax.optimization_barrier((ahead, behind, ready))
        else:
            ahead, behind = lax.optimization_barrier((ahead, behind))
        pieces += [ahead, behind]
    pieces.append(lax.ppermute(ahead, axis, forward))
    return pieces, far, ready


def per_device(
    tokens, x_weight, bc_weight, dt_weight, conv_x, conv_bc, dt_bias, decay_rate, d_skip,
    norm_gain, initial_state, steer,
):
    local, width = tokens.shape
    k_rows, channels = x_weight.shape
    half = channels // 2
    heads = dt_weight.shape[1] // 2
    bc_rows = bc_weight.shape[1] // 2
    small = bc_rows + heads
    seq_count = SIZES["z"] * SIZES["x"] * SIZES["yl"]
    tp_count = SIZES["yh"] * SIZES["c"]
    z = lax.axis_index("z")
    mine = lax.axis_index("yl").astype(jnp.int32).reshape(1)
    f32, bf16 = jnp.float32, jnp.bfloat16

    earlier = lax.ppermute(
        tokens[local - HALO :], SEQ, [(i, i + 1) for i in range(seq_count - 1)]
    )
    line = SIZES["yh"] * 2
    copies = pl.pallas_call(
        token_kernel,
        out_shape=jax.ShapeDtypeStruct((line, local + HALO, width), bf16),
        compiler_params=pltpu.CompilerParams(vmem_limit_bytes=8388608),
        cost_estimate=pl.CostEstimate(
            flops=0, bytes_accessed=3 * line * local * width, transcendentals=0
        ),
    )(earlier, tokens)

    fan = SIZES["x"] * SIZES["yl"]
    packed_rows = small * k_rows // half
    packed = jnp.concatenate(
        [
            bc_weight.reshape(k_rows, 2, bc_rows).transpose(1, 2, 0),
            dt_weight.reshape(k_rows, 2, heads).transpose(1, 2, 0),
        ],
        1,
    ).reshape(2, packed_rows, half)
    panel = jnp.concatenate(
        [
            jnp.stack([x_weight[:, :half], x_weight[:, half:]]),
            packed,
            jnp.zeros((2, -packed_rows % 8, half), bf16),
        ],
        1,
    )
    panel = jnp.broadcast_to(panel[None], (SIZES["x"],) + panel.shape).reshape(
        fan, panel.shape[1], half
    )
    got = lax.all_to_all(panel, ("x", "yl"), 0, 0)
    copies, got = lax.optimization_barrier((copies, got))
    tall = got[:, :k_rows].reshape(fan * k_rows, half)
    flat = got[:, k_rows : k_rows + packed_rows].reshape(
        fan, packed_rows, half // k_rows, k_rows
    )
    flat = flat.transpose(1, 2, 0, 3).reshape(small, fan * k_rows)
    block = jnp.concatenate([tall, flat], 0)
    pieces, far, ready = ring(
        block, fan * k_rows, "z", prepare_parameters,
        (
            d_skip, norm_gain, steer, dt_bias, decay_rate, z.astype(jnp.int32),
            initial_state.reshape(channels, N),
            (lax.axis_index(("yl", "z", "x")) * (channels // SHARES)).astype(jnp.int32),
        ),
    )
    channel_rows, head_columns, where, start = ready

    own = lax.all_to_all(copies, ("yh", "yl"), 0, 0).reshape(
        SIZES["yh"], 2, local + HALO, width
    )
    own = lax.optimization_barrier((own, pieces[5]))[0]
    other = lax.ppermute(own, "c", [(0, 1), (1, 0)])

    bc_pre, dt_raw = narrow_project(where, own, other, pieces[:-1] + [far], bc_rows, heads, 2 * tp_count)
    pieces[-1] = lax.optimization_barrier((pieces[-1], bc_pre))[0]
    x_conv, cumulative, step_size, scaled = project(
        where, dt_raw, conv_x, head_columns, own, other, pieces
    )
    bc_all = lax.all_to_all(bc_pre, ("yh", "c", "yl"), 0, 0).reshape(2 * N, -1)

    pair = 2 * local
    plane = SIZES["z"] * SIZES["x"]
    share = half // plane
    bc_conv, payload, locals_ = call(
        state_kernel,
        [
            jax.ShapeDtypeStruct((pair, 2 * N), bf16),
            jax.ShapeDtypeStruct((plane, share + 8, N), bf16),
            jax.ShapeDtypeStruct((pair // GROUP, half, N), f32),
        ],
        mine, bc_all, conv_bc, cumulative, scaled,
        grant=ALL_VMEM,
    )
    states = lax.all_to_all(payload, ("z", "x"), 0, 0)
    (prefixes,) = call(
        prefix_kernel,
        [jax.ShapeDtypeStruct((plane, share, N), bf16)],
        mine, states, start,
    )
    entering = lax.all_to_all(prefixes, ("z", "x"), 0, 0).reshape(half, N)

    lanes = ((8, half), lambda i, s: (0, s[0]))
    inside, growth = call(
        inside_kernel,
        [jax.ShapeDtypeStruct((pair, half), f32), jax.ShapeDtypeStruct((pair, half), f32)],
        mine, x_conv, bc_conv, cumulative, step_size, locals_, channel_rows,
        blocks={5: lanes},
        flops=10**9, bytes_accessed=12 * pair * half,
    )
    keep, send, dots = call(
        output_kernel,
        [
            jax.ShapeDtypeStruct((local, half), f32),
            jax.ShapeDtypeStruct((local, half), bf16),
            jax.ShapeDtypeStruct((2, 1, local), f32),
        ],
        mine, inside, growth, bc_conv, entering, channel_rows,
        blocks={4: lanes},
    )
    shape = (SIZES["yh"], 2, SIZES["c"], 1, local)
    partials = lax.all_to_all(
        jnp.broadcast_to(dots[None, :, None], shape).reshape(2 * tp_count, 1, local),
        ("yh", "yl", "c"), 0, 0,
    )
    swapped = lax.ppermute(send, "yl", [(0, 1), (1, 0)])
    factor = 1.0 / math.sqrt(channels * tp_count)
    (out,) = call(
        functools.partial(steer_kernel, factor),
        [jax.ShapeDtypeStruct((local, channels), bf16)],
        mine, keep, swapped, partials.reshape(2 * tp_count, local),
        channel_rows,
    )
    return out


def solution(mesh):
    fine = Mesh(mesh.devices.reshape(tuple(SIZES.values())), tuple(SIZES))
    both = P(SEQ, TP)
    placed = (
        both, both, both, both, P(None, TP), P(), P(TP), P(TP), P(TP), P(TP),
        P(TP, None, None), P(TP),
    )
    return jax.shard_map(
        per_device, mesh=fine, in_specs=placed, out_specs=both, check_vma=False
    )
```

```python
import functools
import math

import jax
import jax.numpy as jnp
from jax import lax
from jax.experimental import pallas as pl
from jax.experimental.pallas import tpu as pltpu
from jax.sharding import Mesh, PartitionSpec as P

EPSILON = 1e-05
GROUP = 128
N = 128
HALO = 16
HEAD = 64
ALL_VMEM = 67043328
HIGHEST = lax.Precision.HIGHEST

SEQ = ("z", "x", "yl")
TP = ("yh", "c")
SHARES = 64
OFFSETS = (0, -1, 1, -2, 2, -3, 3, 4)
SIZES = {"z": 8, "x": 4, "yl": 2, "yh": 4, "c": 2}


def call(
    kernel, outs, scalars, *args, blocks=None, scratch=(), flops=0, bytes_accessed=0,
    grant=20 * 1024 * 1024,
):
    blocks = blocks or {}
    specs = [
        pl.BlockSpec(*blocks[at])
        if at in blocks
        else pl.BlockSpec(arg.shape, functools.partial(lambda rank, i, s: (0,) * rank, arg.ndim))
        for at, arg in enumerate(args)
    ]
    whole = [
        pl.BlockSpec(out.shape, functools.partial(lambda rank, i, s: (0,) * rank, len(out.shape)))
        for out in outs
    ]
    return pl.pallas_call(
        kernel,
        grid_spec=pltpu.PrefetchScalarGridSpec(
            num_scalar_prefetch=1,
            grid=(1,),
            in_specs=specs,
            out_specs=whole,
            scratch_shapes=list(scratch),
        ),
        out_shape=outs,
        compiler_params=pltpu.CompilerParams(vmem_limit_bytes=grant),
        cost_estimate=pl.CostEstimate(
            flops=flops, bytes_accessed=bytes_accessed, transcendentals=0
        ),
    )(scalars, *args)


def dot(a, b, dims, precision=None):
    return lax.dot_general(
        a, b, (dims, ((), ())), precision=precision, preferred_element_type=jnp.float32
    )


def parts(value):
    high = value.astype(jnp.bfloat16)
    rest = value - high.astype(jnp.float32)
    middle = rest.astype(jnp.bfloat16)
    low = (rest - middle.astype(jnp.float32)).astype(jnp.bfloat16)
    return high, middle, low


def left_dot(value, exact, dims):
    return sum(dot(part, exact, dims) for part in parts(value))


def right_dot(exact, value, dims):
    return sum(dot(exact, part, dims) for part in parts(value))


def expander(heads, channels):
    row = lax.broadcasted_iota(jnp.int32, (heads, channels), 0)
    column = lax.broadcasted_iota(jnp.int32, (heads, channels), 1)
    return jnp.where(column // (channels // heads) == row, 1.0, 0.0).astype(jnp.bfloat16)


def fetch_tokens(where_ref, own_ref, other_ref, feats, sem):
    for step in range(feats.shape[0]):
        line, mine = where_ref[step], where_ref[feats.shape[0] + step] == 1

        @pl.when(mine)
        def _():
            pltpu.make_async_copy(own_ref.at[line], feats.at[step], sem.at[step]).start()

        @pl.when(jnp.logical_not(mine))
        def _():
            pltpu.make_async_copy(other_ref.at[line], feats.at[step], sem.at[step]).start()


def token_kernel(earlier_ref, tokens_ref, out_ref):
    for at in range(out_ref.shape[0]):
        out_ref[at, 0:HALO] = earlier_ref[...]
        out_ref[at, HALO:] = tokens_ref[...]


def narrow_kernel(
    where_ref, own_ref, other_ref, w0, w1, w2, w3, w4, w5, w6, w7,
    bc_ref, dt_ref, feats, weights, small, sem, weight_sem,
):
    bc_rows, dt_rows = bc_ref.shape[1], dt_ref.shape[0]
    flat = bc_rows + dt_rows
    rows = feats.shape[2]
    tokens = rows - HALO
    blocks = feats.shape[0]
    fetch_tokens(where_ref, own_ref, other_ref, feats, sem)
    copies = []
    for at, ref in enumerate((w0, w1, w2, w3, w4, w5, w6, w7)):
        tall = ref.shape[0] - flat
        copies.append(
            pltpu.make_async_copy(
                ref.at[tall : tall + flat], weights.at[at], weight_sem.at[at]
            )
        )
        copies[at].start()
    small[...] = jnp.zeros_like(small)
    for step in range(blocks):
        pltpu.make_async_copy(own_ref.at[0], feats.at[step], sem.at[step]).wait()
        copies[step].wait()
        for part in range(2):
            small[part * rows : (part + 1) * rows, 0:flat] += dot(
                feats[step, part], weights[step], ((1,), (1,))
            )
    turned = small[...].T[0:bc_rows, 0 : 2 * rows].astype(jnp.bfloat16)
    for at in range(bc_ref.shape[0]):
        bc_ref[at] = turned
    for part in range(2):
        turned = small[part * rows + HALO : (part + 1) * rows].T
        dt_ref[:, part * tokens : (part + 1) * tokens] = turned[bc_rows:flat]


def project_kernel(
    where_ref, dt_ref, conv_ref, head_ref, own_ref, other_ref, w0, w1, w2, w3, w4, w5, w6, w7,
    x_ref, cum_ref, step_ref, scaled_ref, feats, weights, acc, pre, sem, weight_sem,
):
    blocks, depth = weights.shape[0], weights.shape[1]
    fetch_tokens(where_ref, own_ref, other_ref, feats, sem)
    copies = [
        pltpu.make_async_copy(ref.at[0:depth], weights.at[at], weight_sem.at[at])
        for at, ref in enumerate((w0, w1, w2, w3, w4, w5, w6, w7))
    ]
    for copy in copies:
        copy.start()
    for step in range(blocks):
        pltpu.make_async_copy(own_ref.at[0], feats.at[step], sem.at[step]).wait()
        copies[step].wait()
        for part in range(2):
            found = dot(feats[step, part], weights[step], ((1,), (0,)))
            if step == 0:
                acc[part] = found
            elif step < blocks - 1:
                acc[part] += found
            else:
                pre[part] = (acc[part] + found).astype(jnp.bfloat16)
    mine = where_ref[2 * blocks]
    heads, channels = dt_ref.shape[0], x_ref.shape[1]
    convolve_block(
        pre, dt_ref,
        conv_ref.at[:, pl.ds(pl.multiple_of(mine * channels, channels), channels)],
        head_ref.at[pl.ds(pl.multiple_of(mine * heads, heads), heads)],
        x_ref, cum_ref, step_ref, scaled_ref,
    )


def narrow_project(where, own, other, weights, bc_rows, dt_rows, copies):
    _, _, rows, depth = own.shape
    blocks = len(weights)
    flat = bc_rows + dt_rows
    return pl.pallas_call(
        narrow_kernel,
        in_specs=[pl.BlockSpec(memory_space=pltpu.SMEM)]
        + [pl.BlockSpec(memory_space=pl.ANY)] * (blocks + 2),
        out_specs=[pl.BlockSpec(memory_space=pltpu.VMEM)] * 2,
        scratch_shapes=[
            pltpu.VMEM((blocks, 2, rows, depth), jnp.bfloat16),
            pltpu.VMEM((blocks, flat, depth), jnp.bfloat16),
            pltpu.VMEM(((2 * rows + 127) // 128 * 128, 128), jnp.float32),
            pltpu.SemaphoreType.DMA((blocks,)),
            pltpu.SemaphoreType.DMA((blocks,)),
        ],
        out_shape=[
            jax.ShapeDtypeStruct((copies, bc_rows, 2 * rows), jnp.bfloat16),
            jax.ShapeDtypeStruct((dt_rows, 2 * (rows - HALO)), jnp.float32),
        ],
        compiler_params=pltpu.CompilerParams(vmem_limit_bytes=64000000),
        cost_estimate=pl.CostEstimate(flops=10**9, bytes_accessed=10**7, transcendentals=0),
    )(where, own, other, *weights)


def project(where, dt_raw, conv_x, head_columns, own, other, weights):
    _, _, rows, depth = own.shape
    channels = weights[0].shape[1]
    blocks = len(weights)
    heads, tokens = dt_raw.shape
    vmem = pl.BlockSpec(memory_space=pltpu.VMEM)
    return pl.pallas_call(
        project_kernel,
        in_specs=[pl.BlockSpec(memory_space=pltpu.SMEM), vmem, vmem, vmem]
        + [pl.BlockSpec(memory_space=pl.ANY)] * (len(weights) + 2),
        out_specs=[vmem] * 4,
        scratch_shapes=[
            pltpu.VMEM((blocks, 2, rows, depth), jnp.bfloat16),
            pltpu.VMEM((blocks, depth, channels), jnp.bfloat16),
            pltpu.VMEM((2, rows, channels), jnp.float32),
            pltpu.VMEM((2, rows, channels), jnp.bfloat16),
            pltpu.SemaphoreType.DMA((blocks,)),
            pltpu.SemaphoreType.DMA((blocks,)),
        ],
        out_shape=[
            jax.ShapeDtypeStruct((tokens, channels), jnp.bfloat16),
            jax.ShapeDtypeStruct((heads, tokens), jnp.float32),
            jax.ShapeDtypeStruct((heads, tokens), jnp.float32),
            jax.ShapeDtypeStruct((channels, tokens), jnp.bfloat16),
        ],
        compiler_params=pltpu.CompilerParams(vmem_limit_bytes=64000000),
        cost_estimate=pl.CostEstimate(
            flops=3 * 10**9, bytes_accessed=10**7, transcendentals=0
        ),
    )(where, dt_raw, conv_x, head_columns, own, other, *weights)


def convolved(values, taps, tokens):
    summed = taps[0:1] * values[HALO - 3 : HALO - 3 + tokens]
    for k in range(1, 4):
        summed = summed + taps[k : k + 1] * values[HALO - 3 + k : HALO - 3 + k + tokens]
    return (summed / (1.0 + jnp.exp(-summed))).astype(jnp.bfloat16)


def convolve_block(pre_ref, dt_ref, conv_ref, head_ref, x_ref, cum_ref, step_ref, scaled_ref):
    tokens, channels = x_ref.shape
    halves, rows, _ = pre_ref.shape
    local = tokens // halves
    heads = dt_ref.shape[0]
    for part in range(halves):
        at = slice(part * local, (part + 1) * local)
        for lane in range(0, channels, 128):
            on = slice(lane, lane + 128)
            values = pre_ref[part, :, on].astype(jnp.float32)
            x_ref[at, on] = convolved(values, conv_ref[:, on], local)
    raw = dt_ref[...] + head_ref[:, 0:1]
    step_size = jnp.maximum(raw, 0.0) + jnp.log1p(jnp.exp(-jnp.abs(raw)))
    log_decay = -step_size * head_ref[:, 64:65]
    step_ref[...] = step_size
    upper = jnp.where(
        lax.broadcasted_iota(jnp.int32, (GROUP, GROUP), 0)
        <= lax.broadcasted_iota(jnp.int32, (GROUP, GROUP), 1),
        1.0,
        0.0,
    ).astype(jnp.bfloat16)
    spread = expander(heads, channels)
    for block in range(tokens // GROUP):
        at = slice(block * GROUP, (block + 1) * GROUP)
        cumulative = left_dot(log_decay[:, at], upper, ((1,), (0,)))
        cum_ref[:, at] = cumulative
        to_end = jnp.exp(cumulative[:, GROUP - 1 : GROUP] - cumulative) * step_size[:, at]
        wide = left_dot(to_end.T, spread, ((1,), (0,)))
        scaled = x_ref[at, :].astype(jnp.float32) * wide
        scaled_ref[:, at] = scaled.T.astype(jnp.bfloat16)


def state_kernel(
    mine_ref, bc_ref, conv_ref, cum_ref, scaled_ref, bconv_ref, pay_ref, local_ref
):
    rows = bc_ref.shape[1] // 2
    channels, tokens = scaled_ref.shape
    local = tokens // 2
    heads = cum_ref.shape[0]
    row = lax.broadcasted_iota(jnp.int32, (128, 128), 0)
    column = lax.broadcasted_iota(jnp.int32, (128, 128), 1)
    same = jnp.where(row == column, 1.0, 0.0).astype(jnp.bfloat16)
    for lane in range(0, 2 * N, 128):
        on = slice(lane, lane + 128)
        turned = dot(bc_ref[on], same, ((0,), (0,)))
        for part in range(2):
            at = slice(part * local, (part + 1) * local)
            values = turned[part * rows : (part + 1) * rows]
            bconv_ref[at, on] = convolved(values, conv_ref[:, on], local)
    total = jnp.zeros((heads, 1), jnp.float32)
    blocks = tokens // GROUP
    for block in range(blocks):
        at = slice(block * GROUP, (block + 1) * GROUP)
        added = dot(scaled_ref[:, at], bconv_ref[at, 0:N], ((1,), (0,)))
        end = cum_ref[:, (block + 1) * GROUP - 1 : (block + 1) * GROUP]
        total = total + end
        growth = jnp.exp(end)
        for head in range(heads):
            on = slice(head * HEAD, (head + 1) * HEAD)
            if block:
                local_ref[block, on] = (
                    local_ref[block - 1, on] * growth[head : head + 1] + added[on]
                )
            else:
                local_ref[block, on] = added[on]
    total = jnp.exp(total)
    high = total.astype(jnp.bfloat16).astype(jnp.float32)
    low = total - high
    share = pay_ref.shape[0] // heads
    tail_rows = pay_ref.shape[1] - 16
    row = lax.broadcasted_iota(jnp.int32, (tail_rows, N), 0)
    for head in range(heads):
        tail = jnp.where(
            row == 0, high[head : head + 1], jnp.where(row == 1, low[head : head + 1], 0.0)
        ).astype(jnp.bfloat16)
        for part in range(head * share, (head + 1) * share):
            pay_ref[part, 0:16] = local_ref[blocks - 1, part * 16 : (part + 1) * 16].astype(
                jnp.bfloat16
            )
            pay_ref[part, 16:] = tail


def prefix_kernel(at_ref, got_ref, start_ref, out_ref):
    running = start_ref[...]
    for source in range(got_ref.shape[0]):
        out_ref[source] = running.astype(jnp.bfloat16)
        tail = got_ref[source, 16:].astype(jnp.float32)
        running = (tail[0:1] + tail[1:2]) * running + got_ref[source, 0:16].astype(jnp.float32)


def inside_kernel(
    mine_ref, x_ref, bc_ref, cum_ref, step_ref, local_ref, chan_ref, out_ref, growth_ref
):
    tokens, channels = x_ref.shape
    heads = cum_ref.shape[0]
    spread = expander(heads, channels)
    causal = lax.broadcasted_iota(jnp.int32, (GROUP, GROUP), 0) >= lax.broadcasted_iota(
        jnp.int32, (GROUP, GROUP), 1
    )
    before = jnp.zeros((heads, 1), jnp.float32)
    for block in range(tokens // GROUP):
        at = slice(block * GROUP, (block + 1) * GROUP)
        c_block = bc_ref[at, N:]
        scores = dot(c_block, bc_ref[at, 0:N], ((1,), (1,)))
        cumulative = cum_ref[:, at]
        columns = cumulative.T
        growth_ref[at] = left_dot(jnp.exp(cumulative + before).T, spread, ((1,), (0,)))
        before = before + cumulative[:, GROUP - 1 : GROUP]
        rest = chan_ref[0:1] * x_ref[at].astype(jnp.float32)
        if block:
            carried = right_dot(c_block, local_ref[block - 1], ((1,), (1,)))
            rest = rest + left_dot(jnp.exp(columns), spread, ((1,), (0,))) * carried
        for pair in range(0, heads, 2):
            found = []
            for head in (pair, pair + 1):
                differ = columns[:, head : head + 1] - cumulative[head : head + 1]
                decays = jnp.exp(jnp.where(causal, differ, -1e30))
                mixing = (scores * decays * step_ref[head : head + 1, at]).astype(jnp.bfloat16)
                found.append(
                    dot(mixing, x_ref[at, head * HEAD : (head + 1) * HEAD], ((1,), (0,)))
                )
            on = slice(pair * HEAD, (pair + 2) * HEAD)
            out_ref[at, on] = jnp.concatenate(found, 1) + rest[:, on]


def output_kernel(
    mine_ref, inside_ref, growth_ref, bc_ref, entering_ref, chan_ref, keep_ref, send_ref, dot_ref
):
    mine = mine_ref[0]
    tokens, channels = inside_ref.shape
    local = tokens // 2
    spread = expander(channels // HEAD, channels)
    gain, steer = chan_ref[1:2], chan_ref[2:3]
    for block in range(tokens // GROUP):
        at = slice(block * GROUP, (block + 1) * GROUP)
        carried = dot(bc_ref[at, N:], entering_ref[...], ((1,), (1,)))
        y = inside_ref[at] + growth_ref[at] * carried
        squares = left_dot(y * y, spread, ((1,), (1,))) * (1.0 / HEAD)
        scale = left_dot(lax.rsqrt(squares + EPSILON), spread, ((1,), (0,)))
        normed = y * scale * gain
        part = block * GROUP // local
        on = slice(block * GROUP - part * local, (block + 1) * GROUP - part * local)

        @pl.when(mine == part)
        def _():
            keep_ref[on] = normed

        @pl.when(mine != part)
        def _():
            send_ref[on] = normed.astype(jnp.bfloat16)

        terms = normed * steer
        folded = terms[:, 0:128]
        for lane in range(128, channels, 128):
            folded = folded + terms[:, lane : lane + 128]
        dot_ref[part, :, on] = jnp.sum(folded.T, axis=0, keepdims=True)


def steer_kernel(factor, mine_ref, keep_ref, other_ref, dots_ref, chan_ref, out_ref):
    first = mine_ref[0] == 0
    half = keep_ref.shape[1]
    dots = dots_ref[...]
    for lane in range(0, half, 256):
        at = slice(lane, lane + 256)
        later = slice(half + lane, half + lane + 256)
        own, other = keep_ref[:, at], other_ref[:, at].astype(jnp.float32)
        left, right = jnp.where(first, own, other), jnp.where(first, other, own)
        for on, normed in ((at, left), (later, right)):
            steer = jnp.broadcast_to(chan_ref[2:3, on], (dots.shape[0], 256))
            penalty = dot(dots, steer, ((0,), (0,)), HIGHEST)
            out_ref[:, on] = (normed - penalty * factor).astype(jnp.bfloat16)


def prepare_parameters(d_skip, norm_gain, steer, dt_bias, decay_rate, z, start, at):
    channel_rows = jnp.concatenate(
        [
            jnp.repeat(d_skip, HEAD)[None], norm_gain[None], steer[None],
            jnp.zeros((5, steer.shape[0]), jnp.float32),
        ],
        0,
    )
    wide = (dt_bias.shape[0], 64)
    head_columns = jnp.concatenate(
        [jnp.broadcast_to(dt_bias[:, None], wide), jnp.broadcast_to(decay_rate[:, None], wide)], 1
    )
    source = (z + jnp.array(OFFSETS, jnp.int32)) % SIZES["z"]
    where = jnp.concatenate(
        [
            source // 2, (source % 2 == lax.axis_index("c")).astype(jnp.int32),
            lax.axis_index("yl").astype(jnp.int32).reshape(1),
        ]
    )
    start = lax.dynamic_slice_in_dim(start, at, start.shape[0] // SHARES, 0)
    return channel_rows, head_columns, where, start


def ring(block, depth, axis, prepare, raw):
    count = SIZES[axis]
    forward = [(i, (i + 1) % count) for i in range(count)]
    backward = [(i, (i - 1) % count) for i in range(count)]
    across = [(i, (i + count // 2) % count) for i in range(count)]
    pieces = [block]
    ahead = behind = block
    for hop in range(1, count // 2):
        ahead = lax.ppermute(ahead, axis, forward)
        behind = lax.ppermute(behind, axis, backward)
        if hop == 1:
            far = lax.ppermute(block[depth:], axis, across)
            ready = prepare(*lax.optimization_barrier((raw, far))[0])
            ahead, behind, far = lax.optimization_barrier((ahead, behind, far))
        elif hop == 2:
            ahead, behind, ready = lax.optimization_barrier((ahead, behind, ready))
        else:
            ahead, behind = lax.optimization_barrier((ahead, behind))
        pieces += [ahead, behind]
    pieces.append(lax.ppermute(ahead, axis, forward))
    return pieces, far, ready


def per_device(
    tokens, x_weight, bc_weight, dt_weight, conv_x, conv_bc, dt_bias, decay_rate, d_skip,
    norm_gain, initial_state, steer,
):
    local, width = tokens.shape
    k_rows, channels = x_weight.shape
    half = channels // 2
    heads = dt_weight.shape[1] // 2
    bc_rows = bc_weight.shape[1] // 2
    small = bc_rows + heads
    seq_count = SIZES["z"] * SIZES["x"] * SIZES["yl"]
    tp_count = SIZES["yh"] * SIZES["c"]
    z = lax.axis_index("z")
    mine = lax.axis_index("yl").astype(jnp.int32).reshape(1)
    f32, bf16 = jnp.float32, jnp.bfloat16

    earlier = lax.ppermute(
        tokens[local - HALO :], SEQ, [(i, i + 1) for i in range(seq_count - 1)]
    )
    line = SIZES["yh"] * 2
    copies = pl.pallas_call(
        token_kernel,
        out_shape=jax.ShapeDtypeStruct((line, local + HALO, width), bf16),
        compiler_params=pltpu.CompilerParams(vmem_limit_bytes=8388608),
        cost_estimate=pl.CostEstimate(
            flops=0, bytes_accessed=3 * line * local * width, transcendentals=0
        ),
    )(earlier, tokens)

    fan = SIZES["x"] * SIZES["yl"]
    packed_rows = small * k_rows // half
    packed = jnp.concatenate(
        [
            bc_weight.reshape(k_rows, 2, bc_rows).transpose(1, 2, 0),
            dt_weight.reshape(k_rows, 2, heads).transpose(1, 2, 0),
        ],
        1,
    ).reshape(2, packed_rows, half)
    panel = jnp.concatenate(
        [
            jnp.stack([x_weight[:, :half], x_weight[:, half:]]),
            packed,
            jnp.zeros((2, -packed_rows % 8, half), bf16),
        ],
        1,
    )
    panel = jnp.broadcast_to(panel[None], (SIZES["x"],) + panel.shape).reshape(
        fan, panel.shape[1], half
    )
    got = lax.all_to_all(panel, ("x", "yl"), 0, 0)
    copies, got = lax.optimization_barrier((copies, got))
    tall = got[:, :k_rows].reshape(fan * k_rows, half)
    flat = got[:, k_rows : k_rows + packed_rows].reshape(
        fan, packed_rows, half // k_rows, k_rows
    )
    flat = flat.transpose(1, 2, 0, 3).reshape(small, fan * k_rows)
    block = jnp.concatenate([tall, flat], 0)
    pieces, far, ready = ring(
        block, fan * k_rows, "z", prepare_parameters,
        (
            d_skip, norm_gain, steer, dt_bias, decay_rate, z.astype(jnp.int32),
            initial_state.reshape(channels, N),
            (lax.axis_index(("yl", "z", "x")) * (channels // SHARES)).astype(jnp.int32),
        ),
    )
    channel_rows, head_columns, where, start = ready

    own = lax.all_to_all(copies, ("yh", "yl"), 0, 0).reshape(
        SIZES["yh"], 2, local + HALO, width
    )
    own = lax.optimization_barrier((own, pieces[5]))[0]
    other = lax.ppermute(own, "c", [(0, 1), (1, 0)])

    bc_pre, dt_raw = narrow_project(where, own, other, pieces[:-1] + [far], bc_rows, heads, 2 * tp_count)
    pieces[-1] = lax.optimization_barrier((pieces[-1], bc_pre))[0]
    x_conv, cumulative, step_size, scaled = project(
        where, dt_raw, conv_x, head_columns, own, other, pieces
    )
    bc_all = lax.all_to_all(bc_pre, ("yh", "c", "yl"), 0, 0).reshape(2 * N, -1)

    pair = 2 * local
    plane = SIZES["z"] * SIZES["x"]
    share = half // plane
    bc_conv, payload, locals_ = call(
        state_kernel,
        [
            jax.ShapeDtypeStruct((pair, 2 * N), bf16),
            jax.ShapeDtypeStruct((plane, share + 8, N), bf16),
            jax.ShapeDtypeStruct((pair // GROUP, half, N), f32),
        ],
        mine, bc_all, conv_bc, cumulative, scaled,
        grant=ALL_VMEM,
    )
    states = lax.all_to_all(payload, ("z", "x"), 0, 0)
    (prefixes,) = call(
        prefix_kernel,
        [jax.ShapeDtypeStruct((plane, share, N), bf16)],
        mine, states, start,
    )
    entering = lax.all_to_all(prefixes, ("z", "x"), 0, 0).reshape(half, N)

    lanes = ((8, half), lambda i, s: (0, s[0]))
    inside, growth = call(
        inside_kernel,
        [jax.ShapeDtypeStruct((pair, half), f32), jax.ShapeDtypeStruct((pair, half), f32)],
        mine, x_conv, bc_conv, cumulative, step_size, locals_, channel_rows,
        blocks={5: lanes},
        flops=10**9, bytes_accessed=12 * pair * half,
    )
    keep, send, dots = call(
        output_kernel,
        [
            jax.ShapeDtypeStruct((local, half), f32),
            jax.ShapeDtypeStruct((local, half), bf16),
            jax.ShapeDtypeStruct((2, 1, local), f32),
        ],
        mine, inside, growth, bc_conv, entering, channel_rows,
        blocks={4: lanes},
    )
    shape = (SIZES["yh"], 2, SIZES["c"], 1, local)
    partials = lax.all_to_all(
        jnp.broadcast_to(dots[None, :, None], shape).reshape(2 * tp_count, 1, local),
        ("yh", "yl", "c"), 0, 0,
    )
    swapped = lax.ppermute(send, "yl", [(0, 1), (1, 0)])
    factor = 1.0 / math.sqrt(channels * tp_count)
    (out,) = call(
        functools.partial(steer_kernel, factor),
        [jax.ShapeDtypeStruct((local, channels), bf16)],
        mine, keep, swapped, partials.reshape(2 * tp_count, local),
        channel_rows,
    )
    return out


def solution(mesh):
    fine = Mesh(mesh.devices.reshape(tuple(SIZES.values())), tuple(SIZES))
    both = P(SEQ, TP)
    placed = (
        both, both, both, both, P(None, TP), P(), P(TP), P(TP), P(TP), P(TP),
        P(TP, None, None), P(TP),
    )
    return jax.shard_map(
        per_device, mesh=fine, in_specs=placed, out_specs=both, check_vma=False
    )
```

```python
import functools
import math

import jax
import jax.numpy as jnp
from jax import lax
from jax.experimental import pallas as pl
from jax.experimental.pallas import tpu as pltpu
from jax.sharding import Mesh, PartitionSpec as P

EPSILON = 1e-05
GROUP = 128
N = 128
HALO = 16
HEAD = 64
ALL_VMEM = 67043328
HIGHEST = lax.Precision.HIGHEST

SEQ = ("z", "x", "yl")
TP = ("yh", "c")
SHARES = 64
OFFSETS = (0, -1, 1, -2, 2, -3, 3, 4)
SIZES = {"z": 8, "x": 4, "yl": 2, "yh": 4, "c": 2}


def call(
    kernel, outs, scalars, *args, blocks=None, scratch=(), flops=0, bytes_accessed=0,
    grant=20 * 1024 * 1024,
):
    blocks = blocks or {}
    specs = [
        pl.BlockSpec(*blocks[at])
        if at in blocks
        else pl.BlockSpec(arg.shape, functools.partial(lambda rank, i, s: (0,) * rank, arg.ndim))
        for at, arg in enumerate(args)
    ]
    whole = [
        pl.BlockSpec(out.shape, functools.partial(lambda rank, i, s: (0,) * rank, len(out.shape)))
        for out in outs
    ]
    return pl.pallas_call(
        kernel,
        grid_spec=pltpu.PrefetchScalarGridSpec(
            num_scalar_prefetch=1,
            grid=(1,),
            in_specs=specs,
            out_specs=whole,
            scratch_shapes=list(scratch),
        ),
        out_shape=outs,
        compiler_params=pltpu.CompilerParams(vmem_limit_bytes=grant),
        cost_estimate=pl.CostEstimate(
            flops=flops, bytes_accessed=bytes_accessed, transcendentals=0
        ),
    )(scalars, *args)


def dot(a, b, dims, precision=None):
    return lax.dot_general(
        a, b, (dims, ((), ())), precision=precision, preferred_element_type=jnp.float32
    )


def parts(value):
    high = value.astype(jnp.bfloat16)
    rest = value - high.astype(jnp.float32)
    middle = rest.astype(jnp.bfloat16)
    low = (rest - middle.astype(jnp.float32)).astype(jnp.bfloat16)
    return high, middle, low


def left_dot(value, exact, dims):
    return sum(dot(part, exact, dims) for part in parts(value))


def right_dot(exact, value, dims):
    return sum(dot(exact, part, dims) for part in parts(value))


def expander(heads, channels):
    row = lax.broadcasted_iota(jnp.int32, (heads, channels), 0)
    column = lax.broadcasted_iota(jnp.int32, (heads, channels), 1)
    return jnp.where(column // (channels // heads) == row, 1.0, 0.0).astype(jnp.bfloat16)


def fetch_tokens(where_ref, own_ref, other_ref, feats, sem):
    for step in range(feats.shape[0]):
        line, mine = where_ref[step], where_ref[feats.shape[0] + step] == 1

        @pl.when(mine)
        def _():
            pltpu.make_async_copy(own_ref.at[line], feats.at[step], sem.at[step]).start()

        @pl.when(jnp.logical_not(mine))
        def _():
            pltpu.make_async_copy(other_ref.at[line], feats.at[step], sem.at[step]).start()


def token_kernel(earlier_ref, tokens_ref, out_ref):
    for at in range(out_ref.shape[0]):
        out_ref[at, 0:HALO] = earlier_ref[...]
        out_ref[at, HALO:] = tokens_ref[...]


def narrow_kernel(
    where_ref, own_ref, other_ref, w0, w1, w2, w3, w4, w5, w6, w7,
    bc_ref, dt_ref, feats, weights, small, sem, weight_sem,
):
    bc_rows, dt_rows = bc_ref.shape[1], dt_ref.shape[0]
    flat = bc_rows + dt_rows
    rows = feats.shape[2]
    tokens = rows - HALO
    blocks = feats.shape[0]
    fetch_tokens(where_ref, own_ref, other_ref, feats, sem)
    copies = []
    for at, ref in enumerate((w0, w1, w2, w3, w4, w5, w6, w7)):
        tall = ref.shape[0] - flat
        copies.append(
            pltpu.make_async_copy(
                ref.at[tall : tall + flat], weights.at[at], weight_sem.at[at]
            )
        )
        copies[at].start()
    small[...] = jnp.zeros_like(small)
    for step in range(blocks):
        pltpu.make_async_copy(own_ref.at[0], feats.at[step], sem.at[step]).wait()
        copies[step].wait()
        for part in range(2):
            small[part * rows : (part + 1) * rows, 0:flat] += dot(
                feats[step, part], weights[step], ((1,), (1,))
            )
    turned = small[...].T[0:bc_rows, 0 : 2 * rows].astype(jnp.bfloat16)
    for at in range(bc_ref.shape[0]):
        bc_ref[at] = turned
    for part in range(2):
        turned = small[part * rows + HALO : (part + 1) * rows].T
        dt_ref[:, part * tokens : (part + 1) * tokens] = turned[bc_rows:flat]


def project_kernel(
    where_ref, dt_ref, conv_ref, head_ref, own_ref, other_ref, w0, w1, w2, w3, w4, w5, w6, w7,
    x_ref, cum_ref, step_ref, scaled_ref, feats, weights, acc, pre, sem, weight_sem,
):
    blocks, depth = weights.shape[0], weights.shape[1]
    fetch_tokens(where_ref, own_ref, other_ref, feats, sem)
    copies = [
        pltpu.make_async_copy(ref.at[0:depth], weights.at[at], weight_sem.at[at])
        for at, ref in enumerate((w0, w1, w2, w3, w4, w5, w6, w7))
    ]
    for copy in copies:
        copy.start()
    for step in range(blocks):
        pltpu.make_async_copy(own_ref.at[0], feats.at[step], sem.at[step]).wait()
        copies[step].wait()
        for part in range(2):
            found = dot(feats[step, part], weights[step], ((1,), (0,)))
            if step == 0:
                acc[part] = found
            elif step < blocks - 1:
                acc[part] += found
            else:
                pre[part] = (acc[part] + found).astype(jnp.bfloat16)
    mine = where_ref[2 * blocks]
    heads, channels = dt_ref.shape[0], x_ref.shape[1]
    convolve_block(
        pre, dt_ref,
        conv_ref.at[:, pl.ds(pl.multiple_of(mine * channels, channels), channels)],
        head_ref.at[pl.ds(pl.multiple_of(mine * heads, heads), heads)],
        x_ref, cum_ref, step_ref, scaled_ref,
    )


def narrow_project(where, own, other, weights, bc_rows, dt_rows, copies):
    _, _, rows, depth = own.shape
    blocks = len(weights)
    flat = bc_rows + dt_rows
    return pl.pallas_call(
        narrow_kernel,
        in_specs=[pl.BlockSpec(memory_space=pltpu.SMEM)]
        + [pl.BlockSpec(memory_space=pl.ANY)] * (blocks + 2),
        out_specs=[pl.BlockSpec(memory_space=pltpu.VMEM)] * 2,
        scratch_shapes=[
            pltpu.VMEM((blocks, 2, rows, depth), jnp.bfloat16),
            pltpu.VMEM((blocks, flat, depth), jnp.bfloat16),
            pltpu.VMEM(((2 * rows + 127) // 128 * 128, 128), jnp.float32),
            pltpu.SemaphoreType.DMA((blocks,)),
            pltpu.SemaphoreType.DMA((blocks,)),
        ],
        out_shape=[
            jax.ShapeDtypeStruct((copies, bc_rows, 2 * rows), jnp.bfloat16),
            jax.ShapeDtypeStruct((dt_rows, 2 * (rows - HALO)), jnp.float32),
        ],
        compiler_params=pltpu.CompilerParams(vmem_limit_bytes=ALL_VMEM),
        cost_estimate=pl.CostEstimate(flops=10**9, bytes_accessed=10**7, transcendentals=0),
    )(where, own, other, *weights)


def project(where, dt_raw, conv_x, head_columns, own, other, weights):
    _, _, rows, depth = own.shape
    channels = weights[0].shape[1]
    blocks = len(weights)
    heads, tokens = dt_raw.shape
    vmem = pl.BlockSpec(memory_space=pltpu.VMEM)
    return pl.pallas_call(
        project_kernel,
        in_specs=[pl.BlockSpec(memory_space=pltpu.SMEM), vmem, vmem, vmem]
        + [pl.BlockSpec(memory_space=pl.ANY)] * (len(weights) + 2),
        out_specs=[vmem] * 4,
        scratch_shapes=[
            pltpu.VMEM((blocks, 2, rows, depth), jnp.bfloat16),
            pltpu.VMEM((blocks, depth, channels), jnp.bfloat16),
            pltpu.VMEM((2, rows, channels), jnp.float32),
            pltpu.VMEM((2, rows, channels), jnp.bfloat16),
            pltpu.SemaphoreType.DMA((blocks,)),
            pltpu.SemaphoreType.DMA((blocks,)),
        ],
        out_shape=[
            jax.ShapeDtypeStruct((tokens, channels), jnp.bfloat16),
            jax.ShapeDtypeStruct((heads, tokens), jnp.float32),
            jax.ShapeDtypeStruct((heads, tokens), jnp.float32),
            jax.ShapeDtypeStruct((channels, tokens), jnp.bfloat16),
        ],
        compiler_params=pltpu.CompilerParams(vmem_limit_bytes=ALL_VMEM),
        cost_estimate=pl.CostEstimate(
            flops=3 * 10**9, bytes_accessed=10**7, transcendentals=0
        ),
    )(where, dt_raw, conv_x, head_columns, own, other, *weights)


def convolved(values, taps, tokens):
    summed = taps[0:1] * values[HALO - 3 : HALO - 3 + tokens]
    for k in range(1, 4):
        summed = summed + taps[k : k + 1] * values[HALO - 3 + k : HALO - 3 + k + tokens]
    return (summed / (1.0 + jnp.exp(-summed))).astype(jnp.bfloat16)


def convolve_block(pre_ref, dt_ref, conv_ref, head_ref, x_ref, cum_ref, step_ref, scaled_ref):
    tokens, channels = x_ref.shape
    halves, rows, _ = pre_ref.shape
    local = tokens // halves
    heads = dt_ref.shape[0]
    for part in range(halves):
        at = slice(part * local, (part + 1) * local)
        for lane in range(0, channels, 128):
            on = slice(lane, lane + 128)
            values = pre_ref[part, :, on].astype(jnp.float32)
            x_ref[at, on] = convolved(values, conv_ref[:, on], local)
    raw = dt_ref[...] + head_ref[:, 0:1]
    step_size = jnp.maximum(raw, 0.0) + jnp.log1p(jnp.exp(-jnp.abs(raw)))
    log_decay = -step_size * head_ref[:, 64:65]
    step_ref[...] = step_size
    upper = jnp.where(
        lax.broadcasted_iota(jnp.int32, (GROUP, GROUP), 0)
        <= lax.broadcasted_iota(jnp.int32, (GROUP, GROUP), 1),
        1.0,
        0.0,
    ).astype(jnp.bfloat16)
    spread = expander(heads, channels)
    for block in range(tokens // GROUP):
        at = slice(block * GROUP, (block + 1) * GROUP)
        cumulative = left_dot(log_decay[:, at], upper, ((1,), (0,)))
        cum_ref[:, at] = cumulative
        to_end = jnp.exp(cumulative[:, GROUP - 1 : GROUP] - cumulative) * step_size[:, at]
        wide = left_dot(to_end.T, spread, ((1,), (0,)))
        scaled = x_ref[at, :].astype(jnp.float32) * wide
        scaled_ref[:, at] = scaled.T.astype(jnp.bfloat16)


def state_kernel(
    mine_ref, bc_ref, conv_ref, cum_ref, scaled_ref, bconv_ref, pay_ref, local_ref
):
    rows = bc_ref.shape[1] // 2
    channels, tokens = scaled_ref.shape
    local = tokens // 2
    heads = cum_ref.shape[0]
    row = lax.broadcasted_iota(jnp.int32, (128, 128), 0)
    column = lax.broadcasted_iota(jnp.int32, (128, 128), 1)
    same = jnp.where(row == column, 1.0, 0.0).astype(jnp.bfloat16)
    for lane in range(0, 2 * N, 128):
        on = slice(lane, lane + 128)
        turned = dot(bc_ref[on], same, ((0,), (0,)))
        for part in range(2):
            at = slice(part * local, (part + 1) * local)
            values = turned[part * rows : (part + 1) * rows]
            bconv_ref[at, on] = convolved(values, conv_ref[:, on], local)
    total = jnp.zeros((heads, 1), jnp.float32)
    blocks = tokens // GROUP
    for block in range(blocks):
        at = slice(block * GROUP, (block + 1) * GROUP)
        added = dot(scaled_ref[:, at], bconv_ref[at, 0:N], ((1,), (0,)))
        end = cum_ref[:, (block + 1) * GROUP - 1 : (block + 1) * GROUP]
        total = total + end
        growth = jnp.exp(end)
        for head in range(heads):
            on = slice(head * HEAD, (head + 1) * HEAD)
            if block:
                local_ref[block, on] = (
                    local_ref[block - 1, on] * growth[head : head + 1] + added[on]
                )
            else:
                local_ref[block, on] = added[on]
    total = jnp.exp(total)
    high = total.astype(jnp.bfloat16).astype(jnp.float32)
    low = total - high
    share = pay_ref.shape[0] // heads
    tail_rows = pay_ref.shape[1] - 16
    row = lax.broadcasted_iota(jnp.int32, (tail_rows, N), 0)
    for head in range(heads):
        tail = jnp.where(
            row == 0, high[head : head + 1], jnp.where(row == 1, low[head : head + 1], 0.0)
        ).astype(jnp.bfloat16)
        for part in range(head * share, (head + 1) * share):
            pay_ref[part, 0:16] = local_ref[blocks - 1, part * 16 : (part + 1) * 16].astype(
                jnp.bfloat16
            )
            pay_ref[part, 16:] = tail


def prefix_kernel(at_ref, got_ref, start_ref, out_ref):
    running = start_ref[...]
    for source in range(got_ref.shape[0]):
        out_ref[source] = running.astype(jnp.bfloat16)
        tail = got_ref[source, 16:].astype(jnp.float32)
        running = (tail[0:1] + tail[1:2]) * running + got_ref[source, 0:16].astype(jnp.float32)


def inside_kernel(
    mine_ref, x_ref, bc_ref, cum_ref, step_ref, local_ref, chan_ref, out_ref, growth_ref
):
    tokens, channels = x_ref.shape
    heads = cum_ref.shape[0]
    spread = expander(heads, channels)
    causal = lax.broadcasted_iota(jnp.int32, (GROUP, GROUP), 0) >= lax.broadcasted_iota(
        jnp.int32, (GROUP, GROUP), 1
    )
    before = jnp.zeros((heads, 1), jnp.float32)
    for block in range(tokens // GROUP):
        at = slice(block * GROUP, (block + 1) * GROUP)
        c_block = bc_ref[at, N:]
        scores = dot(c_block, bc_ref[at, 0:N], ((1,), (1,)))
        cumulative = cum_ref[:, at]
        columns = cumulative.T
        growth_ref[at] = left_dot(jnp.exp(cumulative + before).T, spread, ((1,), (0,)))
        before = before + cumulative[:, GROUP - 1 : GROUP]
        rest = chan_ref[0:1] * x_ref[at].astype(jnp.float32)
        if block:
            carried = right_dot(c_block, local_ref[block - 1], ((1,), (1,)))
            rest = rest + left_dot(jnp.exp(columns), spread, ((1,), (0,))) * carried
        for pair in range(0, heads, 2):
            found = []
            for head in (pair, pair + 1):
                differ = columns[:, head : head + 1] - cumulative[head : head + 1]
                decays = jnp.exp(jnp.where(causal, differ, -1e30))
                mixing = (scores * decays * step_ref[head : head + 1, at]).astype(jnp.bfloat16)
                found.append(
                    dot(mixing, x_ref[at, head * HEAD : (head + 1) * HEAD], ((1,), (0,)))
                )
            on = slice(pair * HEAD, (pair + 2) * HEAD)
            out_ref[at, on] = jnp.concatenate(found, 1) + rest[:, on]


def output_kernel(
    mine_ref, inside_ref, growth_ref, bc_ref, entering_ref, chan_ref, keep_ref, send_ref, dot_ref
):
    mine = mine_ref[0]
    tokens, channels = inside_ref.shape
    local = tokens // 2
    spread = expander(channels // HEAD, channels)
    gain, steer = chan_ref[1:2], chan_ref[2:3]
    for block in range(tokens // GROUP):
        at = slice(block * GROUP, (block + 1) * GROUP)
        carried = dot(bc_ref[at, N:], entering_ref[...], ((1,), (1,)))
        y = inside_ref[at] + growth_ref[at] * carried
        squares = left_dot(y * y, spread, ((1,), (1,))) * (1.0 / HEAD)
        scale = left_dot(lax.rsqrt(squares + EPSILON), spread, ((1,), (0,)))
        normed = y * scale * gain
        part = block * GROUP // local
        on = slice(block * GROUP - part * local, (block + 1) * GROUP - part * local)

        @pl.when(mine == part)
        def _():
            keep_ref[on] = normed

        @pl.when(mine != part)
        def _():
            send_ref[on] = normed.astype(jnp.bfloat16)

        terms = normed * steer
        folded = terms[:, 0:128]
        for lane in range(128, channels, 128):
            folded = folded + terms[:, lane : lane + 128]
        dot_ref[part, :, on] = jnp.sum(folded.T, axis=0, keepdims=True)


def steer_kernel(factor, mine_ref, keep_ref, other_ref, dots_ref, chan_ref, out_ref):
    first = mine_ref[0] == 0
    half = keep_ref.shape[1]
    dots = dots_ref[...]
    for lane in range(0, half, 256):
        at = slice(lane, lane + 256)
        later = slice(half + lane, half + lane + 256)
        own, other = keep_ref[:, at], other_ref[:, at].astype(jnp.float32)
        left, right = jnp.where(first, own, other), jnp.where(first, other, own)
        for on, normed in ((at, left), (later, right)):
            steer = jnp.broadcast_to(chan_ref[2:3, on], (dots.shape[0], 256))
            penalty = dot(dots, steer, ((0,), (0,)), HIGHEST)
            out_ref[:, on] = (normed - penalty * factor).astype(jnp.bfloat16)


def prepare_parameters(d_skip, norm_gain, steer, dt_bias, decay_rate, z, start, at):
    channel_rows = jnp.concatenate(
        [
            jnp.repeat(d_skip, HEAD)[None], norm_gain[None], steer[None],
            jnp.zeros((5, steer.shape[0]), jnp.float32),
        ],
        0,
    )
    wide = (dt_bias.shape[0], 64)
    head_columns = jnp.concatenate(
        [jnp.broadcast_to(dt_bias[:, None], wide), jnp.broadcast_to(decay_rate[:, None], wide)], 1
    )
    source = (z + jnp.array(OFFSETS, jnp.int32)) % SIZES["z"]
    where = jnp.concatenate(
        [
            source // 2, (source % 2 == lax.axis_index("c")).astype(jnp.int32),
            lax.axis_index("yl").astype(jnp.int32).reshape(1),
        ]
    )
    start = lax.dynamic_slice_in_dim(start, at, start.shape[0] // SHARES, 0)
    return channel_rows, head_columns, where, start


def ring(block, depth, axis, prepare, raw):
    count = SIZES[axis]
    forward = [(i, (i + 1) % count) for i in range(count)]
    backward = [(i, (i - 1) % count) for i in range(count)]
    across = [(i, (i + count // 2) % count) for i in range(count)]
    pieces = [block]
    ahead = behind = block
    for hop in range(1, count // 2):
        ahead = lax.ppermute(ahead, axis, forward)
        behind = lax.ppermute(behind, axis, backward)
        if hop == 1:
            far = lax.ppermute(block[depth:], axis, across)
            ready = prepare(*lax.optimization_barrier((raw, far))[0])
            ahead, behind, far = lax.optimization_barrier((ahead, behind, far))
        elif hop == 2:
            ahead, behind, ready = lax.optimization_barrier((ahead, behind, ready))
        pieces += [ahead, behind]
    pieces.append(lax.ppermute(ahead, axis, forward))
    return pieces, far, ready


def per_device(
    tokens, x_weight, bc_weight, dt_weight, conv_x, conv_bc, dt_bias, decay_rate, d_skip,
    norm_gain, initial_state, steer,
):
    local, width = tokens.shape
    k_rows, channels = x_weight.shape
    half = channels // 2
    heads = dt_weight.shape[1] // 2
    bc_rows = bc_weight.shape[1] // 2
    small = bc_rows + heads
    seq_count = SIZES["z"] * SIZES["x"] * SIZES["yl"]
    tp_count = SIZES["yh"] * SIZES["c"]
    z = lax.axis_index("z")
    mine = lax.axis_index("yl").astype(jnp.int32).reshape(1)
    f32, bf16 = jnp.float32, jnp.bfloat16

    earlier = lax.ppermute(
        tokens[local - HALO :], SEQ, [(i, i + 1) for i in range(seq_count - 1)]
    )
    line = SIZES["yh"] * 2
    copies = pl.pallas_call(
        token_kernel,
        out_shape=jax.ShapeDtypeStruct((line, local + HALO, width), bf16),
        compiler_params=pltpu.CompilerParams(vmem_limit_bytes=8388608),
        cost_estimate=pl.CostEstimate(
            flops=0, bytes_accessed=3 * line * local * width, transcendentals=0
        ),
    )(earlier, tokens)

    fan = SIZES["x"] * SIZES["yl"]
    packed_rows = small * k_rows // half
    packed = jnp.concatenate(
        [
            bc_weight.reshape(k_rows, 2, bc_rows).transpose(1, 2, 0),
            dt_weight.reshape(k_rows, 2, heads).transpose(1, 2, 0),
        ],
        1,
    ).reshape(2, packed_rows, half)
    panel = jnp.concatenate(
        [
            jnp.stack([x_weight[:, :half], x_weight[:, half:]]),
            packed,
            jnp.zeros((2, -packed_rows % 8, half), bf16),
        ],
        1,
    )
    panel = jnp.broadcast_to(panel[None], (SIZES["x"],) + panel.shape).reshape(
        fan, panel.shape[1], half
    )
    got = lax.all_to_all(panel, ("x", "yl"), 0, 0)
    copies, got = lax.optimization_barrier((copies, got))
    tall = got[:, :k_rows].reshape(fan * k_rows, half)
    flat = got[:, k_rows : k_rows + packed_rows].reshape(
        fan, packed_rows, half // k_rows, k_rows
    )
    flat = flat.transpose(1, 2, 0, 3).reshape(small, fan * k_rows)
    block = jnp.concatenate([tall, flat], 0)
    pieces, far, ready = ring(
        block, fan * k_rows, "z", prepare_parameters,
        (
            d_skip, norm_gain, steer, dt_bias, decay_rate, z.astype(jnp.int32),
            initial_state.reshape(channels, N),
            (lax.axis_index(("yl", "z", "x")) * (channels // SHARES)).astype(jnp.int32),
        ),
    )
    channel_rows, head_columns, where, start = ready

    own = lax.all_to_all(copies, ("yh", "yl"), 0, 0).reshape(
        SIZES["yh"], 2, local + HALO, width
    )
    own = lax.optimization_barrier((own, pieces[5]))[0]
    other = lax.ppermute(own, "c", [(0, 1), (1, 0)])

    bc_pre, dt_raw = narrow_project(where, own, other, pieces[:-1] + [far], bc_rows, heads, 2 * tp_count)
    pieces[-1] = lax.optimization_barrier((pieces[-1], bc_pre))[0]
    x_conv, cumulative, step_size, scaled = project(
        where, dt_raw, conv_x, head_columns, own, other, pieces
    )
    bc_all = lax.all_to_all(bc_pre, ("yh", "c", "yl"), 0, 0).reshape(2 * N, -1)

    pair = 2 * local
    plane = SIZES["z"] * SIZES["x"]
    share = half // plane
    bc_conv, payload, locals_ = call(
        state_kernel,
        [
            jax.ShapeDtypeStruct((pair, 2 * N), bf16),
            jax.ShapeDtypeStruct((plane, share + 8, N), bf16),
            jax.ShapeDtypeStruct((pair // GROUP, half, N), f32),
        ],
        mine, bc_all, conv_bc, cumulative, scaled,
        grant=ALL_VMEM,
    )
    states = lax.all_to_all(payload, ("z", "x"), 0, 0)
    (prefixes,) = call(
        prefix_kernel,
        [jax.ShapeDtypeStruct((plane, share, N), bf16)],
        mine, states, start,
    )
    entering = lax.all_to_all(prefixes, ("z", "x"), 0, 0).reshape(half, N)

    lanes = ((8, half), lambda i, s: (0, s[0]))
    inside, growth = call(
        inside_kernel,
        [jax.ShapeDtypeStruct((pair, half), f32), jax.ShapeDtypeStruct((pair, half), f32)],
        mine, x_conv, bc_conv, cumulative, step_size, locals_, channel_rows,
        blocks={5: lanes},
        flops=10**9, bytes_accessed=12 * pair * half,
    )
    keep, send, dots = call(
        output_kernel,
        [
            jax.ShapeDtypeStruct((local, half), f32),
            jax.ShapeDtypeStruct((local, half), bf16),
            jax.ShapeDtypeStruct((2, 1, local), f32),
        ],
        mine, inside, growth, bc_conv, entering, channel_rows,
        blocks={4: lanes},
    )
    shape = (SIZES["yh"], 2, SIZES["c"], 1, local)
    partials = lax.all_to_all(
        jnp.broadcast_to(dots[None, :, None], shape).reshape(2 * tp_count, 1, local),
        ("yh", "yl", "c"), 0, 0,
    )
    swapped = lax.ppermute(send, "yl", [(0, 1), (1, 0)])
    factor = 1.0 / math.sqrt(channels * tp_count)
    (out,) = call(
        functools.partial(steer_kernel, factor),
        [jax.ShapeDtypeStruct((local, channels), bf16)],
        mine, keep, swapped, partials.reshape(2 * tp_count, local),
        channel_rows,
    )
    return out


def solution(mesh):
    fine = Mesh(mesh.devices.reshape(tuple(SIZES.values())), tuple(SIZES))
    both = P(SEQ, TP)
    placed = (
        both, both, both, both, P(None, TP), P(), P(TP), P(TP), P(TP), P(TP),
        P(TP, None, None), P(TP),
    )
    return jax.shard_map(
        per_device, mesh=fine, in_specs=placed, out_specs=both, check_vma=False
    )
```
